32 devices in a mesh: rows: 16 (over z, x, core), probe: 2 (over y).
Axes of the slice: x: 2, y: 2, z: 4, core: 2. Of those that a mesh axis runs over, the one named last changes fastest.
Arguments:
- targets: float32 [3, 4096], P(None, 'rows'), may hold values from 0 to 1
- sources: bfloat16 [3, 2048], P(None, 'rows'), may hold values from 0 to 1
- probes: bfloat16 [256, 2048], P('probe', 'rows'), may hold values from -6 to 6
- cluster_sizes: int32 [32], P(('rows', 'probe')), may hold values from 64 to 128, as said below
- leaf_ranks: int32 [32], P(('rows', 'probe')), may hold values from 128 to 256, as said below
Outputs:
- leaf_basis: float32 [256, 2, 4096], P(None, None, ('rows', 'probe'))
- top_factor: float32 [32, 256, 256], P(('rows', 'probe'))
The draws below stay inside these ranges and needn't reach their ends.
Inputs may be any that keep to these rules, and one draw needn't show every extreme that they name: `cluster_sizes`: some leaf uses all 128 points in every draw. `leaf_ranks`: some leaf keeps all 256 rows in every draw.
All inputs are finite; a program needn't handle non-finite values.
Results may differ from the reference program's by a relative error of at most 0.0033.
Values may be sent and summed in bfloat16 or wider, within the bound.
No kernel may reach another device: no remote copies, remote signals or barrier semaphores. Data moves between devices by JAX's collectives and lax.ppermute only.
A program may use at most 64 MiB of HBM per device.

```python
import jax
import jax.numpy as jnp
from jax import lax

LEAF = 128
NPROBE = 256
NCOL = 2048
LEAVES = 32
NROWS = 4096
N_ROWS = 16
N_PROBE = 2


def draw_cluster_sizes(key, part):
    values = jax.random.randint(key, (LEAVES,), LEAF // 2, LEAF + 1)
    position = jax.random.randint(jax.random.fold_in(key, 7), (), 0, LEAVES)
    lowest = jax.random.randint(jax.random.fold_in(key, 11), (), 0, LEAVES)
    values = values.at[lowest].set(LEAF // 2)
    return values.at[position].set(LEAF).astype(jnp.int32)


def draw_leaf_ranks(key, part):
    values = jax.random.randint(key, (LEAVES,), NPROBE // 2, NPROBE + 1)
    position = jax.random.randint(jax.random.fold_in(key, 13), (), 0, LEAVES)
    return values.at[position].set(NPROBE).astype(jnp.int32)


def level_of(key, shape, cuts, low, top_value):
    loudness = 1.0
    for axis_at, shards_of in cuts:
        steps = jax.random.uniform(jax.random.fold_in(jax.random.fold_in(key, 6), axis_at), (shards_of,), jnp.float32, low / len(cuts), top_value / len(cuts))
        loudness = loudness * jnp.repeat(jnp.exp(steps), shape[axis_at] // shards_of).reshape((-1,) + (1,) * (len(shape) - 1 - axis_at))
    return loudness


def scatter_about(rng, dims, deviation, most, pieces=(), kind=jnp.bfloat16):
    loudness = level_of(rng, dims, pieces, -0.22, 0.18) if pieces else 1.0
    array = jax.random.normal(rng, dims, jnp.float32) * deviation * loudness
    return jnp.minimum(jnp.maximum(array, -most), most).astype(kind)


def setup_inputs(seed: int = 0) -> dict:
    splits = jax.random.split(jax.random.key(seed), 6)
    return {
        "targets": jnp.clip(1.0 * jax.random.uniform(splits[0], (3, NROWS), jnp.float32) ** level_of(splits[0], (3, NROWS), ((1, 16),), -0.2, 0.2), 0.0, 1.0),
        "sources": jnp.clip(1.0 * jax.random.uniform(splits[1], (3, NCOL), jnp.float32) ** level_of(splits[1], (3, NCOL), ((1, 16),), -0.2, 0.2), 0.0, 1.0).astype(jnp.bfloat16),
        "probes": scatter_about(splits[2], (NPROBE, NCOL), 1.0, 6.0, ((0, 2), (1, 16))),
        "cluster_sizes": draw_cluster_sizes(jax.random.fold_in(splits[5], 71), 0),
        "leaf_ranks": draw_leaf_ranks(jax.random.fold_in(splits[5], 71), 0),
    }


wavenumber = 30.0
softening = 0.02

def kernel_pair(source_pts, target_pts, col_total):
    diff_x = source_pts[0][:, None] - target_pts[0][None, :]
    diff_y = source_pts[1][:, None] - target_pts[1][None, :]
    diff_z = source_pts[2][:, None] - target_pts[2][None, :]
    distance = jnp.sqrt(diff_x * diff_x + diff_y * diff_y + diff_z * diff_z + softening * softening)
    amplitude = 1.0 / (distance * jnp.sqrt(jnp.float32(col_total)))
    kernel_cos = (amplitude * jnp.cos(wavenumber * distance)).astype(jnp.bfloat16)
    kernel_sin = (amplitude * jnp.sin(wavenumber * distance)).astype(jnp.bfloat16)
    return (kernel_cos, kernel_sin)

def cholesky_basis(matrix):
    gram_matrix = jnp.dot(matrix, matrix.T, precision=lax.Precision.HIGHEST)
    shift_value = jnp.trace(gram_matrix) / NPROBE
    factor = jnp.linalg.cholesky(gram_matrix + shift_value * jnp.eye(NPROBE, dtype=matrix.dtype))
    return jax.scipy.linalg.solve_triangular(factor, matrix, lower=True)

def merge_node(stacked):
    basis_rows = cholesky_basis(stacked)
    return jnp.dot(stacked, basis_rows.T, precision=lax.Precision.HIGHEST)

def merge_level(projected):
    left_part = projected[0::2]
    right_part = projected[1::2]
    stacked = jnp.concatenate([left_part, right_part], axis=-1)
    shape_kept = stacked.shape
    flat = stacked.reshape(-1, NPROBE, 2 * NPROBE)
    merged = lax.map(merge_node, flat)
    return merged.reshape(shape_kept[0], shape_kept[1], NPROBE, NPROBE)

def reference(targets, sources, probes, cluster_sizes, leaf_ranks):
    source_pts = sources.astype(jnp.float32)
    probe_vals = probes.astype(jnp.float32)

    def one_leaf(leaf_index):
        target_pts = lax.dynamic_slice_in_dim(targets, leaf_index * LEAF, LEAF, 1)
        kernel_cos, kernel_sin = kernel_pair(source_pts, target_pts, NCOL)
        sample_cos = jnp.dot(probe_vals, kernel_cos.astype(jnp.float32), precision=lax.Precision.HIGHEST)
        sample_sin = jnp.dot(probe_vals, kernel_sin.astype(jnp.float32), precision=lax.Precision.HIGHEST)
        kept_rows = (jnp.arange(LEAF) < cluster_sizes[leaf_index]).astype(jnp.float32)
        matrix = jnp.concatenate([sample_cos * kept_rows, sample_sin * kept_rows], axis=1)
        basis_rows = cholesky_basis(matrix)
        rank_rows = (jnp.arange(NPROBE) < leaf_ranks[leaf_index]).astype(jnp.float32)
        basis_rows = basis_rows * rank_rows[:, None]
        projected = jnp.dot(matrix, basis_rows.T, precision=lax.Precision.HIGHEST)
        return (basis_rows, projected)
    leaf_bases, leaf_projs = lax.map(one_leaf, jnp.arange(LEAVES, dtype=jnp.int32))
    leaf_basis = leaf_bases.reshape(LEAVES, NPROBE, 2, LEAF).transpose(1, 2, 0, 3).reshape(NPROBE, 2, NROWS)
    grouped = leaf_projs.reshape(N_ROWS, N_PROBE, NPROBE, NPROBE)
    level_one = merge_level(grouped)
    level_two = merge_level(level_one)
    top_factor = jnp.repeat(level_two, 4, axis=0).reshape(LEAVES, NPROBE, NPROBE)
    return (leaf_basis, top_factor)
```

```python
import math

import jax
import jax.numpy as jnp
from jax import lax
from jax.experimental import pallas as pl
from jax.experimental.pallas import tpu as pltpu
from jax.sharding import PartitionSpec as P

wavenumber = 30.0
softening = 0.02

F32 = jnp.float32
BF16 = jnp.bfloat16
VMEM = pl.BlockSpec(memory_space=pltpu.VMEM)
SMEM = pl.BlockSpec(memory_space=pltpu.SMEM)
NN = ((1,), (0,))
NT = ((1,), (1,))
TN = ((0,), (0,))

LANES = 128
PANEL = 32
GROUP = 8


def split_bf16(value):
    high = value.astype(BF16)
    return high, (value - high.astype(F32)).astype(BF16)


def mxu(left, right, dims):
    return lax.dot_general(left, right, (dims, ((), ())), preferred_element_type=F32)


def dot3(left, right, dims):
    lh, ll = split_bf16(left)
    rh, rl = split_bf16(right)
    return mxu(lh, rh, dims) + (mxu(lh, rl, dims) + mxu(ll, rh, dims))


def pick_lane(tile, lane):
    where = jnp.full(tile.shape, lane, jnp.int32)
    return jnp.take_along_axis(tile, where, axis=1, mode="promise_in_bounds")


def pick_row(tile, row):
    return jnp.broadcast_to(tile[row : row + 1, :], tile.shape)


def sweep(t_ref):
    n = t_ref.shape[0]
    tiles = n // LANES
    steps = PANEL // 8
    lane = lax.broadcasted_iota(jnp.int32, (8, LANES), 1)
    row = lax.broadcasted_iota(jnp.int32, (8, LANES), 0)
    along_lanes = [jnp.ones((8, LANES), F32) for _ in range(tiles)]
    along_rows = []
    for start in range(0, n, PANEL):
        at, low = divmod(start, LANES)
        block = [
            [t_ref[start + 8 * i : start + 8 * i + 8, LANES * t : LANES * (t + 1)] for t in range(tiles)]
            for i in range(steps)
        ]
        pivots = [jnp.zeros((8, LANES), F32) for _ in range(steps)]
        for first in range(0, PANEL, GROUP):
            i0 = first // 8
            cols = [[pick_lane(block[i][at], low + first + a) for i in range(i0, steps)] for a in range(GROUP)]
            rows = [[pick_row(block[i0][t], a) for t in range(tiles)] for a in range(GROUP)]
            for a in range(GROUP):
                here = lane == low + first + a
                pivot = pick_row(cols[a][0], a)
                inverse = 1.0 / pivot
                along_lanes[at] = jnp.where(here, pivot, along_lanes[at])
                pivots[i0] = jnp.where(row == a, pivot, pivots[i0])
                swept = list(rows[a])
                swept[at] = jnp.where(here, 2.0 * swept[at], swept[at])
                factors = [c * inverse for c in cols[a]]
                factors[0] = jnp.where(row > a, factors[0], 0.0)
                for b in range(a + 1, GROUP):
                    entry = pick_row(cols[b][0], a)
                    factor = pick_row(factors[0], b)
                    cols[b] = [c - f * entry for c, f in zip(cols[b], factors)]
                    rows[b] = [r - factor * s for r, s in zip(rows[b], swept)]
                for x, i in enumerate(range(i0, steps)):
                    for t in range(tiles):
                        block[i][t] = block[i][t] - factors[x] * swept[t]
        for i in range(steps):
            for t in range(tiles):
                t_ref[start + 8 * i : start + 8 * i + 8, LANES * t : LANES * (t + 1)] = block[i][t]
        along_rows += pivots
        end = start + PANEL
        if end < n:
            whole = t_ref[start:end, :]
            rowi = lax.broadcasted_iota(jnp.int32, (PANEL, n), 0)
            coli = lax.broadcasted_iota(jnp.int32, (PANEL, n), 1)
            kept = jnp.where((coli < end) & (coli - start > rowi), 0.0, whole)
            scale = 1.0 / jnp.concatenate(pivots, axis=0)
            factors = (whole * jnp.concatenate([scale] * tiles, axis=1)).T
            colr = lax.broadcasted_iota(jnp.int32, (n - end, n), 1)
            rest = t_ref[end:n, :]
            rest = jnp.where((colr >= start) & (colr < end), 0.0, rest)
            t_ref[end:n, :] = rest - dot3(factors[end:n, :], kept, NN)
    return along_lanes, along_rows


def grids(n):
    rows = lax.broadcasted_iota(jnp.int32, (n, n), 0)
    cols = lax.broadcasted_iota(jnp.int32, (n, n), 1)
    return rows, cols


def factorize(gram, t_ref):
    n = gram.shape[0]
    rows, cols = grids(n)
    diagonal = jnp.where(rows == cols, gram, 0.0)
    shift = jnp.sum(jnp.sum(diagonal, axis=0, keepdims=True), axis=1, keepdims=True) / n
    t_ref[...] = gram / shift + jnp.where(rows == cols, 1.0, 0.0)
    along_lanes, along_rows = sweep(t_ref)
    by_col = jnp.concatenate([jnp.broadcast_to(x[0:1, :], (n, LANES)) for x in along_lanes], axis=1)
    by_row = jnp.concatenate([jnp.concatenate([x] * (n // LANES), axis=1) for x in along_rows], axis=0)
    return shift, by_row, by_col


def projected_rows(t_ref, by_row, by_col):
    rows, cols = grids(t_ref.shape[0])
    held = t_ref[...]
    return lax.rsqrt(by_row) * jnp.where(
        rows < cols, held, jnp.where(rows > cols, -held / by_col, by_row - 1.0)
    )


def inverse_factor(t_ref, by_row, by_col):
    rows, cols = grids(t_ref.shape[0])
    held = t_ref[...]
    return lax.rsqrt(by_row) * jnp.where(rows > cols, held / by_col, jnp.where(rows == cols, 1.0, 0.0))


def fold(full_ref, packed_ref):
    n = full_ref.shape[0]
    half = n // 2
    rows, cols = grids(half)
    upper = full_ref[0:half, 0:half]
    lower = full_ref[half:n, half:n]
    packed_ref[0:half, :] = full_ref[0:half, half:n]
    packed_ref[half:n, :] = jnp.where(rows <= cols, upper, lower)
    packed_ref[n : n + 8, :] = jnp.broadcast_to(
        jnp.sum(jnp.where(rows == cols, lower, 0.0), axis=0, keepdims=True), (8, half)
    )


def unfold_add(packed_ref, full_ref):
    n = full_ref.shape[0]
    half = n // 2
    rows, cols = grids(half)
    corner = packed_ref[0:half, :]
    both = packed_ref[half:n, :]
    turned = both.T
    line = jnp.broadcast_to(packed_ref[n : n + 1, :], (half, half))
    upper = jnp.where(rows <= cols, both, turned)
    lower = jnp.where(rows == cols, line, jnp.where(rows > cols, both, turned))
    top = jnp.concatenate([upper, corner], axis=1)
    bottom = jnp.concatenate([corner.T, lower], axis=1)
    return full_ref[...] + jnp.concatenate([top, bottom], axis=0)


def kernel_body(col_total, targets_ref, sources_ref, out_ref):
    pieces, _, width = sources_ref.shape
    m = targets_ref.shape[1]
    turned = jnp.concatenate([targets_ref[...], jnp.zeros((m - 8, m), F32)], axis=0).T
    points = [jnp.broadcast_to(turned[:, c : c + 1], (m, width)) for c in range(3)]
    size = 1.0 / math.sqrt(col_total)
    turns = wavenumber * 2.0 / math.pi
    h = math.pi / 2
    for i in range(pieces):
        source = sources_ref[i].astype(F32)
        square = softening * softening
        for c in range(3):
            diff = source[c : c + 1, :] - points[c]
            square = square + diff * diff
        near = lax.rsqrt(square)
        amplitude = near * size
        quarter = (square * near) * turns
        whole = jnp.round(quarter)
        rest = quarter - whole
        r2 = rest * rest
        sine = rest * (h + r2 * (-(h**3) / 6 + r2 * (h**5 / 120 + r2 * (-(h**7) / 5040))))
        cosine = 1.0 + r2 * (-(h**2) / 2 + r2 * (h**4 / 24 + r2 * (-(h**6) / 720 + r2 * (h**8 / 40320))))
        count = whole.astype(jnp.int32)
        odd = (count & 1) == 1
        first = jnp.where(odd, sine, cosine)
        second = jnp.where(odd, cosine, sine)
        first = jnp.where(((count + 1) & 2) == 0, first, -first)
        second = jnp.where((count & 2) == 0, second, -second)
        out_ref[i, 0:m, :] = (amplitude * first).astype(BF16)
        out_ref[i, m : 2 * m, :] = (amplitude * second).astype(BF16)


def accumulate(probe_ref, kernel_ref, total):
    pieces = probe_ref.shape[0]
    both = 2 if pieces % 2 == 0 else 1

    def one(i, total):
        left = jnp.concatenate([probe_ref[both * i + k] for k in range(both)], axis=1)
        right = jnp.concatenate([kernel_ref[both * i + k] for k in range(both)], axis=1)
        return total + mxu(left, right, NT)

    count = pieces // both
    return lax.fori_loop(0, count, one, total, unroll=count <= 8)


def leaf_body(blocks, place_ref, sizes_ref, ranks_ref, *refs):
    near, far = refs[:blocks], refs[blocks : 2 * blocks]
    near_kernel, far_kernel, h_ref, w_ref, m_ref, t_ref = refs[2 * blocks :]
    n = h_ref.shape[0]
    rows, cols = grids(n)
    high = n // blocks
    for o in range(blocks):
        total = jnp.zeros((high, n), F32)
        total = accumulate(near[o], near_kernel, total)
        total = accumulate(far[o], far_kernel, total)
        at = pl.multiple_of((place_ref[0] ^ o) * high, high)
        m_ref[pl.ds(at, high), :] = total
    used = sizes_ref[0]
    half = n // 2
    inside = cols - jnp.where(cols >= half, half, 0) < used
    matrix = jnp.where(inside, m_ref[...], 0.0)
    m_ref[...] = matrix
    gram = dot3(matrix, matrix, NT)
    shift, by_row, by_col = factorize(gram, t_ref)
    in_rank = rows < ranks_ref[0]
    value = jnp.where(in_rank, projected_rows(t_ref, by_row, by_col), 0.0)
    h_ref[...] = dot3(value, value, TN) * shift
    w_ref[...] = jnp.where(in_rank, inverse_factor(t_ref, by_row, by_col) * lax.rsqrt(shift), 0.0)


def basis_body(w_ref, m_ref, b_ref):
    b_ref[...] = dot3(w_ref[...], m_ref[...], NN)


def node_body(own_ref, other_ref, h_ref, packed_ref, t_ref):
    shift, by_row, by_col = factorize(own_ref[...] + other_ref[...], t_ref)
    value = projected_rows(t_ref, by_row, by_col)
    h_ref[...] = dot3(value, value, TN) * shift
    fold(h_ref, packed_ref)


def top_body(own_ref, other_ref, z_ref, t_ref):
    shift, by_row, by_col = factorize(unfold_add(other_ref, own_ref), t_ref)
    value = projected_rows(t_ref, by_row, by_col)
    z_ref[...] = (value * jnp.sqrt(shift)).T


def call(body, name, outs, operands, specs=None, scratch=(), flops=0):
    bytes_used = sum(x.size * x.dtype.itemsize for x in (*outs, *operands))
    return pl.pallas_call(
        body,
        name=name,
        out_shape=list(outs),
        in_specs=list(specs or [VMEM] * len(operands)),
        out_specs=[VMEM] * len(outs),
        scratch_shapes=list(scratch),
        cost_estimate=pl.CostEstimate(flops=flops, bytes_accessed=bytes_used, transcendentals=0),
    )(*operands)


def flip(value, axis, mask):
    pairs = [(source, source ^ mask) for source in range(lax.axis_size(axis))]
    return lax.ppermute(value, axis, pairs)


def per_device(targets, sources, probes, cluster_sizes, leaf_ranks):
    rows_size = lax.axis_size("rows")
    probe_size = lax.axis_size("probe")
    col_total = sources.shape[1] * rows_size
    n = probes.shape[0] * probe_size
    leaf_rows = targets.shape[1] // probe_size
    place = lax.axis_index("probe")

    points = lax.dynamic_slice_in_dim(targets, place * leaf_rows, leaf_rows, 1)
    points = jnp.pad(points, ((0, 8 - points.shape[0]), (0, 0)))

    def evaluate(pieces):
        out = jax.ShapeDtypeStruct((pieces.shape[0], 2 * leaf_rows, pieces.shape[2]), BF16)
        return call(
            lambda *refs: kernel_body(col_total, *refs), "kernel_values", [out], [points, pieces],
            flops=100 * out.size,
        )[0]

    mask = rows_size // 2
    held, held_sources = probes[None], sources[None]
    values = []
    done = 0
    while mask > 1:
        more_sources = flip(held_sources, "rows", mask)
        more = flip(held, "rows", mask)
        held = jnp.concatenate([held, more], axis=0)
        held_sources = jnp.concatenate([held_sources, more_sources], axis=0)
        mask //= 2
    near = [held]
    far_sources = flip(held_sources, "rows", 1)
    bit = 1
    while bit < probe_size:
        near += [flip(x, "probe", bit) for x in near]
        bit *= 2
    far = [flip(x, "rows", 1) for x in near]
    near_kernel = evaluate(held_sources)
    far_kernel = evaluate(far_sources)

    square = jax.ShapeDtypeStruct((n, n), F32)
    scratch = [pltpu.VMEM((n, n), F32)]
    blocks = len(near)
    h, w, m = call(
        lambda *refs: leaf_body(blocks, *refs), "leaf", [square] * 3,
        [place[None], cluster_sizes, leaf_ranks, *near, *far, near_kernel, far_kernel],
        specs=[SMEM] * 3 + [VMEM] * (2 * blocks + 2), scratch=scratch, flops=n**3,
    )
    other = flip(h, "rows", 1)
    basis = call(basis_body, "basis", [square], [w, m], flops=6 * n**3)[0]
    packed = jax.ShapeDtypeStruct((n + 8, n // 2), F32)
    h, sent = call(node_body, "node", [square, packed], [h, other], scratch=scratch, flops=n**3)
    other = flip(sent, "rows", 2)
    top = call(top_body, "top", [square], [h, other], scratch=scratch, flops=n**3)[0]
    return (basis.reshape(n, 2, leaf_rows), top[None])


def solution(mesh):
    return jax.shard_map(
        per_device,
        mesh=mesh,
        in_specs=(
            P(None, "rows"),
            P(None, "rows"),
            P("probe", "rows"),
            P(("rows", "probe")),
            P(("rows", "probe")),
        ),
        out_specs=(P(None, None, ("rows", "probe")), P(("rows", "probe"), None, None)),
        check_vma=False,
    )
```

```python
import math

import jax
import jax.numpy as jnp
from jax import lax
from jax.experimental import pallas as pl
from jax.experimental.pallas import tpu as pltpu
from jax.sharding import PartitionSpec as P


wavenumber = 30.0
softening = 0.02

F32 = jnp.float32
BF16 = jnp.bfloat16
VMEM = pl.BlockSpec(memory_space=pltpu.VMEM)
SMEM = pl.BlockSpec(memory_space=pltpu.SMEM)
NN = ((1,), (0,))
NT = ((1,), (1,))
TN = ((0,), (0,))

LANES = 128
PANEL = 32
GROUP = 8


def split_bf16(value):
    high = value.astype(BF16)
    return high, (value - high.astype(F32)).astype(BF16)


def mxu(left, right, dims):
    return lax.dot_general(left, right, (dims, ((), ())), preferred_element_type=F32)


def dot3(left, right, dims):
    lh, ll = split_bf16(left)
    rh, rl = split_bf16(right)
    return mxu(lh, rh, dims) + (mxu(lh, rl, dims) + mxu(ll, rh, dims))


def pick_lane(tile, lane):
    where = jnp.full(tile.shape, lane, jnp.int32)
    return jnp.take_along_axis(tile, where, axis=1, mode="promise_in_bounds")


def pick_row(tile, row):
    return jnp.broadcast_to(tile[row : row + 1, :], tile.shape)


def sweep(t_ref):
    n = t_ref.shape[0]
    tiles = n // LANES
    steps = PANEL // 8
    lane = lax.broadcasted_iota(jnp.int32, (8, LANES), 1)
    row = lax.broadcasted_iota(jnp.int32, (8, LANES), 0)
    along_lanes = [jnp.ones((8, LANES), F32) for _ in range(tiles)]
    along_rows = []
    for start in range(0, n, PANEL):
        at, low = divmod(start, LANES)
        block = [
            [t_ref[start + 8 * i : start + 8 * i + 8, LANES * t : LANES * (t + 1)] for t in range(tiles)]
            for i in range(steps)
        ]
        pivots = [jnp.zeros((8, LANES), F32) for _ in range(steps)]
        for first in range(0, PANEL, GROUP):
            i0 = first // 8
            cols = [[pick_lane(block[i][at], low + first + a) for i in range(i0, steps)] for a in range(GROUP)]
            rows = [[pick_row(block[i0][t], a) for t in range(tiles)] for a in range(GROUP)]
            for a in range(GROUP):
                here = lane == low + first + a
                pivot = pick_row(cols[a][0], a)
                inverse = 1.0 / pivot
                along_lanes[at] = jnp.where(here, pivot, along_lanes[at])
                pivots[i0] = jnp.where(row == a, pivot, pivots[i0])
                swept = list(rows[a])
                swept[at] = jnp.where(here, 2.0 * swept[at], swept[at])
                factors = [c * inverse for c in cols[a]]
                factors[0] = jnp.where(row > a, factors[0], 0.0)
                for b in range(a + 1, GROUP):
                    entry = pick_row(cols[b][0], a)
                    factor = pick_row(factors[0], b)
                    cols[b] = [c - f * entry for c, f in zip(cols[b], factors)]
                    rows[b] = [r - factor * s for r, s in zip(rows[b], swept)]
                for x, i in enumerate(range(i0, steps)):
                    for t in range(tiles):
                        block[i][t] = block[i][t] - factors[x] * swept[t]
        for i in range(steps):
            for t in range(tiles):
                t_ref[start + 8 * i : start + 8 * i + 8, LANES * t : LANES * (t + 1)] = block[i][t]
        along_rows += pivots
        end = start + PANEL
        if end < n:
            whole = t_ref[start:end, :]
            rowi = lax.broadcasted_iota(jnp.int32, (PANEL, n), 0)
            coli = lax.broadcasted_iota(jnp.int32, (PANEL, n), 1)
            kept = jnp.where((coli < end) & (coli - start > rowi), 0.0, whole)
            scale = 1.0 / jnp.concatenate(pivots, axis=0)
            factors = (whole * jnp.concatenate([scale] * tiles, axis=1)).T
            colr = lax.broadcasted_iota(jnp.int32, (n - end, n), 1)
            rest = t_ref[end:n, :]
            rest = jnp.where((colr >= start) & (colr < end), 0.0, rest)
            t_ref[end:n, :] = rest - dot3(factors[end:n, :], kept, NN)
    return along_lanes, along_rows


def grids(n):
    rows = lax.broadcasted_iota(jnp.int32, (n, n), 0)
    cols = lax.broadcasted_iota(jnp.int32, (n, n), 1)
    return rows, cols


def factorize(gram, t_ref):
    n = gram.shape[0]
    rows, cols = grids(n)
    diagonal = jnp.where(rows == cols, gram, 0.0)
    shift = jnp.sum(jnp.sum(diagonal, axis=0, keepdims=True), axis=1, keepdims=True) / n
    t_ref[...] = gram / shift + jnp.where(rows == cols, 1.0, 0.0)
    along_lanes, along_rows = sweep(t_ref)
    by_col = jnp.concatenate([jnp.broadcast_to(x[0:1, :], (n, LANES)) for x in along_lanes], axis=1)
    by_row = jnp.concatenate([jnp.concatenate([x] * (n // LANES), axis=1) for x in along_rows], axis=0)
    return shift, by_row, by_col


def projected_rows(t_ref, by_row, by_col):
    rows, cols = grids(t_ref.shape[0])
    held = t_ref[...]
    return lax.rsqrt(by_row) * jnp.where(
        rows < cols, held, jnp.where(rows > cols, -held / by_col, by_row - 1.0)
    )


def inverse_factor(t_ref, by_row, by_col):
    rows, cols = grids(t_ref.shape[0])
    held = t_ref[...]
    return lax.rsqrt(by_row) * jnp.where(rows > cols, held / by_col, jnp.where(rows == cols, 1.0, 0.0))


def fold(full_ref, packed_ref):
    n = full_ref.shape[0]
    half = n // 2
    rows, cols = grids(half)
    upper = full_ref[0:half, 0:half]
    lower = full_ref[half:n, half:n]
    packed_ref[0:half, :] = full_ref[0:half, half:n]
    packed_ref[half:n, :] = jnp.where(rows <= cols, upper, lower)
    packed_ref[n : n + 8, :] = jnp.broadcast_to(
        jnp.sum(jnp.where(rows == cols, lower, 0.0), axis=0, keepdims=True), (8, half)
    )


def unfold_add(packed_ref, full_ref):
    n = full_ref.shape[0]
    half = n // 2
    rows, cols = grids(half)
    corner = packed_ref[0:half, :]
    both = packed_ref[half:n, :]
    turned = both.T
    line = jnp.broadcast_to(packed_ref[n : n + 1, :], (half, half))
    upper = jnp.where(rows <= cols, both, turned)
    lower = jnp.where(rows == cols, line, jnp.where(rows > cols, both, turned))
    top = jnp.concatenate([upper, corner], axis=1)
    bottom = jnp.concatenate([corner.T, lower], axis=1)
    return full_ref[...] + jnp.concatenate([top, bottom], axis=0)


def kernel_body(col_total, high, targets_ref, *refs):
    m = targets_ref.shape[1]
    width = refs[0].shape[2]
    turned = jnp.concatenate([targets_ref[...], jnp.zeros((m - 8, m), F32)], axis=0).T
    points = [jnp.broadcast_to(turned[:, c : c + 1], (m, width)) for c in range(3)]
    count = len(refs) // 2
    for piece_ref, out_ref in zip(refs[:count], refs[count:]):
        for i in range(piece_ref.shape[0]):
            source = piece_ref[i, high : high + 3, :].astype(F32)
            first, second = kernel_values(source, points, col_total)
            out_ref[i, 0:m, :] = first
            out_ref[i, m : 2 * m, :] = second


def kernel_values(source, points, col_total):
    size = 1.0 / math.sqrt(col_total)
    turns = wavenumber * 2.0 / math.pi
    h = math.pi / 2
    square = softening * softening
    for c in range(3):
        diff = source[c : c + 1, :] - points[c]
        square = square + diff * diff
    near = lax.rsqrt(square)
    amplitude = near * size
    quarter = (square * near) * turns
    whole = jnp.round(quarter)
    rest = quarter - whole
    r2 = rest * rest
    sine = rest * (h + r2 * (-(h**3) / 6 + r2 * (h**5 / 120 + r2 * (-(h**7) / 5040))))
    cosine = 1.0 + r2 * (-(h**2) / 2 + r2 * (h**4 / 24 + r2 * (-(h**6) / 720 + r2 * (h**8 / 40320))))
    count = whole.astype(jnp.int32)
    odd = (count & 1) == 1
    first = jnp.where(odd, sine, cosine)
    second = jnp.where(odd, cosine, sine)
    first = jnp.where(((count + 1) & 2) == 0, first, -first)
    second = jnp.where((count & 2) == 0, second, -second)
    return (amplitude * first).astype(BF16), (amplitude * second).astype(BF16)


def accumulate(probe_ref, kernel_ref, high, total):
    pieces = probe_ref.shape[0]
    both = 2 if pieces % 2 == 0 else 1

    def one(i, total):
        left = jnp.concatenate([probe_ref[both * i + k, 0:high, :] for k in range(both)], axis=1)
        right = jnp.concatenate([kernel_ref[both * i + k] for k in range(both)], axis=1)
        return total + mxu(left, right, NT)

    count = pieces // both
    return lax.fori_loop(0, count, one, total, unroll=count <= 8)


def leaf_body(groups, blocks, place_ref, sizes_ref, ranks_ref, *refs):
    probe_refs = refs[: groups * blocks]
    kernel_refs = refs[groups * blocks : groups * (blocks + 1)]
    h_ref, w_ref, m_ref, t_ref = refs[groups * (blocks + 1) :]
    n = h_ref.shape[0]
    rows, cols = grids(n)
    high = n // blocks
    for o in range(blocks):
        total = jnp.zeros((high, n), F32)
        for g in range(groups):
            total = accumulate(probe_refs[groups * o + g], kernel_refs[g], high, total)
        at = pl.multiple_of((place_ref[0] ^ o) * high, high)
        m_ref[pl.ds(at, high), :] = total
    used = sizes_ref[0]
    half = n // 2
    inside = cols - jnp.where(cols >= half, half, 0) < used
    matrix = jnp.where(inside, m_ref[...], 0.0)
    m_ref[...] = matrix
    gram = dot3(matrix, matrix, NT)
    shift, by_row, by_col = factorize(gram, t_ref)
    in_rank = rows < ranks_ref[0]
    value = jnp.where(in_rank, projected_rows(t_ref, by_row, by_col), 0.0)
    h_ref[...] = dot3(value, value, TN) * shift
    w_ref[...] = jnp.where(in_rank, inverse_factor(t_ref, by_row, by_col) * lax.rsqrt(shift), 0.0)


def basis_body(w_ref, m_ref, b_ref):
    b_ref[...] = dot3(w_ref[...], m_ref[...], NN)


def node_body(own_ref, other_ref, h_ref, packed_ref, t_ref):
    shift, by_row, by_col = factorize(own_ref[...] + other_ref[...], t_ref)
    value = projected_rows(t_ref, by_row, by_col)
    h_ref[...] = dot3(value, value, TN) * shift
    fold(h_ref, packed_ref)


def top_body(own_ref, other_ref, z_ref, t_ref):
    shift, by_row, by_col = factorize(unfold_add(other_ref, own_ref), t_ref)
    value = projected_rows(t_ref, by_row, by_col)
    z_ref[...] = (value * jnp.sqrt(shift)).T


def call(body, outs, operands, specs=None, scratch=(), flops=0):
    bytes_used = sum(x.size * x.dtype.itemsize for x in (*outs, *operands))
    return pl.pallas_call(
        body,
        out_shape=list(outs),
        in_specs=list(specs or [VMEM] * len(operands)),
        out_specs=[VMEM] * len(outs),
        scratch_shapes=list(scratch),
        cost_estimate=pl.CostEstimate(flops=flops, bytes_accessed=bytes_used, transcendentals=0),
        compiler_params=pltpu.CompilerParams(vmem_limit_bytes=2 * bytes_used + (6 << 20)),
    )(*operands)


def flip(value, rows_mask, probe_mask=0):
    probe_size = lax.axis_size("probe")
    if probe_mask == 0:
        pairs = [(i, i ^ rows_mask) for i in range(lax.axis_size("rows"))]
        return lax.ppermute(value, "rows", pairs)
    if rows_mask == 0:
        pairs = [(i, i ^ probe_mask) for i in range(probe_size)]
        return lax.ppermute(value, "probe", pairs)
    pairs = [
        (i * probe_size + j, (i ^ rows_mask) * probe_size + (j ^ probe_mask))
        for i in range(lax.axis_size("rows"))
        for j in range(probe_size)
    ]
    return lax.ppermute(value, ("rows", "probe"), pairs)


def per_device(targets, sources, probes, cluster_sizes, leaf_ranks):
    rows_size = lax.axis_size("rows")
    probe_size = lax.axis_size("probe")
    col_total = sources.shape[1] * rows_size
    high = probes.shape[0]
    n = high * probe_size
    leaf_rows = targets.shape[1] // probe_size
    place = lax.axis_index("probe")

    points = lax.dynamic_slice_in_dim(targets, place * leaf_rows, leaf_rows, 1)
    points = jnp.pad(points, ((0, 8 - points.shape[0]), (0, 0)))

    def evaluate(arrays):
        outs = [jax.ShapeDtypeStruct((x.shape[0], 2 * leaf_rows, x.shape[2]), BF16) for x in arrays]
        return call(
            lambda *refs: kernel_body(col_total, high, *refs), outs, [points, *arrays],
            flops=2000 * sum(x.size for x in outs),
        )

    pieces = jnp.concatenate([probes, jnp.pad(sources, ((0, 16 - sources.shape[0]), (0, 0)))], axis=0)[None]
    mask = rows_size // 2
    while mask > 2:
        low = mask // 2 if mask // 2 > 2 else 0
        received = [flip(pieces, m) for m in ([low, mask, mask + low] if low else [mask])]
        pieces = jnp.concatenate([pieces, *received], axis=0)
        mask //= 4 if low else 2
    masks = [0, 2] if rows_size > 2 else [0]
    values = []
    groups = []
    for o in range(probe_size):
        both = []
        for m in masks:
            near = pieces if (m, o) == (0, 0) else flip(pieces, m, o)
            far = flip(near, 1)
            both += [near, far]
            if o == 0:
                values += evaluate([near, far])
        groups.append(both)

    square = jax.ShapeDtypeStruct((n, n), F32)
    scratch = [pltpu.VMEM((n, n), F32)]
    flat = [x for both in groups for x in both]
    h, w, m = call(
        lambda *refs: leaf_body(len(values), probe_size, *refs), [square] * 3,
        [place[None], cluster_sizes, leaf_ranks, *flat, *values],
        specs=[SMEM] * 3 + [VMEM] * (len(flat) + len(values)), scratch=scratch, flops=n**3,
    )
    other = flip(h, 1)
    basis = call(basis_body, [square], [w, m], flops=60 * n**3)[0]
    packed = jax.ShapeDtypeStruct((n + 8, n // 2), F32)
    h, sent = call(node_body, [square, packed], [h, other], scratch=scratch, flops=n**3)
    other = flip(sent, 2)
    top = call(top_body, [square], [h, other], scratch=scratch, flops=n**3)[0]
    return (basis.reshape(n, 2, leaf_rows), top[None])


def solution(mesh):
    return jax.shard_map(
        per_device,
        mesh=mesh,
        in_specs=(
            P(None, "rows"),
            P(None, "rows"),
            P("probe", "rows"),
            P(("rows", "probe")),
            P(("rows", "probe")),
        ),
        out_specs=(P(None, None, ("rows", "probe")), P(("rows", "probe"), None, None)),
        check_vma=False,
    )
```

```python
import math

import jax
import jax.numpy as jnp
from jax import lax
from jax.experimental import pallas as pl
from jax.experimental.pallas import tpu as pltpu
from jax.sharding import PartitionSpec as P


wavenumber = 30.0
softening = 0.02

F32 = jnp.float32
BF16 = jnp.bfloat16
VMEM = pl.BlockSpec(memory_space=pltpu.VMEM)
SMEM = pl.BlockSpec(memory_space=pltpu.SMEM)
NN = ((1,), (0,))
NT = ((1,), (1,))
TN = ((0,), (0,))

LANES = 128
PANEL = 32
GROUP = 8
CHUNK = 256


def split_bf16(value):
    high = value.astype(BF16)
    return high, (value - high.astype(F32)).astype(BF16)


def mxu(left, right, dims):
    return lax.dot_general(left, right, (dims, ((), ())), preferred_element_type=F32)


def dot3(left, right, dims):
    lh, ll = split_bf16(left)
    rh, rl = split_bf16(right)
    return mxu(lh, rh, dims) + (mxu(lh, rl, dims) + mxu(ll, rh, dims))


def pick_lane(tile, lane):
    where = jnp.full(tile.shape, lane, jnp.int32)
    return jnp.take_along_axis(tile, where, axis=1, mode="promise_in_bounds")


def pick_row(tile, row):
    return jnp.broadcast_to(tile[row : row + 1, :], tile.shape)


def sweep(t_ref):
    n = t_ref.shape[0]
    tiles = n // LANES
    steps = PANEL // 8
    lane = lax.broadcasted_iota(jnp.int32, (8, LANES), 1)
    row = lax.broadcasted_iota(jnp.int32, (8, LANES), 0)
    along_lanes = [jnp.ones((8, LANES), F32) for _ in range(tiles)]
    along_rows = []
    for start in range(0, n, PANEL):
        at, low = divmod(start, LANES)
        block = [
            [t_ref[start + 8 * i : start + 8 * i + 8, LANES * t : LANES * (t + 1)] for t in range(tiles)]
            for i in range(steps)
        ]
        pivots = [jnp.zeros((8, LANES), F32) for _ in range(steps)]
        for first in range(0, PANEL, GROUP):
            i0 = first // 8
            cols = [[pick_lane(block[i][at], low + first + a) for i in range(i0, steps)] for a in range(GROUP)]
            for a in range(GROUP):
                here = lane == low + first + a
                pivot = pick_row(cols[a][0], a)
                inverse = 1.0 / pivot
                along_lanes[at] = jnp.where(here, pivot, along_lanes[at])
                pivots[i0] = jnp.where(row == a, pivot, pivots[i0])
                factors = [c * inverse for c in cols[a]]
                factors[0] = jnp.where(row > a, factors[0], 0.0)
                for b in range(a + 1, GROUP):
                    entry = pick_row(cols[b][0], a)
                    cols[b] = [c - f * entry for c, f in zip(cols[b], factors)]
                swept = [pick_row(block[i0][t], a) for t in range(tiles)]
                swept[at] = jnp.where(here, 2.0 * swept[at], swept[at])
                for x, i in enumerate(range(i0, steps)):
                    for t in range(tiles):
                        block[i][t] = block[i][t] - factors[x] * swept[t]
        for i in range(steps):
            for t in range(tiles):
                t_ref[start + 8 * i : start + 8 * i + 8, LANES * t : LANES * (t + 1)] = block[i][t]
        along_rows += pivots
        end = start + PANEL
        if end < n:
            rowi = lax.broadcasted_iota(jnp.int32, (PANEL, n), 0)
            coli = lax.broadcasted_iota(jnp.int32, (PANEL, n), 1)
            whole = jnp.concatenate([jnp.concatenate(x, axis=1) for x in block], axis=0)
            kept = jnp.where((coli < end) & (coli - start > rowi), 0.0, whole)
            scale = 1.0 / jnp.concatenate(pivots, axis=0)
            base = end // LANES * LANES
            factors = whole[:, base:] * jnp.concatenate([scale] * ((n - base) // LANES), axis=1)
            fh, fl = split_bf16(factors)
            kh, kl = split_bf16(kept)
            left = jnp.concatenate([fh, fh, fl], axis=0)
            left = left.T
            right = jnp.concatenate([kh, kl, kh], axis=0)
            for to in range(end, n, CHUNK):
                high = min(CHUNK, n - to)
                change = mxu(left[to - base : to - base + high, :], right, NN)
                colr = lax.broadcasted_iota(jnp.int32, (high, LANES), 1)
                for t in range(tiles):
                    at_t = slice(LANES * t, LANES * (t + 1))
                    rest = t_ref[to : to + high, at_t]
                    if t == at:
                        rest = jnp.where((colr >= low) & (colr < low + PANEL), 0.0, rest)
                    t_ref[to : to + high, at_t] = rest - change[:, at_t]
    return along_lanes, along_rows


def grids(n):
    rows = lax.broadcasted_iota(jnp.int32, (n, n), 0)
    cols = lax.broadcasted_iota(jnp.int32, (n, n), 1)
    return rows, cols


def factorize(gram, t_ref):
    n = gram.shape[0]
    rows, cols = grids(n)
    diagonal = jnp.where(rows == cols, gram, 0.0)
    shift = jnp.sum(jnp.sum(diagonal, axis=0, keepdims=True), axis=1, keepdims=True) / n
    t_ref[...] = gram / shift + jnp.where(rows == cols, 1.0, 0.0)
    along_lanes, along_rows = sweep(t_ref)
    by_col = jnp.concatenate([jnp.broadcast_to(x[0:1, :], (n, LANES)) for x in along_lanes], axis=1)
    by_row = jnp.concatenate([jnp.concatenate([x] * (n // LANES), axis=1) for x in along_rows], axis=0)
    return shift, by_row, by_col


def projected_rows(t_ref, by_row, by_col):
    rows, cols = grids(t_ref.shape[0])
    held = t_ref[...]
    return lax.rsqrt(by_row) * jnp.where(
        rows < cols, held, jnp.where(rows > cols, -held / by_col, by_row - 1.0)
    )


def inverse_factor(t_ref, by_row, by_col):
    rows, cols = grids(t_ref.shape[0])
    held = t_ref[...]
    return lax.rsqrt(by_row) * jnp.where(rows > cols, held / by_col, jnp.where(rows == cols, 1.0, 0.0))


def fold(full_ref, packed_ref):
    n = full_ref.shape[0]
    half = n // 2
    rows, cols = grids(half)
    upper = full_ref[0:half, 0:half]
    lower = full_ref[half:n, half:n]
    packed_ref[0:half, :] = full_ref[0:half, half:n]
    packed_ref[half:n, :] = jnp.where(rows <= cols, upper, lower)
    packed_ref[n : n + 8, :] = jnp.broadcast_to(
        jnp.sum(jnp.where(rows == cols, lower, 0.0), axis=0, keepdims=True), (8, half)
    )


def unfold_add(packed_ref, full_ref):
    n = full_ref.shape[0]
    half = n // 2
    rows, cols = grids(half)
    corner = packed_ref[0:half, :]
    both = packed_ref[half:n, :]
    turned = both.T
    line = jnp.broadcast_to(packed_ref[n : n + 1, :], (half, half))
    upper = jnp.where(rows <= cols, both, turned)
    lower = jnp.where(rows == cols, line, jnp.where(rows > cols, both, turned))
    top = jnp.concatenate([upper, corner], axis=1)
    bottom = jnp.concatenate([corner.T, lower], axis=1)
    return full_ref[...] + jnp.concatenate([top, bottom], axis=0)


def kernel_body(col_total, high, targets_ref, *refs):
    m = targets_ref.shape[1]
    width = refs[0].shape[2]
    turned = jnp.concatenate([targets_ref[...], jnp.zeros((m - 8, m), F32)], axis=0).T
    points = [jnp.broadcast_to(turned[:, c : c + 1], (m, width)) for c in range(3)]
    count = len(refs) // 2
    for piece_ref, out_ref in zip(refs[:count], refs[count:]):
        for i in range(piece_ref.shape[0]):
            source = piece_ref[i, high : high + 3, :].astype(F32)
            first, second = kernel_values(source, points, col_total)
            out_ref[i, 0:m, :] = first
            out_ref[i, m : 2 * m, :] = second


def kernel_values(source, points, col_total):
    size = 1.0 / math.sqrt(col_total)
    turns = wavenumber * 2.0 / math.pi
    h = math.pi / 2
    square = softening * softening
    for c in range(3):
        diff = source[c : c + 1, :] - points[c]
        square = square + diff * diff
    near = lax.rsqrt(square)
    amplitude = near * size
    quarter = (square * near) * turns
    whole = jnp.round(quarter)
    rest = quarter - whole
    r2 = rest * rest
    sine = rest * (h + r2 * (-(h**3) / 6 + r2 * (h**5 / 120 + r2 * (-(h**7) / 5040))))
    cosine = 1.0 + r2 * (-(h**2) / 2 + r2 * (h**4 / 24 + r2 * (-(h**6) / 720 + r2 * (h**8 / 40320))))
    count = whole.astype(jnp.int32)
    odd = (count & 1) == 1
    first = jnp.where(odd, sine, cosine)
    second = jnp.where(odd, cosine, sine)
    first = jnp.where(((count + 1) & 2) == 0, first, -first)
    second = jnp.where((count & 2) == 0, second, -second)
    return (amplitude * first).astype(BF16), (amplitude * second).astype(BF16)


def accumulate(probe_ref, kernel_ref, high, total):
    pieces = probe_ref.shape[0]
    both = 2 if pieces % 2 == 0 else 1

    def one(i, total):
        left = jnp.concatenate([probe_ref[both * i + k, 0:high, :] for k in range(both)], axis=1)
        right = jnp.concatenate([kernel_ref[both * i + k] for k in range(both)], axis=1)
        return total + mxu(left, right, NT)

    count = pieces // both
    return lax.fori_loop(0, count, one, total, unroll=count <= 8)


def leaf_body(groups, blocks, place_ref, sizes_ref, ranks_ref, *refs):
    probe_refs = refs[: groups * blocks]
    kernel_refs = refs[groups * blocks : groups * (blocks + 1)]
    h_ref, w_ref, m_ref, t_ref = refs[groups * (blocks + 1) :]
    n = h_ref.shape[0]
    rows, cols = grids(n)
    high = n // blocks
    for o in range(blocks):
        total = jnp.zeros((high, n), F32)
        for g in range(groups):
            total = accumulate(probe_refs[groups * o + g], kernel_refs[g], high, total)
        at = pl.multiple_of((place_ref[0] ^ o) * high, high)
        m_ref[pl.ds(at, high), :] = total
    used = sizes_ref[0]
    half = n // 2
    inside = cols - jnp.where(cols >= half, half, 0) < used
    matrix = jnp.where(inside, m_ref[...], 0.0)
    m_ref[...] = matrix
    gram = dot3(matrix, matrix, NT)
    shift, by_row, by_col = factorize(gram, t_ref)
    in_rank = rows < ranks_ref[0]
    value = jnp.where(in_rank, projected_rows(t_ref, by_row, by_col), 0.0)
    h_ref[...] = dot3(value, value, TN) * shift
    w_ref[...] = jnp.where(in_rank, inverse_factor(t_ref, by_row, by_col) * lax.rsqrt(shift), 0.0)


def basis_body(w_ref, m_ref, b_ref):
    b_ref[...] = dot3(w_ref[...], m_ref[...], NN)


def node_body(own_ref, other_ref, h_ref, packed_ref, t_ref):
    shift, by_row, by_col = factorize(own_ref[...] + other_ref[...], t_ref)
    value = projected_rows(t_ref, by_row, by_col)
    h_ref[...] = dot3(value, value, TN) * shift
    fold(h_ref, packed_ref)


def top_body(own_ref, other_ref, z_ref, t_ref):
    shift, by_row, by_col = factorize(unfold_add(other_ref, own_ref), t_ref)
    value = projected_rows(t_ref, by_row, by_col)
    z_ref[...] = (value * jnp.sqrt(shift)).T


def call(body, outs, operands, specs=None, scratch=(), flops=0):
    bytes_used = sum(x.size * x.dtype.itemsize for x in (*outs, *operands))
    return pl.pallas_call(
        body,
        out_shape=list(outs),
        in_specs=list(specs or [VMEM] * len(operands)),
        out_specs=[VMEM] * len(outs),
        scratch_shapes=list(scratch),
        cost_estimate=pl.CostEstimate(flops=flops, bytes_accessed=bytes_used, transcendentals=0),
        compiler_params=pltpu.CompilerParams(vmem_limit_bytes=2 * bytes_used + (6 << 20)),
    )(*operands)


def flip(value, rows_mask, probe_mask=0):
    probe_size = lax.axis_size("probe")
    if probe_mask == 0:
        pairs = [(i, i ^ rows_mask) for i in range(lax.axis_size("rows"))]
        return lax.ppermute(value, "rows", pairs)
    if rows_mask == 0:
        pairs = [(i, i ^ probe_mask) for i in range(probe_size)]
        return lax.ppermute(value, "probe", pairs)
    pairs = [
        (i * probe_size + j, (i ^ rows_mask) * probe_size + (j ^ probe_mask))
        for i in range(lax.axis_size("rows"))
        for j in range(probe_size)
    ]
    return lax.ppermute(value, ("rows", "probe"), pairs)


def per_device(targets, sources, probes, cluster_sizes, leaf_ranks):
    rows_size = lax.axis_size("rows")
    probe_size = lax.axis_size("probe")
    col_total = sources.shape[1] * rows_size
    high = probes.shape[0]
    n = high * probe_size
    leaf_rows = targets.shape[1] // probe_size
    place = lax.axis_index("probe")

    points = lax.dynamic_slice_in_dim(targets, place * leaf_rows, leaf_rows, 1)
    points = jnp.pad(points, ((0, 8 - points.shape[0]), (0, 0)))

    def evaluate(arrays):
        outs = [jax.ShapeDtypeStruct((x.shape[0], 2 * leaf_rows, x.shape[2]), BF16) for x in arrays]
        return call(
            lambda *refs: kernel_body(col_total, high, *refs), outs, [points, *arrays],
            flops=2000 * sum(x.size for x in outs),
        )

    pieces = jnp.concatenate([probes, jnp.pad(sources, ((0, 16 - sources.shape[0]), (0, 0)))], axis=0)[None]
    mask = rows_size // 2
    while mask > 2:
        low = mask // 2 if mask // 2 > 2 else 0
        received = [flip(pieces, m) for m in ([low, mask, mask + low] if low else [mask])]
        pieces = jnp.concatenate([pieces, *received], axis=0)
        mask //= 4 if low else 2
    masks = [0, 2] if rows_size > 2 else [0]
    values = []
    groups = []
    for o in range(probe_size):
        both = []
        for m in masks:
            near = pieces if (m, o) == (0, 0) else flip(pieces, m, o)
            far = flip(near, 1)
            both += [near, far]
            if o == 0:
                for x in (near, far):
                    values += evaluate([x])
        groups.append(both)

    square = jax.ShapeDtypeStruct((n, n), F32)
    scratch = [pltpu.VMEM((n, n), F32)]
    flat = [x for both in groups for x in both]
    h, w, m = call(
        lambda *refs: leaf_body(len(values), probe_size, *refs), [square] * 3,
        [place[None], cluster_sizes, leaf_ranks, *flat, *values],
        specs=[SMEM] * 3 + [VMEM] * (len(flat) + len(values)), scratch=scratch, flops=n**3,
    )
    other = flip(h, 1)
    basis = call(basis_body, [square], [w, m], flops=60 * n**3)[0]
    packed = jax.ShapeDtypeStruct((n + 8, n // 2), F32)
    h, sent = call(node_body, [square, packed], [h, other], scratch=scratch, flops=n**3)
    other = flip(sent, 2)
    top = call(top_body, [square], [h, other], scratch=scratch, flops=n**3)[0]
    return (basis.reshape(n, 2, leaf_rows), top[None])


def solution(mesh):
    return jax.shard_map(
        per_device,
        mesh=mesh,
        in_specs=(
            P(None, "rows"),
            P(None, "rows"),
            P("probe", "rows"),
            P(("rows", "probe")),
            P(("rows", "probe")),
        ),
        out_specs=(P(None, None, ("rows", "probe")), P(("rows", "probe"), None, None)),
        check_vma=False,
    )
```

```python
import math

import jax
import jax.numpy as jnp
from jax import lax
from jax.experimental import pallas as pl
from jax.experimental.pallas import tpu as pltpu
from jax.sharding import PartitionSpec as P


wavenumber = 30.0
softening = 0.02

F32 = jnp.float32
BF16 = jnp.bfloat16
VMEM = pl.BlockSpec(memory_space=pltpu.VMEM)
SMEM = pl.BlockSpec(memory_space=pltpu.SMEM)
NN = ((1,), (0,))
NT = ((1,), (1,))
TN = ((0,), (0,))

LANES = 128
PANEL = 64
CHUNK = 256


def split_bf16(value):
    high = value.astype(BF16)
    return high, (value - high.astype(F32)).astype(BF16)


def mxu(left, right, dims):
    return lax.dot_general(left, right, (dims, ((), ())), preferred_element_type=F32)


def dot3(left, right, dims):
    lh, ll = split_bf16(left)
    rh, rl = split_bf16(right)
    return mxu(lh, rh, dims) + (mxu(lh, rl, dims) + mxu(ll, rh, dims))


def pick_lane(tile, lane):
    where = jnp.full(tile.shape, lane, jnp.int32)
    return jnp.take_along_axis(tile, where, axis=1, mode="promise_in_bounds")


def pick_row(tile, row):
    return jnp.broadcast_to(tile[row : row + 1, :], tile.shape)


def sweep(t_ref):
    n = t_ref.shape[0]
    tiles = n // LANES
    steps = PANEL // 8
    lane = lax.broadcasted_iota(jnp.int32, (8, LANES), 1)
    row = lax.broadcasted_iota(jnp.int32, (8, LANES), 0)
    along_lanes = [jnp.zeros((8, LANES), F32) for _ in range(tiles)]
    along_rows = []
    for start in range(0, n, PANEL):
        at, low = divmod(start, LANES)
        block = [
            [t_ref[start + 8 * i : start + 8 * i + 8, LANES * t : LANES * (t + 1)] for t in range(tiles)]
            for i in range(steps)
        ]
        pivots = [jnp.zeros((8, LANES), F32) for _ in range(steps)]
        ahead = None
        for i0 in range(steps):
            first = low + 8 * i0

            def columns(i, base):
                return [pick_lane(block[i][at], base + a) for a in range(8)]

            cols = ahead or columns(i0, first)
            below = {i: columns(i, first) for i in range(i0 + 1, steps)}
            after = columns(i0 + 1, first + 8) if i0 + 1 < steps else None
            sums = [jnp.zeros((8, LANES), F32)] * 8
            for a in range(8):
                here = lane == first + a
                pivot = pick_row(cols[a], a)
                inverse = 1.0 / pivot
                pivots[i0] = jnp.where(row == a, pivot, pivots[i0])
                factor = jnp.where(row > a, cols[a] * inverse, 0.0)
                entries = {b: pick_row(cols[b], a) for b in range(a + 1, 8)}
                for b in entries:
                    cols[b] = cols[b] - factor * entries[b]
                swept = [pick_row(block[i0][t], a) for t in range(tiles)]
                swept[at] = jnp.where(here, 2.0 * swept[at], swept[at])
                for t in range(tiles):
                    block[i0][t] = block[i0][t] - factor * swept[t]
                for i, mine in below.items():
                    factor = mine[a] * inverse
                    for b in entries:
                        mine[b] = mine[b] - factor * entries[b]
                    for t in range(tiles):
                        block[i][t] = block[i][t] - factor * swept[t]
                    if after and i == i0 + 1:
                        sums = [x + factor * pick_row(mine[a], b) for b, x in enumerate(sums)]
            along_lanes[at] = along_lanes[at] + jnp.where(lane == first + row, block[i0][at], 0.0)
            ahead = after and [x - y for x, y in zip(after, sums)]
        for i in range(steps):
            for t in range(tiles):
                t_ref[start + 8 * i : start + 8 * i + 8, LANES * t : LANES * (t + 1)] = block[i][t]
        along_rows += pivots
        end = start + PANEL
        if end < n:
            rowi = lax.broadcasted_iota(jnp.int32, (PANEL, n), 0)
            coli = lax.broadcasted_iota(jnp.int32, (PANEL, n), 1)
            whole = jnp.concatenate([jnp.concatenate(x, axis=1) for x in block], axis=0)
            kept = jnp.where((coli < end) & (coli - start > rowi), 0.0, whole)
            scale = 1.0 / jnp.concatenate(pivots, axis=0)
            base = end // LANES * LANES
            factors = whole[:, base:] * jnp.concatenate([scale] * ((n - base) // LANES), axis=1)
            fh, fl = split_bf16(factors)
            kh, kl = split_bf16(kept)
            left = jnp.concatenate([fh, fh, fl], axis=0).T
            right = jnp.concatenate([kh, kl, kh], axis=0)
            for to in range(end, n, CHUNK):
                high = min(CHUNK, n - to)
                change = mxu(left[to - base : to - base + high, :], right, NN)
                colr = lax.broadcasted_iota(jnp.int32, (high, LANES), 1)
                for t in range(tiles):
                    at_t = slice(LANES * t, LANES * (t + 1))
                    rest = t_ref[to : to + high, at_t]
                    if t == at:
                        rest = jnp.where((colr >= low) & (colr < low + PANEL), 0.0, rest)
                    t_ref[to : to + high, at_t] = rest - change[:, at_t]
    return along_lanes, along_rows


def grids(n):
    rows = lax.broadcasted_iota(jnp.int32, (n, n), 0)
    cols = lax.broadcasted_iota(jnp.int32, (n, n), 1)
    return rows, cols


def factorize(gram, t_ref):
    n = gram.shape[0]
    rows, cols = grids(n)
    diagonal = jnp.where(rows == cols, gram, 0.0)
    shift = jnp.sum(jnp.sum(diagonal, axis=0, keepdims=True), axis=1, keepdims=True) / n
    t_ref[...] = gram / shift + jnp.where(rows == cols, 1.0, 0.0)
    along_lanes, along_rows = sweep(t_ref)
    sums = [jnp.sum(x, axis=0, keepdims=True) for x in along_lanes]
    by_col = jnp.concatenate([jnp.broadcast_to(x, (n, LANES)) for x in sums], axis=1)
    by_row = jnp.concatenate([jnp.concatenate([x] * (n // LANES), axis=1) for x in along_rows], axis=0)
    return shift, by_row, by_col


def projected_rows(t_ref, by_row, by_col):
    rows, cols = grids(t_ref.shape[0])
    held = t_ref[...]
    return lax.rsqrt(by_row) * jnp.where(
        rows < cols, held, jnp.where(rows > cols, -held / by_col, by_row - 1.0)
    )


def inverse_factor(t_ref, by_row, by_col):
    rows, cols = grids(t_ref.shape[0])
    held = t_ref[...]
    return lax.rsqrt(by_row) * jnp.where(rows > cols, held / by_col, jnp.where(rows == cols, 1.0, 0.0))


def fold(full_ref, packed_ref):
    n = full_ref.shape[0]
    half = n // 2
    rows, cols = grids(half)
    upper = full_ref[0:half, 0:half]
    lower = full_ref[half:n, half:n]
    packed_ref[0:half, :] = full_ref[0:half, half:n]
    packed_ref[half:n, :] = jnp.where(rows <= cols, upper, lower)
    packed_ref[n : n + 8, :] = jnp.broadcast_to(
        jnp.sum(jnp.where(rows == cols, lower, 0.0), axis=0, keepdims=True), (8, half)
    )


def unfold_add(packed_ref, full_ref):
    n = full_ref.shape[0]
    half = n // 2
    rows, cols = grids(half)
    corner = packed_ref[0:half, :]
    both = packed_ref[half:n, :]
    turned = both.T
    line = jnp.broadcast_to(packed_ref[n : n + 1, :], (half, half))
    upper = jnp.where(rows <= cols, both, turned)
    lower = jnp.where(rows == cols, line, jnp.where(rows > cols, both, turned))
    top = jnp.concatenate([upper, corner], axis=1)
    bottom = jnp.concatenate([corner.T, lower], axis=1)
    return full_ref[...] + jnp.concatenate([top, bottom], axis=0)


def kernel_body(col_total, high, targets_ref, *refs):
    m = targets_ref.shape[1]
    width = refs[0].shape[2]
    turned = jnp.concatenate([targets_ref[...], jnp.zeros((m - 8, m), F32)], axis=0).T
    points = [jnp.broadcast_to(turned[:, c : c + 1], (m, width)) for c in range(3)]
    count = len(refs) // 2
    for piece_ref, out_ref in zip(refs[:count], refs[count:]):
        for i in range(piece_ref.shape[0]):
            source = piece_ref[i, high : high + 3, :].astype(F32)
            first, second = kernel_values(source, points, col_total)
            out_ref[i, 0:m, :] = first
            out_ref[i, m : 2 * m, :] = second


def kernel_values(source, points, col_total):
    size = 1.0 / math.sqrt(col_total)
    turns = wavenumber * 2.0 / math.pi
    h = math.pi / 2
    square = softening * softening
    for c in range(3):
        diff = source[c : c + 1, :] - points[c]
        square = square + diff * diff
    near = lax.rsqrt(square)
    amplitude = near * size
    quarter = (square * near) * turns
    whole = jnp.round(quarter)
    rest = quarter - whole
    r2 = rest * rest
    sine = rest * (h + r2 * (-(h**3) / 6 + r2 * (h**5 / 120 + r2 * (-(h**7) / 5040))))
    cosine = 1.0 + r2 * (-(h**2) / 2 + r2 * (h**4 / 24 + r2 * (-(h**6) / 720 + r2 * (h**8 / 40320))))
    count = whole.astype(jnp.int32)
    odd = (count & 1) == 1
    first = jnp.where(odd, sine, cosine)
    second = jnp.where(odd, cosine, sine)
    first = jnp.where(((count + 1) & 2) == 0, first, -first)
    second = jnp.where((count & 2) == 0, second, -second)
    return (amplitude * first).astype(BF16), (amplitude * second).astype(BF16)


def accumulate(probe_ref, kernel_ref, high, total):
    pieces = probe_ref.shape[0]
    both = 2 if pieces % 2 == 0 else 1

    def one(i, total):
        left = jnp.concatenate([probe_ref[both * i + k, 0:high, :] for k in range(both)], axis=1)
        right = jnp.concatenate([kernel_ref[both * i + k] for k in range(both)], axis=1)
        return total + mxu(left, right, NT)

    count = pieces // both
    return lax.fori_loop(0, count, one, total, unroll=count <= 8)


def leaf_body(groups, blocks, place_ref, sizes_ref, ranks_ref, *refs):
    probe_refs = refs[: groups * blocks]
    kernel_refs = refs[groups * blocks : groups * (blocks + 1)]
    h_ref, w_ref, m_ref, t_ref = refs[groups * (blocks + 1) :]
    n = h_ref.shape[0]
    rows, cols = grids(n)
    high = n // blocks
    for o in range(blocks):
        total = jnp.zeros((high, n), F32)
        for g in range(groups):
            total = accumulate(probe_refs[groups * o + g], kernel_refs[g], high, total)
        at = pl.multiple_of((place_ref[0] ^ o) * high, high)
        m_ref[pl.ds(at, high), :] = total
    used = sizes_ref[0]
    half = n // 2
    inside = cols - jnp.where(cols >= half, half, 0) < used
    matrix = jnp.where(inside, m_ref[...], 0.0)
    m_ref[...] = matrix
    gram = dot3(matrix, matrix, NT)
    shift, by_row, by_col = factorize(gram, t_ref)
    in_rank = rows < ranks_ref[0]
    value = jnp.where(in_rank, projected_rows(t_ref, by_row, by_col), 0.0)
    h_ref[...] = dot3(value, value, TN) * shift
    w_ref[...] = jnp.where(in_rank, inverse_factor(t_ref, by_row, by_col) * lax.rsqrt(shift), 0.0)


def basis_body(w_ref, m_ref, b_ref):
    b_ref[...] = dot3(w_ref[...], m_ref[...], NN)


def node_body(own_ref, other_ref, h_ref, packed_ref, t_ref):
    shift, by_row, by_col = factorize(own_ref[...] + other_ref[...], t_ref)
    value = projected_rows(t_ref, by_row, by_col)
    h_ref[...] = dot3(value, value, TN) * shift
    fold(h_ref, packed_ref)


def top_body(own_ref, other_ref, z_ref, t_ref):
    shift, by_row, by_col = factorize(unfold_add(other_ref, own_ref), t_ref)
    value = projected_rows(t_ref, by_row, by_col)
    z_ref[...] = (value * jnp.sqrt(shift)).T


def call(body, outs, operands, specs=None, scratch=(), flops=0):
    bytes_used = sum(x.size * x.dtype.itemsize for x in (*outs, *operands))
    return pl.pallas_call(
        body,
        out_shape=list(outs),
        in_specs=list(specs or [VMEM] * len(operands)),
        out_specs=[VMEM] * len(outs),
        scratch_shapes=list(scratch),
        cost_estimate=pl.CostEstimate(flops=flops, bytes_accessed=bytes_used, transcendentals=0),
        compiler_params=pltpu.CompilerParams(vmem_limit_bytes=2 * bytes_used + (6 << 20)),
    )(*operands)


def flip(value, rows_mask, probe_mask=0):
    probe_size = lax.axis_size("probe")
    if probe_mask == 0:
        pairs = [(i, i ^ rows_mask) for i in range(lax.axis_size("rows"))]
        return lax.ppermute(value, "rows", pairs)
    if rows_mask == 0:
        pairs = [(i, i ^ probe_mask) for i in range(probe_size)]
        return lax.ppermute(value, "probe", pairs)
    pairs = [
        (i * probe_size + j, (i ^ rows_mask) * probe_size + (j ^ probe_mask))
        for i in range(lax.axis_size("rows"))
        for j in range(probe_size)
    ]
    return lax.ppermute(value, ("rows", "probe"), pairs)


def per_device(targets, sources, probes, cluster_sizes, leaf_ranks):
    rows_size = lax.axis_size("rows")
    probe_size = lax.axis_size("probe")
    col_total = sources.shape[1] * rows_size
    high = probes.shape[0]
    n = high * probe_size
    leaf_rows = targets.shape[1] // probe_size
    place = lax.axis_index("probe")

    points = lax.dynamic_slice_in_dim(targets, place * leaf_rows, leaf_rows, 1)
    points = jnp.pad(points, ((0, 8 - points.shape[0]), (0, 0)))

    def evaluate(arrays):
        outs = [jax.ShapeDtypeStruct((x.shape[0], 2 * leaf_rows, x.shape[2]), BF16) for x in arrays]
        return call(
            lambda *refs: kernel_body(col_total, high, *refs), outs, [points, *arrays],
            flops=2000 * sum(x.size for x in outs),
        )

    pieces = jnp.concatenate([probes, jnp.pad(sources, ((0, 16 - sources.shape[0]), (0, 0)))], axis=0)[None]
    mask = rows_size // 2
    while mask > 2:
        low = mask // 2 if mask // 2 > 2 else 0
        received = [flip(pieces, m) for m in ([low, mask, mask + low] if low else [mask])]
        pieces = jnp.concatenate([pieces, *received], axis=0)
        mask //= 4 if low else 2
    masks = [0, 2] if rows_size > 2 else [0]
    values = []
    groups = []
    for o in range(probe_size):
        both = []
        for m in masks:
            near = pieces if (m, o) == (0, 0) else flip(pieces, m, o)
            far = flip(near, 1)
            both += [near, far]
            if o == 0:
                for x in (near, far):
                    values += evaluate([x])
        groups.append(both)

    square = jax.ShapeDtypeStruct((n, n), F32)
    scratch = [pltpu.VMEM((n, n), F32)]
    flat = [x for both in groups for x in both]
    h, w, m = call(
        lambda *refs: leaf_body(len(values), probe_size, *refs), [square] * 3,
        [place[None], cluster_sizes, leaf_ranks, *flat, *values],
        specs=[SMEM] * 3 + [VMEM] * (len(flat) + len(values)), scratch=scratch, flops=n**3,
    )
    other = flip(h, 1)
    basis = call(basis_body, [square], [w, m], flops=60 * n**3)[0]
    packed = jax.ShapeDtypeStruct((n + 8, n // 2), F32)
    h, sent = call(node_body, [square, packed], [h, other], scratch=scratch, flops=n**3)
    other = flip(sent, 2)
    top = call(top_body, [square], [h, other], scratch=scratch, flops=n**3)[0]
    return (basis.reshape(n, 2, leaf_rows), top[None])


def solution(mesh):
    return jax.shard_map(
        per_device,
        mesh=mesh,
        in_specs=(
            P(None, "rows"),
            P(None, "rows"),
            P("probe", "rows"),
            P(("rows", "probe")),
            P(("rows", "probe")),
        ),
        out_specs=(P(None, None, ("rows", "probe")), P(("rows", "probe"), None, None)),
        check_vma=False,
    )
```

```python
import math

import jax
import jax.numpy as jnp
from jax import lax
from jax.experimental import pallas as pl
from jax.experimental.pallas import tpu as pltpu
from jax.sharding import PartitionSpec as P


wavenumber = 30.0
softening = 0.02

F32 = jnp.float32
BF16 = jnp.bfloat16
VMEM = pl.BlockSpec(memory_space=pltpu.VMEM)
SMEM = pl.BlockSpec(memory_space=pltpu.SMEM)
NN = ((1,), (0,))
NT = ((1,), (1,))

LANES = 128
PANEL = 64
CHUNK = 256


def split_bf16(value):
    high = value.astype(BF16)
    return high, (value - high.astype(F32)).astype(BF16)


def mxu(left, right, dims):
    return lax.dot_general(left, right, (dims, ((), ())), preferred_element_type=F32)


def dot3(left, right, dims):
    lh, ll = split_bf16(left)
    rh, rl = split_bf16(right)
    return mxu(lh, rh, dims) + (mxu(lh, rl, dims) + mxu(ll, rh, dims))


def rows_gram(value):
    n = value.shape[1]
    high, low = split_bf16(value)
    turned = jnp.concatenate([high, low], axis=1).T
    first = mxu(turned, high, NN)
    return first[:n] + (first[n:] + mxu(turned[:n], low, NN))


def pick_lane(tile, lane):
    where = jnp.full(tile.shape, lane, jnp.int32)
    return jnp.take_along_axis(tile, where, axis=1, mode="promise_in_bounds")


def pick_row(tile, row):
    return jnp.broadcast_to(tile[row : row + 1, :], tile.shape)


def sweep(t_ref):
    n = t_ref.shape[0]
    tiles = n // LANES
    steps = PANEL // 8
    lane = lax.broadcasted_iota(jnp.int32, (8, LANES), 1)
    row = lax.broadcasted_iota(jnp.int32, (8, LANES), 0)
    along_lanes = [jnp.zeros((8, LANES), F32) for _ in range(tiles)]
    along_rows = []
    for start in range(0, n, PANEL):
        at, low = divmod(start, LANES)
        block = [
            [t_ref[start + 8 * i : start + 8 * i + 8, LANES * t : LANES * (t + 1)] for t in range(tiles)]
            for i in range(steps)
        ]
        pivots = [jnp.zeros((8, LANES), F32) for _ in range(steps)]
        ahead = None
        for i0 in range(steps):
            first = low + 8 * i0

            def columns(i, base):
                return [pick_lane(block[i][at], base + a) for a in range(8)]

            cols = ahead or columns(i0, first)
            below = {i: columns(i, first) for i in range(i0 + 1, steps)}
            after = columns(i0 + 1, first + 8) if i0 + 1 < steps else None
            sums = [jnp.zeros((8, LANES), F32)] * 8
            for a in range(8):
                here = lane == first + a
                pivot = pick_row(cols[a], a)
                inverse = 1.0 / pivot
                pivots[i0] = jnp.where(row == a, pivot, pivots[i0])
                factor = jnp.where(row > a, cols[a] * inverse, 0.0)
                entries = {b: pick_row(cols[b], a) for b in range(a + 1, 8)}
                for b in entries:
                    cols[b] = cols[b] - factor * entries[b]
                swept = [pick_row(block[i0][t], a) for t in range(tiles)]
                swept[at] = jnp.where(here, 2.0 * swept[at], swept[at])
                for t in range(tiles):
                    block[i0][t] = block[i0][t] - factor * swept[t]
                for i, mine in below.items():
                    factor = mine[a] * inverse
                    for b in entries:
                        mine[b] = mine[b] - factor * entries[b]
                    for t in range(tiles):
                        block[i][t] = block[i][t] - factor * swept[t]
                    if after and i == i0 + 1:
                        sums = [x + factor * pick_row(mine[a], b) for b, x in enumerate(sums)]
            along_lanes[at] = along_lanes[at] + jnp.where(lane == first + row, block[i0][at], 0.0)
            ahead = after and [x - y for x, y in zip(after, sums)]
        for i in range(steps):
            for t in range(tiles):
                t_ref[start + 8 * i : start + 8 * i + 8, LANES * t : LANES * (t + 1)] = block[i][t]
        along_rows += pivots
        end = start + PANEL
        if end < n:
            rowi = lax.broadcasted_iota(jnp.int32, (PANEL, n), 0)
            coli = lax.broadcasted_iota(jnp.int32, (PANEL, n), 1)
            whole = jnp.concatenate([jnp.concatenate(x, axis=1) for x in block], axis=0)
            kept = jnp.where((coli < end) & (coli - start > rowi), 0.0, whole)
            scale = 1.0 / jnp.concatenate(pivots, axis=0)
            base = end // LANES * LANES
            factors = whole[:, base:] * jnp.concatenate([scale] * ((n - base) // LANES), axis=1)
            fh, fl = split_bf16(factors)
            kh, kl = split_bf16(kept)
            left = jnp.concatenate([fh, fh, fl], axis=0).T
            right = jnp.concatenate([kh, kl, kh], axis=0)
            for to in range(end, n, CHUNK):
                high = min(CHUNK, n - to)
                change = mxu(left[to - base : to - base + high, :], right, NN)
                colr = lax.broadcasted_iota(jnp.int32, (high, LANES), 1)
                for t in range(tiles):
                    at_t = slice(LANES * t, LANES * (t + 1))
                    rest = t_ref[to : to + high, at_t]
                    if t == at:
                        rest = jnp.where((colr >= low) & (colr < low + PANEL), 0.0, rest)
                    t_ref[to : to + high, at_t] = rest - change[:, at_t]
    return along_lanes, along_rows


def grids(n):
    rows = lax.broadcasted_iota(jnp.int32, (n, n), 0)
    cols = lax.broadcasted_iota(jnp.int32, (n, n), 1)
    return rows, cols


def factorize(gram, t_ref):
    n = gram.shape[0]
    rows, cols = grids(n)
    diagonal = jnp.where(rows == cols, gram, 0.0)
    shift = jnp.sum(jnp.sum(diagonal, axis=0, keepdims=True), axis=1, keepdims=True) / n
    t_ref[...] = gram / shift + jnp.where(rows == cols, 1.0, 0.0)
    along_lanes, along_rows = sweep(t_ref)
    sums = [jnp.sum(x, axis=0, keepdims=True) for x in along_lanes]
    by_col = jnp.concatenate([jnp.broadcast_to(x, (n, LANES)) for x in sums], axis=1)
    by_row = jnp.concatenate([jnp.concatenate([x] * (n // LANES), axis=1) for x in along_rows], axis=0)
    return shift, by_row, by_col


def projected_rows(t_ref, by_row, by_col):
    rows, cols = grids(t_ref.shape[0])
    held = t_ref[...]
    return lax.rsqrt(by_row) * jnp.where(
        rows < cols, held, jnp.where(rows > cols, -held / by_col, by_row - 1.0)
    )


def fold(full_ref, packed_ref):
    n = full_ref.shape[0]
    half = n // 2
    rows, cols = grids(half)
    upper = full_ref[0:half, 0:half]
    lower = full_ref[half:n, half:n]
    packed_ref[0:half, :] = full_ref[0:half, half:n]
    packed_ref[half:n, :] = jnp.where(rows <= cols, upper, lower)
    packed_ref[n : n + 8, :] = jnp.broadcast_to(
        jnp.sum(jnp.where(rows == cols, lower, 0.0), axis=0, keepdims=True), (8, half)
    )


def unfold_add(packed_ref, full_ref):
    n = full_ref.shape[0]
    half = n // 2
    rows, cols = grids(half)
    corner = packed_ref[0:half, :]
    both = packed_ref[half:n, :]
    turned = both.T
    line = jnp.broadcast_to(packed_ref[n : n + 1, :], (half, half))
    upper = jnp.where(rows <= cols, both, turned)
    lower = jnp.where(rows == cols, line, jnp.where(rows > cols, both, turned))
    top = jnp.concatenate([upper, corner], axis=1)
    bottom = jnp.concatenate([corner.T, lower], axis=1)
    return full_ref[...] + jnp.concatenate([top, bottom], axis=0)


def kernel_body(col_total, high, targets_ref, *refs):
    m = targets_ref.shape[1]
    width = refs[0].shape[2]
    turned = jnp.concatenate([targets_ref[...], jnp.zeros((m - 8, m), F32)], axis=0).T
    points = [jnp.broadcast_to(turned[:, c : c + 1], (m, width)) for c in range(3)]
    count = len(refs) // 2
    for piece_ref, out_ref in zip(refs[:count], refs[count:]):
        for i in range(piece_ref.shape[0]):
            source = piece_ref[i, high : high + 3, :].astype(F32)
            first, second = kernel_values(source, points, col_total)
            out_ref[i, 0:m, :] = first
            out_ref[i, m : 2 * m, :] = second


def kernel_values(source, points, col_total):
    size = 1.0 / math.sqrt(col_total)
    turns = wavenumber * 2.0 / math.pi
    h = math.pi / 2
    square = softening * softening
    for c in range(3):
        diff = source[c : c + 1, :] - points[c]
        square = square + diff * diff
    near = lax.rsqrt(square)
    amplitude = near * size
    quarter = (square * near) * turns
    whole = jnp.round(quarter)
    rest = quarter - whole
    r2 = rest * rest
    sine = rest * (h + r2 * (-(h**3) / 6 + r2 * (h**5 / 120 + r2 * (-(h**7) / 5040))))
    cosine = 1.0 + r2 * (-(h**2) / 2 + r2 * (h**4 / 24 + r2 * (-(h**6) / 720 + r2 * (h**8 / 40320))))
    count = whole.astype(jnp.int32)
    odd = (count & 1) == 1
    first = jnp.where(odd, sine, cosine)
    second = jnp.where(odd, cosine, sine)
    first = jnp.where(((count + 1) & 2) == 0, first, -first)
    second = jnp.where((count & 2) == 0, second, -second)
    return (amplitude * first).astype(BF16), (amplitude * second).astype(BF16)


def accumulate(probe_ref, kernel_ref, high, total):
    pieces = probe_ref.shape[0]
    both = 2 if pieces % 2 == 0 else 1

    def one(i, total):
        left = jnp.concatenate([probe_ref[both * i + k, 0:high, :] for k in range(both)], axis=1)
        right = jnp.concatenate([kernel_ref[both * i + k] for k in range(both)], axis=1)
        return total + mxu(left, right, NT)

    count = pieces // both
    return lax.fori_loop(0, count, one, total, unroll=count <= 8)


def sample_body(groups, *refs):
    out_ref = refs[-1]
    high, n = out_ref.shape
    total = jnp.zeros((high, n), F32)
    for g in range(groups):
        total = accumulate(refs[g], refs[groups + g], high, total)
    out_ref[...] = total


def leaf_body(blocks, place_ref, sizes_ref, ranks_ref, probe_ref, kernel_ref, *refs):
    h_ref, m_ref, t_ref = refs[blocks:]
    n = h_ref.shape[0]
    rows, cols = grids(n)
    high = n // blocks
    for o in range(blocks):
        total = refs[o][...]
        if o == blocks - 1:
            total = accumulate(probe_ref, kernel_ref, high, total)
        at = pl.multiple_of((place_ref[0] ^ o) * high, high)
        m_ref[pl.ds(at, high), :] = total
    used = sizes_ref[0]
    half = n // 2
    inside = cols - jnp.where(cols >= half, half, 0) < used
    matrix = jnp.where(inside, m_ref[...], 0.0)
    m_ref[...] = matrix
    shift, by_row, by_col = factorize(dot3(matrix, matrix, NT), t_ref)
    in_rank = rows < ranks_ref[0]
    value = jnp.where(in_rank, projected_rows(t_ref, by_row, by_col), 0.0)
    h_ref[...] = rows_gram(value) * shift


def basis_body(ranks_ref, t_ref, m_ref, b_ref):
    n = t_ref.shape[0]
    rows, cols = grids(n)
    held = t_ref[...]
    matrix = m_ref[...]
    shift = jnp.sum(jnp.sum(matrix * matrix, axis=0, keepdims=True), axis=1, keepdims=True) / n
    diagonal = jnp.where(rows == cols, held, 0.0)
    by_row = jnp.sum(diagonal, axis=1, keepdims=True)
    by_col = jnp.sum(diagonal, axis=0, keepdims=True)
    inverse = jnp.where(rows > cols, held / by_col, jnp.where(rows == cols, 1.0, 0.0))
    scale = jnp.where(rows < ranks_ref[0], lax.rsqrt(by_row * shift), 0.0)
    b_ref[...] = dot3(inverse * scale, matrix, NN)


def node_body(own_ref, other_ref, h_ref, packed_ref, t_ref):
    shift, by_row, by_col = factorize(own_ref[...] + other_ref[...], t_ref)
    value = projected_rows(t_ref, by_row, by_col)
    h_ref[...] = rows_gram(value) * shift
    fold(h_ref, packed_ref)


def top_body(own_ref, other_ref, z_ref, t_ref):
    shift, by_row, by_col = factorize(unfold_add(other_ref, own_ref), t_ref)
    value = projected_rows(t_ref, by_row, by_col)
    z_ref[...] = (value * jnp.sqrt(shift)).T


def call(body, outs, operands, specs=None, scratch=(), flops=0):
    bytes_used = sum(x.size * x.dtype.itemsize for x in (*outs, *operands))
    return pl.pallas_call(
        body,
        out_shape=list(outs),
        in_specs=list(specs or [VMEM] * len(operands)),
        out_specs=[VMEM] * len(outs),
        scratch_shapes=list(scratch),
        cost_estimate=pl.CostEstimate(flops=flops, bytes_accessed=bytes_used, transcendentals=0),
        compiler_params=pltpu.CompilerParams(vmem_limit_bytes=2 * bytes_used + (6 << 20)),
    )(*operands)


def flip(value, rows_mask, probe_mask=0):
    probe_size = lax.axis_size("probe")
    if probe_mask == 0:
        pairs = [(i, i ^ rows_mask) for i in range(lax.axis_size("rows"))]
        return lax.ppermute(value, "rows", pairs)
    if rows_mask == 0:
        pairs = [(i, i ^ probe_mask) for i in range(probe_size)]
        return lax.ppermute(value, "probe", pairs)
    pairs = [
        (i * probe_size + j, (i ^ rows_mask) * probe_size + (j ^ probe_mask))
        for i in range(lax.axis_size("rows"))
        for j in range(probe_size)
    ]
    return lax.ppermute(value, ("rows", "probe"), pairs)


def per_device(targets, sources, probes, cluster_sizes, leaf_ranks):
    rows_size = lax.axis_size("rows")
    probe_size = lax.axis_size("probe")
    col_total = sources.shape[1] * rows_size
    high = probes.shape[0]
    n = high * probe_size
    leaf_rows = targets.shape[1] // probe_size
    place = lax.axis_index("probe")

    points = lax.dynamic_slice_in_dim(targets, place * leaf_rows, leaf_rows, 1)
    points = jnp.pad(points, ((0, 8 - points.shape[0]), (0, 0)))

    def evaluate(arrays):
        outs = [jax.ShapeDtypeStruct((x.shape[0], 2 * leaf_rows, x.shape[2]), BF16) for x in arrays]
        return call(
            lambda *refs: kernel_body(col_total, high, *refs), outs, [points, *arrays],
            flops=2000 * sum(x.size for x in outs),
        )

    pieces = jnp.concatenate([probes, jnp.pad(sources, ((0, 16 - sources.shape[0]), (0, 0)))], axis=0)[None]
    mask = rows_size // 2
    while mask > 2:
        low = mask // 2 if mask // 2 > 2 else 0
        received = [flip(pieces, m) for m in ([low, mask, mask + low] if low else [mask])]
        pieces = jnp.concatenate([pieces, *received], axis=0)
        mask //= 4 if low else 2
    masks = [0, 2] if rows_size > 2 else [0]
    probes_only = pieces[:, :high]
    square = jax.ShapeDtypeStruct((n, n), F32)
    block = jax.ShapeDtypeStruct((high, n), F32)
    values = []
    samples = []
    for o in range(probe_size):
        held = []
        for m in masks:
            near = pieces if (m, o) == (0, 0) else flip(probes_only if o else pieces, m, o)
            far = flip(near, 1)
            held += [near, far]
            if o == 0:
                for x in (near, far):
                    values += evaluate([x])
        count = len(held) - (o == probe_size - 1)
        samples += call(
            lambda *refs, count=count: sample_body(count, *refs), [block],
            [*held[:count], *values[:count]], flops=200 * high * n * n,
        )
    scratch = [pltpu.VMEM((n, n), F32)]
    h, m, t = call(
        lambda *refs: leaf_body(probe_size, *refs), [square] * 3,
        [place[None], cluster_sizes, leaf_ranks, held[-1], values[-1], *samples],
        specs=[SMEM] * 3 + [VMEM] * (2 + len(samples)), flops=n**3,
    )
    other = flip(h, 1)
    basis = call(basis_body, [square], [leaf_ranks, t, m], specs=[SMEM, VMEM, VMEM], flops=60 * n**3)[0]
    packed = jax.ShapeDtypeStruct((n + 8, n // 2), F32)
    h, sent = call(node_body, [square, packed], [h, other], scratch=scratch, flops=n**3)
    other = flip(sent, 2)
    top = call(top_body, [square], [h, other], scratch=scratch, flops=n**3)[0]
    return (basis.reshape(n, 2, leaf_rows), top[None])


def solution(mesh):
    return jax.shard_map(
        per_device,
        mesh=mesh,
        in_specs=(
            P(None, "rows"),
            P(None, "rows"),
            P("probe", "rows"),
            P(("rows", "probe")),
            P(("rows", "probe")),
        ),
        out_specs=(P(None, None, ("rows", "probe")), P(("rows", "probe"), None, None)),
        check_vma=False,
    )
```

```python
import math

import jax
import jax.numpy as jnp
from jax import lax
from jax.experimental import pallas as pl
from jax.experimental.pallas import tpu as pltpu
from jax.sharding import PartitionSpec as P


wavenumber = 30.0
softening = 0.02

F32 = jnp.float32
BF16 = jnp.bfloat16
VMEM = pl.BlockSpec(memory_space=pltpu.VMEM)
SMEM = pl.BlockSpec(memory_space=pltpu.SMEM)
NN = ((1,), (0,))
NT = ((1,), (1,))

LANES = 128
PANEL = 64
CHUNK = 256


def split_bf16(value):
    high = value.astype(BF16)
    return high, (value - high.astype(F32)).astype(BF16)


def mxu(left, right, dims):
    return lax.dot_general(left, right, (dims, ((), ())), preferred_element_type=F32)


def dot3(left, right, dims):
    lh, ll = split_bf16(left)
    rh, rl = split_bf16(right)
    return mxu(lh, rh, dims) + (mxu(lh, rl, dims) + mxu(ll, rh, dims))


def rows_gram(value):
    n = value.shape[1]
    high, low = split_bf16(value)
    turned = jnp.concatenate([high, low], axis=1).T
    first = mxu(turned, high, NN)
    return first[:n] + (first[n:] + mxu(turned[:n], low, NN))


def pick_lane(tile, lane):
    where = jnp.full(tile.shape, lane, jnp.int32)
    return jnp.take_along_axis(tile, where, axis=1, mode="promise_in_bounds")


def pick_row(tile, row):
    return jnp.broadcast_to(tile[row : row + 1, :], tile.shape)


def sweep(t_ref):
    n = t_ref.shape[0]
    tiles = n // LANES
    steps = PANEL // 8
    lane = lax.broadcasted_iota(jnp.int32, (8, LANES), 1)
    row = lax.broadcasted_iota(jnp.int32, (8, LANES), 0)
    along_lanes = [jnp.zeros((8, LANES), F32) for _ in range(tiles)]
    along_rows = []
    for start in range(0, n, PANEL):
        at, low = divmod(start, LANES)
        block = [
            [t_ref[start + 8 * i : start + 8 * i + 8, LANES * t : LANES * (t + 1)] for t in range(tiles)]
            for i in range(steps)
        ]
        pivots = [jnp.zeros((8, LANES), F32) for _ in range(steps)]
        ahead = None
        for i0 in range(steps):
            first = low + 8 * i0

            def columns(i, base):
                return [pick_lane(block[i][at], base + a) for a in range(8)]

            cols = ahead or columns(i0, first)
            below = {i: columns(i, first) for i in range(i0 + 1, steps)}
            after = columns(i0 + 1, first + 8) if i0 + 1 < steps else None
            sums = [jnp.zeros((8, LANES), F32)] * 8
            for a in range(8):
                here = lane == first + a
                pivot = pick_row(cols[a], a)
                inverse = 1.0 / pivot
                pivots[i0] = jnp.where(row == a, pivot, pivots[i0])
                factor = jnp.where(row > a, cols[a] * inverse, 0.0)
                entries = {b: pick_row(cols[b], a) for b in range(a + 1, 8)}
                for b in entries:
                    cols[b] = cols[b] - factor * entries[b]
                swept = [pick_row(block[i0][t], a) for t in range(tiles)]
                swept[at] = jnp.where(here, 2.0 * swept[at], swept[at])
                for t in range(tiles):
                    block[i0][t] = block[i0][t] - factor * swept[t]
                for i, mine in below.items():
                    factor = mine[a] * inverse
                    for b in entries:
                        mine[b] = mine[b] - factor * entries[b]
                    for t in range(tiles):
                        block[i][t] = block[i][t] - factor * swept[t]
                    if after and i == i0 + 1:
                        sums = [x + factor * pick_row(mine[a], b) for b, x in enumerate(sums)]
            along_lanes[at] = along_lanes[at] + jnp.where(lane == first + row, block[i0][at], 0.0)
            ahead = after and [x - y for x, y in zip(after, sums)]
        for i in range(steps):
            for t in range(tiles):
                t_ref[start + 8 * i : start + 8 * i + 8, LANES * t : LANES * (t + 1)] = block[i][t]
        along_rows += pivots
        end = start + PANEL
        if end < n:
            rowi = lax.broadcasted_iota(jnp.int32, (PANEL, n), 0)
            coli = lax.broadcasted_iota(jnp.int32, (PANEL, n), 1)
            whole = jnp.concatenate([jnp.concatenate(x, axis=1) for x in block], axis=0)
            kept = jnp.where((coli < end) & (coli - start > rowi), 0.0, whole)
            scale = 1.0 / jnp.concatenate(pivots, axis=0)
            base = end // LANES * LANES
            factors = whole[:, base:] * jnp.concatenate([scale] * ((n - base) // LANES), axis=1)
            fh, fl = split_bf16(factors)
            kh, kl = split_bf16(kept)
            left = jnp.concatenate([fh, fh, fl], axis=0).T
            right = jnp.concatenate([kh, kl, kh], axis=0)
            for to in range(end, n, CHUNK):
                high = min(CHUNK, n - to)
                change = mxu(left[to - base : to - base + high, :], right, NN)
                colr = lax.broadcasted_iota(jnp.int32, (high, LANES), 1)
                for t in range(tiles):
                    at_t = slice(LANES * t, LANES * (t + 1))
                    rest = t_ref[to : to + high, at_t]
                    if t == at:
                        rest = jnp.where((colr >= low) & (colr < low + PANEL), 0.0, rest)
                    t_ref[to : to + high, at_t] = rest - change[:, at_t]
    return along_lanes, along_rows


def grids(n):
    rows = lax.broadcasted_iota(jnp.int32, (n, n), 0)
    cols = lax.broadcasted_iota(jnp.int32, (n, n), 1)
    return rows, cols


def factorize(gram, t_ref):
    n = gram.shape[0]
    rows, cols = grids(n)
    diagonal = jnp.where(rows == cols, gram, 0.0)
    shift = jnp.sum(jnp.sum(diagonal, axis=0, keepdims=True), axis=1, keepdims=True) / n
    t_ref[...] = gram / shift + jnp.where(rows == cols, 1.0, 0.0)
    along_lanes, along_rows = sweep(t_ref)
    sums = [jnp.sum(x, axis=0, keepdims=True) for x in along_lanes]
    by_col = jnp.concatenate([jnp.broadcast_to(x, (n, LANES)) for x in sums], axis=1)
    by_row = jnp.concatenate([jnp.concatenate([x] * (n // LANES), axis=1) for x in along_rows], axis=0)
    return shift, by_row, by_col


def projected_rows(t_ref, by_row, by_col):
    rows, cols = grids(t_ref.shape[0])
    held = t_ref[...]
    return lax.rsqrt(by_row) * jnp.where(
        rows < cols, held, jnp.where(rows > cols, -held / by_col, by_row - 1.0)
    )


def fold(full_ref, packed_ref):
    n = full_ref.shape[0]
    half = n // 2
    rows, cols = grids(half)
    upper = full_ref[0:half, 0:half]
    lower = full_ref[half:n, half:n]
    packed_ref[0:half, :] = full_ref[0:half, half:n]
    packed_ref[half:n, :] = jnp.where(rows <= cols, upper, lower)
    packed_ref[n : n + 8, :] = jnp.broadcast_to(
        jnp.sum(jnp.where(rows == cols, lower, 0.0), axis=0, keepdims=True), (8, half)
    )


def unfold_add(packed_ref, full_ref):
    n = full_ref.shape[0]
    half = n // 2
    rows, cols = grids(half)
    corner = packed_ref[0:half, :]
    both = packed_ref[half:n, :]
    turned = both.T
    line = jnp.broadcast_to(packed_ref[n : n + 1, :], (half, half))
    upper = jnp.where(rows <= cols, both, turned)
    lower = jnp.where(rows == cols, line, jnp.where(rows > cols, both, turned))
    top = jnp.concatenate([upper, corner], axis=1)
    bottom = jnp.concatenate([corner.T, lower], axis=1)
    return full_ref[...] + jnp.concatenate([top, bottom], axis=0)


def kernel_body(col_total, high, targets_ref, *refs):
    m = targets_ref.shape[1]
    width = refs[0].shape[2]
    turned = jnp.concatenate([targets_ref[...], jnp.zeros((m - 8, m), F32)], axis=0).T
    points = [jnp.broadcast_to(turned[:, c : c + 1], (m, width)) for c in range(3)]
    count = len(refs) // 2
    for piece_ref, out_ref in zip(refs[:count], refs[count:]):
        for i in range(piece_ref.shape[0]):
            source = piece_ref[i, high : high + 3, :].astype(F32)
            first, second = kernel_values(source, points, col_total)
            out_ref[i, 0:m, :] = first
            out_ref[i, m : 2 * m, :] = second


def kernel_values(source, points, col_total):
    size = 1.0 / math.sqrt(col_total)
    turns = wavenumber * 2.0 / math.pi
    h = math.pi / 2
    square = softening * softening
    for c in range(3):
        diff = source[c : c + 1, :] - points[c]
        square = square + diff * diff
    near = lax.rsqrt(square)
    amplitude = near * size
    quarter = (square * near) * turns
    whole = jnp.round(quarter)
    rest = quarter - whole
    r2 = rest * rest
    sine = rest * (h + r2 * (-(h**3) / 6 + r2 * (h**5 / 120 + r2 * (-(h**7) / 5040))))
    cosine = 1.0 + r2 * (-(h**2) / 2 + r2 * (h**4 / 24 + r2 * (-(h**6) / 720 + r2 * (h**8 / 40320))))
    count = whole.astype(jnp.int32)
    odd = (count & 1) == 1
    first = jnp.where(odd, sine, cosine)
    second = jnp.where(odd, cosine, sine)
    first = jnp.where(((count + 1) & 2) == 0, first, -first)
    second = jnp.where((count & 2) == 0, second, -second)
    return (amplitude * first).astype(BF16), (amplitude * second).astype(BF16)


def accumulate(probe_ref, kernel_ref, high, total):
    pieces = probe_ref.shape[0]
    both = 2 if pieces % 2 == 0 else 1

    def one(i, total):
        left = jnp.concatenate([probe_ref[both * i + k, 0:high, :] for k in range(both)], axis=1)
        right = jnp.concatenate([kernel_ref[both * i + k] for k in range(both)], axis=1)
        return total + mxu(left, right, NT)

    count = pieces // both
    return lax.fori_loop(0, count, one, total, unroll=count <= 8)


def sample_body(groups, *refs):
    out_ref = refs[-1]
    high, n = out_ref.shape
    total = jnp.zeros((high, n), F32)
    for g in range(groups):
        total = accumulate(refs[g], refs[groups + g], high, total)
    out_ref[...] = total


def leaf_body(blocks, place_ref, points_ref, probe_ref, kernel_ref, *refs):
    h_ref, m_ref, t_ref = refs[blocks:]
    n = h_ref.shape[0]
    rows, cols = grids(n)
    high = n // blocks
    for o in range(blocks):
        total = refs[o][...]
        if o == blocks - 1:
            total = accumulate(probe_ref, kernel_ref, high, total)
        at = pl.multiple_of((place_ref[0] ^ o) * high, high)
        m_ref[pl.ds(at, high), :] = total
    half = n // 2
    inside = (cols - jnp.where(cols >= half, half, 0)).astype(F32) < points_ref[3:4, 0:1]
    matrix = jnp.where(inside, m_ref[...], 0.0)
    m_ref[...] = matrix
    shift, by_row, by_col = factorize(dot3(matrix, matrix, NT), t_ref)
    in_rank = rows.astype(F32) < points_ref[4:5, 0:1]
    value = jnp.where(in_rank, projected_rows(t_ref, by_row, by_col), 0.0)
    h_ref[...] = rows_gram(value) * shift


def basis_body(points_ref, t_ref, m_ref, b_ref):
    n = t_ref.shape[0]
    rows, cols = grids(n)
    held = t_ref[...]
    matrix = m_ref[...]
    shift = jnp.sum(jnp.sum(matrix * matrix, axis=0, keepdims=True), axis=1, keepdims=True) / n
    diagonal = jnp.where(rows == cols, held, 0.0)
    by_row = jnp.sum(diagonal, axis=1, keepdims=True)
    by_col = jnp.sum(diagonal, axis=0, keepdims=True)
    inverse = jnp.where(rows > cols, held / by_col, jnp.where(rows == cols, 1.0, 0.0))
    scale = jnp.where(rows.astype(F32) < points_ref[4:5, 0:1], lax.rsqrt(by_row * shift), 0.0)
    b_ref[...] = dot3(inverse * scale, matrix, NN)


def node_body(own_ref, other_ref, h_ref, packed_ref, t_ref):
    shift, by_row, by_col = factorize(own_ref[...] + other_ref[...], t_ref)
    value = projected_rows(t_ref, by_row, by_col)
    h_ref[...] = rows_gram(value) * shift
    fold(h_ref, packed_ref)


def top_body(own_ref, other_ref, z_ref, t_ref):
    shift, by_row, by_col = factorize(unfold_add(other_ref, own_ref), t_ref)
    value = projected_rows(t_ref, by_row, by_col)
    z_ref[...] = (value * jnp.sqrt(shift)).T


def call(body, outs, operands, specs=None, scratch=(), flops=0):
    bytes_used = sum(x.size * x.dtype.itemsize for x in (*outs, *operands))
    return pl.pallas_call(
        body,
        out_shape=list(outs),
        in_specs=list(specs or [VMEM] * len(operands)),
        out_specs=[VMEM] * len(outs),
        scratch_shapes=list(scratch),
        cost_estimate=pl.CostEstimate(flops=flops, bytes_accessed=bytes_used, transcendentals=0),
        compiler_params=pltpu.CompilerParams(vmem_limit_bytes=2 * bytes_used + (6 << 20)),
    )(*operands)


def flip(value, rows_mask, probe_mask=0):
    probe_size = lax.axis_size("probe")
    if probe_mask == 0:
        pairs = [(i, i ^ rows_mask) for i in range(lax.axis_size("rows"))]
        return lax.ppermute(value, "rows", pairs)
    if rows_mask == 0:
        pairs = [(i, i ^ probe_mask) for i in range(probe_size)]
        return lax.ppermute(value, "probe", pairs)
    pairs = [
        (i * probe_size + j, (i ^ rows_mask) * probe_size + (j ^ probe_mask))
        for i in range(lax.axis_size("rows"))
        for j in range(probe_size)
    ]
    return lax.ppermute(value, ("rows", "probe"), pairs)


def per_device(targets, sources, probes, cluster_sizes, leaf_ranks):
    rows_size = lax.axis_size("rows")
    probe_size = lax.axis_size("probe")
    col_total = sources.shape[1] * rows_size
    high = probes.shape[0]
    n = high * probe_size
    leaf_rows = targets.shape[1] // probe_size
    place = lax.axis_index("probe")

    points = lax.dynamic_slice_in_dim(targets, place * leaf_rows, leaf_rows, 1)
    limits = [jnp.full((1, leaf_rows), x[0]).astype(F32) for x in (cluster_sizes, leaf_ranks)]
    points = jnp.concatenate([points, *limits, jnp.zeros((3, leaf_rows), F32)], axis=0)

    def evaluate(arrays):
        outs = [jax.ShapeDtypeStruct((x.shape[0], 2 * leaf_rows, x.shape[2]), BF16) for x in arrays]
        return call(
            lambda *refs: kernel_body(col_total, high, *refs), outs, [points, *arrays],
            flops=2000 * sum(x.size for x in outs),
        )

    pieces = jnp.concatenate([probes, jnp.pad(sources, ((0, 16 - sources.shape[0]), (0, 0)))], axis=0)[None]
    mask = rows_size // 2
    while mask > 2:
        low = mask // 2 if mask // 2 > 2 else 0
        received = []
        for m in [low, mask, mask + low] if low else [mask]:
            received.append(flip(pieces, m))
        pieces = jnp.concatenate([pieces, *received], axis=0)
        mask //= 4 if low else 2
    masks = [0, 2] if rows_size > 2 else [0]
    probes_only = pieces[:, :high]
    square = jax.ShapeDtypeStruct((n, n), F32)
    block = jax.ShapeDtypeStruct((high, n), F32)
    values = []
    samples = []
    for o in range(probe_size):
        held = []
        for m in masks:
            near = pieces if (m, o) == (0, 0) else flip(probes_only if o else pieces, m, o)
            far = flip(near, 1)
            held += [near, far]
            if o == 0:
                for x in (near, far):
                    values += evaluate([x])
        count = len(held) - (o == probe_size - 1)
        samples += call(
            lambda *refs, count=count: sample_body(count, *refs), [block],
            [*held[:count], *values[:count]], flops=200 * high * n * n,
        )
    scratch = [pltpu.VMEM((n, n), F32)]
    h, m, t = call(
        lambda *refs: leaf_body(probe_size, *refs), [square] * 3,
        [place[None], points, held[-1], values[-1], *samples],
        specs=[SMEM] + [VMEM] * (3 + len(samples)), flops=n**3,
    )
    other = flip(h, 1)
    basis = call(basis_body, [square], [points, t, m], flops=60 * n**3)[0]
    packed = jax.ShapeDtypeStruct((n + 8, n // 2), F32)
    h, sent = call(node_body, [square, packed], [h, other], scratch=scratch, flops=n**3)
    other = flip(sent, 2)
    top = call(top_body, [square], [h, other], scratch=scratch, flops=n**3)[0]
    return (basis.reshape(n, 2, leaf_rows), top[None])


def solution(mesh):
    return jax.shard_map(
        per_device,
        mesh=mesh,
        in_specs=(
            P(None, "rows"),
            P(None, "rows"),
            P("probe", "rows"),
            P(("rows", "probe")),
            P(("rows", "probe")),
        ),
        out_specs=(P(None, None, ("rows", "probe")), P(("rows", "probe"), None, None)),
        check_vma=False,
    )
```

```python
import math

import jax
import jax.numpy as jnp
from jax import lax
from jax.experimental import pallas as pl
from jax.experimental.pallas import tpu as pltpu
from jax.sharding import PartitionSpec as P


wavenumber = 30.0
softening = 0.02

F32 = jnp.float32
BF16 = jnp.bfloat16
VMEM = pl.BlockSpec(memory_space=pltpu.VMEM)
SMEM = pl.BlockSpec(memory_space=pltpu.SMEM)
NN = ((1,), (0,))
NT = ((1,), (1,))

SINE = (3.1415927410125732, -5.167710304260254, 2.550077438354492, -0.598291277885437, 0.07765766233205795)
COSINE = (0.9999999403953552, -4.934792995452881, 4.058411121368408, -1.331876516342163, 0.21968960762023926)

LANES = 128
PANEL = 64
CHUNK = 256
COARSE = 0.2


def split_bf16(value):
    high = value.astype(BF16)
    return high, (value - high.astype(F32)).astype(BF16)


def mxu(left, right, dims):
    return lax.dot_general(left, right, (dims, ((), ())), preferred_element_type=F32)


def dot3(left, right, dims):
    lh, ll = split_bf16(left)
    rh, rl = split_bf16(right)
    return mxu(lh, rh, dims) + (mxu(lh, rl, dims) + mxu(ll, rh, dims))


def rows_gram(value):
    n = value.shape[1]
    high, low = split_bf16(value)
    turned = jnp.concatenate([high, low], axis=1).T
    first = mxu(turned, high, NN)
    return first[:n] + (first[n:] + mxu(turned[:n], low, NN))


def pick_lane(tile, lane):
    where = jnp.full(tile.shape, lane, jnp.int32)
    return jnp.take_along_axis(tile, where, axis=1, mode="promise_in_bounds")


def pick_row(tile, row):
    return jnp.broadcast_to(tile[row : row + 1, :], tile.shape)


def sweep(t_ref):
    n = t_ref.shape[0]
    tiles = n // LANES
    steps = PANEL // 8
    lane = lax.broadcasted_iota(jnp.int32, (8, LANES), 1)
    row = lax.broadcasted_iota(jnp.int32, (8, LANES), 0)
    along_lanes = [jnp.zeros((8, LANES), F32) for _ in range(tiles)]
    along_rows = []
    for start in range(0, n, PANEL):
        at, low = divmod(start, LANES)
        block = [
            [t_ref[start + 8 * i : start + 8 * i + 8, LANES * t : LANES * (t + 1)] for t in range(tiles)]
            for i in range(steps)
        ]
        pivots = [jnp.zeros((8, LANES), F32) for _ in range(steps)]
        ahead = None
        for i0 in range(steps):
            first = low + 8 * i0

            def columns(i, base):
                return [pick_lane(block[i][at], base + a) for a in range(8)]

            cols = ahead or columns(i0, first)
            below = {i: columns(i, first) for i in range(i0 + 1, steps)}
            after = columns(i0 + 1, first + 8) if i0 + 1 < steps else None
            sums = [jnp.zeros((8, LANES), F32)] * 8
            for a in range(8):
                here = lane == first + a
                pivot = pick_row(cols[a], a)
                inverse = 1.0 / pivot
                pivots[i0] = jnp.where(row == a, pivot, pivots[i0])
                factor = jnp.where(row > a, cols[a] * inverse, 0.0)
                entries = {b: pick_row(cols[b], a) for b in range(a + 1, 8)}
                for b in entries:
                    cols[b] = cols[b] - factor * entries[b]
                swept = [pick_row(block[i0][t], a) for t in range(tiles)]
                swept[at] = jnp.where(here, 2.0 * swept[at], swept[at])
                for t in range(tiles):
                    block[i0][t] = block[i0][t] - factor * swept[t]
                for i, mine in below.items():
                    factor = mine[a] * inverse
                    for b in entries:
                        mine[b] = mine[b] - factor * entries[b]
                    for t in range(tiles):
                        block[i][t] = block[i][t] - factor * swept[t]
                    if after and i == i0 + 1:
                        sums = [x + factor * pick_row(mine[a], b) for b, x in enumerate(sums)]
            along_lanes[at] = along_lanes[at] + jnp.where(lane == first + row, block[i0][at], 0.0)
            ahead = after and [x - y for x, y in zip(after, sums)]
        for i in range(steps):
            for t in range(tiles):
                t_ref[start + 8 * i : start + 8 * i + 8, LANES * t : LANES * (t + 1)] = block[i][t]
        along_rows += pivots
        end = start + PANEL
        if end < n:
            rowi = lax.broadcasted_iota(jnp.int32, (PANEL, n), 0)
            coli = lax.broadcasted_iota(jnp.int32, (PANEL, n), 1)
            whole = jnp.concatenate([jnp.concatenate(x, axis=1) for x in block], axis=0)
            kept = jnp.where((coli < end) & (coli - start > rowi), 0.0, whole)
            scale = 1.0 / jnp.concatenate(pivots, axis=0)
            base = end // LANES * LANES
            factors = whole[:, base:] * jnp.concatenate([scale] * ((n - base) // LANES), axis=1)
            fh, fl = split_bf16(factors)
            kh, kl = split_bf16(kept)
            left = jnp.concatenate([fh, fh, fl], axis=0).T
            right = jnp.concatenate([kh, kl, kh], axis=0)
            for to in range(end, n, CHUNK):
                high = min(CHUNK, n - to)
                change = mxu(left[to - base : to - base + high, :], right, NN)
                colr = lax.broadcasted_iota(jnp.int32, (high, LANES), 1)
                for t in range(tiles):
                    at_t = slice(LANES * t, LANES * (t + 1))
                    rest = t_ref[to : to + high, at_t]
                    if t == at:
                        rest = jnp.where((colr >= low) & (colr < low + PANEL), 0.0, rest)
                    t_ref[to : to + high, at_t] = rest - change[:, at_t]
    return along_lanes, along_rows


def grids(n):
    rows = lax.broadcasted_iota(jnp.int32, (n, n), 0)
    cols = lax.broadcasted_iota(jnp.int32, (n, n), 1)
    return rows, cols


def trace(matrix):
    rows, cols = grids(matrix.shape[0])
    diagonal = jnp.where(rows == cols, matrix, 0.0)
    return jnp.sum(jnp.sum(diagonal, axis=0, keepdims=True), axis=1, keepdims=True)


def factorize(gram, t_ref):
    n = gram.shape[0]
    rows, cols = grids(n)
    shift = trace(gram) / n
    t_ref[...] = gram / shift + jnp.where(rows == cols, 1.0, 0.0)
    along_lanes, along_rows = sweep(t_ref)
    sums = [jnp.sum(x, axis=0, keepdims=True) for x in along_lanes]
    by_col = jnp.concatenate([jnp.broadcast_to(x, (n, LANES)) for x in sums], axis=1)
    by_row = jnp.concatenate([jnp.concatenate([x] * (n // LANES), axis=1) for x in along_rows], axis=0)
    return shift, by_row, by_col


def projected_rows(t_ref, by_row, by_col):
    rows, cols = grids(t_ref.shape[0])
    held = t_ref[...]
    return lax.rsqrt(by_row) * jnp.where(
        rows < cols, held, jnp.where(rows > cols, -held / by_col, by_row - 1.0)
    )


def fold(full_ref, packed_ref):
    n = full_ref.shape[0]
    half = n // 2
    rows, cols = grids(half)
    upper = full_ref[0:half, 0:half]
    lower = full_ref[half:n, half:n]
    packed_ref[0:half, :] = full_ref[0:half, half:n]
    packed_ref[half:n, :] = jnp.where(rows <= cols, upper, lower)
    packed_ref[n : n + 8, :] = jnp.broadcast_to(
        jnp.sum(jnp.where(rows == cols, lower, 0.0), axis=0, keepdims=True), (8, half)
    )


def unfold_add(packed_ref, full_ref):
    n = full_ref.shape[0]
    half = n // 2
    rows, cols = grids(half)
    corner = packed_ref[0:half, :]
    both = packed_ref[half:n, :]
    turned = both.T
    line = jnp.broadcast_to(packed_ref[n : n + 1, :], (half, half))
    upper = jnp.where(rows <= cols, both, turned)
    lower = jnp.where(rows == cols, line, jnp.where(rows > cols, both, turned))
    top = jnp.concatenate([upper, corner], axis=1)
    bottom = jnp.concatenate([corner.T, lower], axis=1)
    return full_ref[...] + jnp.concatenate([top, bottom], axis=0)


def kernel_body(col_total, high, targets_ref, *refs):
    m = targets_ref.shape[1]
    width = refs[0].shape[2]
    turned = jnp.concatenate([targets_ref[...], jnp.zeros((m - 8, m), F32)], axis=0).T
    points = [jnp.broadcast_to(turned[:, c : c + 1], (m, width)) for c in range(3)]
    count = len(refs) // 2
    for piece_ref, out_ref in zip(refs[:count], refs[count:]):
        for i in range(piece_ref.shape[0]):
            source = piece_ref[i, high : high + 3, :].astype(F32)
            first, second = kernel_values(source, points, col_total)
            out_ref[i, 0:m, :] = first
            out_ref[i, m : 2 * m, :] = second


def kernel_values(source, points, col_total):
    size = 1.0 / math.sqrt(col_total)
    square = softening * softening
    for c in range(3):
        diff = source[c : c + 1, :] - points[c]
        square = square + diff * diff
    near = lax.rsqrt(square)
    amplitude = near * size
    turns = (square * near) * (wavenumber / math.pi)
    whole = jnp.round(turns)
    rest = turns - whole
    r2 = rest * rest
    sine = rest * power_series(SINE, r2)
    cosine = power_series(COSINE, r2)
    odd = (whole.astype(jnp.int32) & 1) == 1
    amplitude = jnp.where(odd, -amplitude, amplitude)
    return (amplitude * cosine).astype(BF16), (amplitude * sine).astype(BF16)


def power_series(terms, x):
    value = terms[-1]
    for term in terms[-2::-1]:
        value = value * x + term
    return value


def accumulate(probe_ref, kernel_ref, high, total):
    pieces = probe_ref.shape[0]
    both = 2 if pieces % 2 == 0 else 1

    def one(i, total):
        left = jnp.concatenate([probe_ref[both * i + k, 0:high, :] for k in range(both)], axis=1)
        right = jnp.concatenate([kernel_ref[both * i + k] for k in range(both)], axis=1)
        return total + mxu(left, right, NT)

    count = pieces // both
    return lax.fori_loop(0, count, one, total, unroll=count <= 8)


def sample_body(groups, *refs):
    out_ref = refs[-1]
    high, n = out_ref.shape
    total = jnp.zeros((high, n), F32)
    for g in range(groups):
        total = accumulate(refs[g], refs[groups + g], high, total)
    out_ref[...] = total


def leaf_body(blocks, place_ref, points_ref, probe_ref, kernel_ref, *refs):
    h_ref, m_ref, t_ref = refs[blocks:]
    n = h_ref.shape[0]
    rows, cols = grids(n)
    high = n // blocks
    for o in range(blocks):
        total = refs[o][...]
        if o == blocks - 1:
            total = accumulate(probe_ref, kernel_ref, high, total)
        at = pl.multiple_of((place_ref[0] ^ o) * high, high)
        m_ref[pl.ds(at, high), :] = total
    half = n // 2
    inside = (cols - jnp.where(cols >= half, half, 0)).astype(F32) < points_ref[3:4, 0:1]
    matrix = jnp.where(inside, m_ref[...], 0.0)
    m_ref[...] = matrix
    shift, by_row, by_col = factorize(dot3(matrix, matrix, NT), t_ref)
    in_rank = rows.astype(F32) < points_ref[4:5, 0:1]
    value = jnp.where(in_rank, projected_rows(t_ref, by_row, by_col), 0.0)
    h_ref[...] = rows_gram(value) * shift


def basis_body(points_ref, t_ref, m_ref, b_ref):
    n = t_ref.shape[0]
    rows, cols = grids(n)
    held = t_ref[...]
    matrix = m_ref[...]
    shift = jnp.sum(jnp.sum(matrix * matrix, axis=0, keepdims=True), axis=1, keepdims=True) / n
    diagonal = jnp.where(rows == cols, held, 0.0)
    by_row = jnp.sum(diagonal, axis=1, keepdims=True)
    by_col = jnp.sum(diagonal, axis=0, keepdims=True)
    inverse = jnp.where(rows > cols, held / by_col, jnp.where(rows == cols, 1.0, 0.0))
    scale = jnp.where(rows.astype(F32) < points_ref[4:5, 0:1], lax.rsqrt(by_row * shift), 0.0)
    b_ref[...] = dot3(inverse * scale, matrix, NN)


def inverse(matrix):
    n = matrix.shape[0]
    rows, cols = grids(n)
    high, low = split_bf16(matrix)
    least, most = 1.0, 1.001 * (n + 1.0)
    scale = 2.0 / (least + most)
    guess = jnp.where(rows == cols, 2.0 * scale, 0.0) - scale * scale * matrix
    spread = (most - least) / (most + least)
    while spread > 1e-3:
        least = 1.0 - spread * spread
        scale = 2.0 / (1.0 + least)
        spread = (1.0 - least) / (1.0 + least)
        if spread > COARSE:
            rough = guess.astype(BF16)
            product = mxu(high, rough, NN).astype(BF16)
            change = mxu(rough, product, NN)
        else:
            gh, gl = split_bf16(guess)
            product = mxu(high, gh, NN) + (mxu(high, gl, NN) + mxu(low, gh, NN))
            ph, pl_ = split_bf16(product)
            change = mxu(gh, ph, NN) + (mxu(gh, pl_, NN) + mxu(gl, ph, NN))
        guess = (2.0 * scale) * guess - (scale * scale) * change
    return guess


def node_body(own_ref, other_ref, h_ref, packed_ref):
    gram = own_ref[...] + other_ref[...]
    n = gram.shape[0]
    rows, cols = grids(n)
    shift = trace(gram) / n
    scaled = gram / shift
    start = scaled + jnp.where(rows == cols, 1.0, 0.0)
    h_ref[...] = (scaled - jnp.where(rows == cols, 1.0, 0.0) + inverse(start)) * shift
    fold(h_ref, packed_ref)


def top_body(own_ref, other_ref, z_ref, t_ref):
    shift, by_row, by_col = factorize(unfold_add(other_ref, own_ref), t_ref)
    value = projected_rows(t_ref, by_row, by_col)
    z_ref[...] = (value * jnp.sqrt(shift)).T


def call(body, outs, operands, specs=None, scratch=(), flops=0):
    bytes_used = sum(x.size * x.dtype.itemsize for x in (*outs, *operands))
    return pl.pallas_call(
        body,
        out_shape=list(outs),
        in_specs=list(specs or [VMEM] * len(operands)),
        out_specs=[VMEM] * len(outs),
        scratch_shapes=list(scratch),
        cost_estimate=pl.CostEstimate(flops=flops, bytes_accessed=bytes_used, transcendentals=0),
        compiler_params=pltpu.CompilerParams(vmem_limit_bytes=2 * bytes_used + (6 << 20)),
    )(*operands)


def flip(value, rows_mask, probe_mask=0):
    probe_size = lax.axis_size("probe")
    if probe_mask == 0:
        pairs = [(i, i ^ rows_mask) for i in range(lax.axis_size("rows"))]
        return lax.ppermute(value, "rows", pairs)
    if rows_mask == 0:
        pairs = [(i, i ^ probe_mask) for i in range(probe_size)]
        return lax.ppermute(value, "probe", pairs)
    pairs = [
        (i * probe_size + j, (i ^ rows_mask) * probe_size + (j ^ probe_mask))
        for i in range(lax.axis_size("rows"))
        for j in range(probe_size)
    ]
    return lax.ppermute(value, ("rows", "probe"), pairs)


def per_device(targets, sources, probes, cluster_sizes, leaf_ranks):
    rows_size = lax.axis_size("rows")
    probe_size = lax.axis_size("probe")
    col_total = sources.shape[1] * rows_size
    high = probes.shape[0]
    n = high * probe_size
    leaf_rows = targets.shape[1] // probe_size
    place = lax.axis_index("probe")

    points = lax.dynamic_slice_in_dim(targets, place * leaf_rows, leaf_rows, 1)
    limits = [jnp.full((1, leaf_rows), x[0]).astype(F32) for x in (cluster_sizes, leaf_ranks)]
    points = jnp.concatenate([points, *limits, jnp.zeros((3, leaf_rows), F32)], axis=0)

    def evaluate(arrays):
        outs = [jax.ShapeDtypeStruct((x.shape[0], 2 * leaf_rows, x.shape[2]), BF16) for x in arrays]
        return call(
            lambda *refs: kernel_body(col_total, high, *refs), outs, [points, *arrays],
            flops=2000 * sum(x.size for x in outs),
        )

    pieces = jnp.concatenate([probes, jnp.pad(sources, ((0, 16 - sources.shape[0]), (0, 0)))], axis=0)[None]
    mask = rows_size // 2
    while mask > 2:
        low = mask // 2 if mask // 2 > 2 else 0
        received = []
        for m in [low, mask, mask + low] if low else [mask]:
            received.append(flip(pieces, m))
        pieces = jnp.concatenate([pieces, *received], axis=0)
        mask //= 4 if low else 2
    masks = [0, 2] if rows_size > 2 else [0]
    probes_only = pieces[:, :high]
    square = jax.ShapeDtypeStruct((n, n), F32)
    block = jax.ShapeDtypeStruct((high, n), F32)
    values = []
    samples = []
    for o in range(probe_size):
        held = []
        for m in masks:
            near = pieces if (m, o) == (0, 0) else flip(probes_only if o else pieces, m, o)
            far = flip(near, 1)
            held += [near, far]
            if o == 0:
                for x in (near, far):
                    values += evaluate([x])
        count = len(held) - (o == probe_size - 1)
        samples += call(
            lambda *refs, count=count: sample_body(count, *refs), [block],
            [*held[:count], *values[:count]], flops=200 * high * n * n,
        )
    scratch = [pltpu.VMEM((n, n), F32)]
    h, m, t = call(
        lambda *refs: leaf_body(probe_size, *refs), [square] * 3,
        [place[None], points, held[-1], values[-1], *samples],
        specs=[SMEM] + [VMEM] * (3 + len(samples)), flops=n**3,
    )
    other = flip(h, 1)
    basis = call(basis_body, [square], [points, t, m], flops=60 * n**3)[0]
    packed = jax.ShapeDtypeStruct((n + 8, n // 2), F32)
    h, sent = call(node_body, [square, packed], [h, other], flops=n**3)
    other = flip(sent, 2)
    top = call(top_body, [square], [h, other], scratch=scratch, flops=n**3)[0]
    return (basis.reshape(n, 2, leaf_rows), top[None])


def solution(mesh):
    return jax.shard_map(
        per_device,
        mesh=mesh,
        in_specs=(
            P(None, "rows"),
            P(None, "rows"),
            P("probe", "rows"),
            P(("rows", "probe")),
            P(("rows", "probe")),
        ),
        out_specs=(P(None, None, ("rows", "probe")), P(("rows", "probe"), None, None)),
        check_vma=False,
    )
```

```python
import math

import jax
import jax.numpy as jnp
from jax import lax
from jax.experimental import pallas as pl
from jax.experimental.pallas import tpu as pltpu
from jax.sharding import PartitionSpec as P


wavenumber = 30.0
softening = 0.02

F32 = jnp.float32
BF16 = jnp.bfloat16
VMEM = pl.BlockSpec(memory_space=pltpu.VMEM)
SMEM = pl.BlockSpec(memory_space=pltpu.SMEM)
NN = ((1,), (0,))
NT = ((1,), (1,))

SINE = (3.1415927410125732, -5.167710304260254, 2.550077438354492, -0.598291277885437, 0.07765766233205795)
COSINE = (0.9999999403953552, -4.934792995452881, 4.058411121368408, -1.331876516342163, 0.21968960762023926)

LANES = 128
PANEL = 64
CHUNK = 256
COARSE = 0.2


def split_bf16(value):
    high = value.astype(BF16)
    return high, (value - high.astype(F32)).astype(BF16)


def mxu(left, right, dims):
    return lax.dot_general(left, right, (dims, ((), ())), preferred_element_type=F32)


def dot3(left, right, dims):
    lh, ll = split_bf16(left)
    rh, rl = split_bf16(right)
    return mxu(lh, rh, dims) + (mxu(lh, rl, dims) + mxu(ll, rh, dims))


def rows_gram(value):
    n = value.shape[1]
    high, low = split_bf16(value)
    turned = jnp.concatenate([high, low], axis=1).T
    first = mxu(turned, high, NN)
    return first[:n] + (first[n:] + mxu(turned[:n], low, NN))


def pick_lane(tile, lane):
    where = jnp.full(tile.shape, lane, jnp.int32)
    return jnp.take_along_axis(tile, where, axis=1, mode="promise_in_bounds")


def pick_row(tile, row):
    return jnp.broadcast_to(tile[row : row + 1, :], tile.shape)


def sweep(t_ref):
    n = t_ref.shape[0]
    tiles = n // LANES
    steps = PANEL // 8
    lane = lax.broadcasted_iota(jnp.int32, (8, LANES), 1)
    row = lax.broadcasted_iota(jnp.int32, (8, LANES), 0)
    along_lanes = [jnp.zeros((8, LANES), F32) for _ in range(tiles)]
    along_rows = []
    for start in range(0, n, PANEL):
        at, low = divmod(start, LANES)
        block = [
            [t_ref[start + 8 * i : start + 8 * i + 8, LANES * t : LANES * (t + 1)] for t in range(tiles)]
            for i in range(steps)
        ]
        pivots = [jnp.zeros((8, LANES), F32) for _ in range(steps)]
        ahead = None
        for i0 in range(steps):
            first = low + 8 * i0

            def columns(i, base):
                return [pick_lane(block[i][at], base + a) for a in range(8)]

            cols = ahead or columns(i0, first)
            below = {i: columns(i, first) for i in range(i0 + 1, steps)}
            after = columns(i0 + 1, first + 8) if i0 + 1 < steps else None
            sums = [jnp.zeros((8, LANES), F32)] * 8
            for a in range(8):
                here = lane == first + a
                pivot = pick_row(cols[a], a)
                inverse = 1.0 / pivot
                pivots[i0] = jnp.where(row == a, pivot, pivots[i0])
                factor = jnp.where(row > a, cols[a] * inverse, 0.0)
                entries = {b: pick_row(cols[b], a) for b in range(a + 1, 8)}
                for b in entries:
                    cols[b] = cols[b] - factor * entries[b]
                swept = [pick_row(block[i0][t], a) for t in range(tiles)]
                swept[at] = jnp.where(here, 2.0 * swept[at], swept[at])
                for t in range(tiles):
                    block[i0][t] = block[i0][t] - factor * swept[t]
                for i, mine in below.items():
                    factor = mine[a] * inverse
                    for b in entries:
                        mine[b] = mine[b] - factor * entries[b]
                    for t in range(tiles):
                        block[i][t] = block[i][t] - factor * swept[t]
                    if after and i == i0 + 1:
                        sums = [x + factor * pick_row(mine[a], b) for b, x in enumerate(sums)]
            along_lanes[at] = along_lanes[at] + jnp.where(lane == first + row, block[i0][at], 0.0)
            ahead = after and [x - y for x, y in zip(after, sums)]
        for i in range(steps):
            for t in range(tiles):
                t_ref[start + 8 * i : start + 8 * i + 8, LANES * t : LANES * (t + 1)] = block[i][t]
        along_rows += pivots
        end = start + PANEL
        if end < n:
            rowi = lax.broadcasted_iota(jnp.int32, (PANEL, n), 0)
            coli = lax.broadcasted_iota(jnp.int32, (PANEL, n), 1)
            whole = jnp.concatenate([jnp.concatenate(x, axis=1) for x in block], axis=0)
            kept = jnp.where((coli < end) & (coli - start > rowi), 0.0, whole)
            scale = 1.0 / jnp.concatenate(pivots, axis=0)
            base = end // LANES * LANES
            factors = whole[:, base:] * jnp.concatenate([scale] * ((n - base) // LANES), axis=1)
            fh, fl = split_bf16(factors)
            kh, kl = split_bf16(kept)
            left = jnp.concatenate([fh, fh, fl], axis=0).T
            right = jnp.concatenate([kh, kl, kh], axis=0)
            for to in range(end, n, CHUNK):
                high = min(CHUNK, n - to)
                change = mxu(left[to - base : to - base + high, :], right, NN)
                colr = lax.broadcasted_iota(jnp.int32, (high, LANES), 1)
                for t in range(tiles):
                    at_t = slice(LANES * t, LANES * (t + 1))
                    rest = t_ref[to : to + high, at_t]
                    if t == at:
                        rest = jnp.where((colr >= low) & (colr < low + PANEL), 0.0, rest)
                    t_ref[to : to + high, at_t] = rest - change[:, at_t]
    return along_lanes, along_rows


def grids(n):
    rows = lax.broadcasted_iota(jnp.int32, (n, n), 0)
    cols = lax.broadcasted_iota(jnp.int32, (n, n), 1)
    return rows, cols


def trace(matrix):
    rows, cols = grids(matrix.shape[0])
    diagonal = jnp.where(rows == cols, matrix, 0.0)
    return jnp.sum(jnp.sum(diagonal, axis=0, keepdims=True), axis=1, keepdims=True)


def factorize(gram, t_ref):
    n = gram.shape[0]
    rows, cols = grids(n)
    shift = trace(gram) / n
    t_ref[...] = gram / shift + jnp.where(rows == cols, 1.0, 0.0)
    along_lanes, along_rows = sweep(t_ref)
    sums = [jnp.sum(x, axis=0, keepdims=True) for x in along_lanes]
    by_col = jnp.concatenate([jnp.broadcast_to(x, (n, LANES)) for x in sums], axis=1)
    by_row = jnp.concatenate([jnp.concatenate([x] * (n // LANES), axis=1) for x in along_rows], axis=0)
    return shift, by_row, by_col


def projected_rows(t_ref, by_row, by_col):
    rows, cols = grids(t_ref.shape[0])
    held = t_ref[...]
    return lax.rsqrt(by_row) * jnp.where(
        rows < cols, held, jnp.where(rows > cols, -held / by_col, by_row - 1.0)
    )


def fold(full_ref, packed_ref):
    n = full_ref.shape[0]
    half = n // 2
    rows, cols = grids(half)
    upper = full_ref[0:half, 0:half]
    lower = full_ref[half:n, half:n]
    packed_ref[0:half, :] = full_ref[0:half, half:n]
    packed_ref[half:n, :] = jnp.where(rows <= cols, upper, lower)
    packed_ref[n : n + 8, :] = jnp.broadcast_to(
        jnp.sum(jnp.where(rows == cols, lower, 0.0), axis=0, keepdims=True), (8, half)
    )


def unfold_add(packed_ref, full_ref):
    n = full_ref.shape[0]
    half = n // 2
    rows, cols = grids(half)
    corner = packed_ref[0:half, :]
    both = packed_ref[half:n, :]
    turned = both.T
    line = jnp.broadcast_to(packed_ref[n : n + 1, :], (half, half))
    upper = jnp.where(rows <= cols, both, turned)
    lower = jnp.where(rows == cols, line, jnp.where(rows > cols, both, turned))
    top = jnp.concatenate([upper, corner], axis=1)
    bottom = jnp.concatenate([corner.T, lower], axis=1)
    return full_ref[...] + jnp.concatenate([top, bottom], axis=0)


def kernel_body(col_total, high, targets_ref, *refs):
    m = targets_ref.shape[1]
    width = refs[0].shape[2]
    turned = jnp.concatenate([targets_ref[...], jnp.zeros((m - 8, m), F32)], axis=0).T
    points = [jnp.broadcast_to(turned[:, c : c + 1], (m, width)) for c in range(3)]
    count = len(refs) // 2
    for piece_ref, out_ref in zip(refs[:count], refs[count:]):
        for i in range(piece_ref.shape[0]):
            source = piece_ref[i, high : high + 3, :].astype(F32)
            first, second = kernel_values(source, points, col_total)
            out_ref[i, 0:m, :] = first
            out_ref[i, m : 2 * m, :] = second


def kernel_values(source, points, col_total):
    size = 1.0 / math.sqrt(col_total)
    square = softening * softening
    for c in range(3):
        diff = source[c : c + 1, :] - points[c]
        square = square + diff * diff
    near = lax.rsqrt(square)
    amplitude = near * size
    turns = (square * near) * (wavenumber / math.pi)
    whole = jnp.round(turns)
    rest = turns - whole
    r2 = rest * rest
    sine = rest * power_series(SINE, r2)
    cosine = power_series(COSINE, r2)
    odd = (whole.astype(jnp.int32) & 1) == 1
    amplitude = jnp.where(odd, -amplitude, amplitude)
    return (amplitude * cosine).astype(BF16), (amplitude * sine).astype(BF16)


def power_series(terms, x):
    value = terms[-1]
    for term in terms[-2::-1]:
        value = value * x + term
    return value


def accumulate(probe_ref, kernel_ref, high, total):
    pieces = probe_ref.shape[0]
    both = 2 if pieces % 2 == 0 else 1

    def one(i, total):
        left = jnp.concatenate([probe_ref[both * i + k, 0:high, :] for k in range(both)], axis=1)
        right = jnp.concatenate([kernel_ref[both * i + k] for k in range(both)], axis=1)
        return total + mxu(left, right, NT)

    count = pieces // both
    return lax.fori_loop(0, count, one, total, unroll=count <= 8)


def sample_body(groups, *refs):
    out_ref = refs[-1]
    high, n = out_ref.shape
    total = refs[2 * groups][...] if len(refs) == 2 * groups + 2 else jnp.zeros((high, n), F32)
    for g in range(groups):
        total = accumulate(refs[g], refs[groups + g], high, total)
    out_ref[...] = total


def leaf_body(blocks, place_ref, points_ref, probe_ref, kernel_ref, *refs):
    h_ref, m_ref, t_ref = refs[blocks:]
    n = h_ref.shape[0]
    rows, cols = grids(n)
    high = n // blocks
    for o in range(blocks):
        total = refs[o][...]
        if o == blocks - 1:
            total = accumulate(probe_ref, kernel_ref, high, total)
        at = pl.multiple_of((place_ref[0] ^ o) * high, high)
        m_ref[pl.ds(at, high), :] = total
    half = n // 2
    inside = (cols - jnp.where(cols >= half, half, 0)).astype(F32) < points_ref[3:4, 0:1]
    matrix = jnp.where(inside, m_ref[...], 0.0)
    m_ref[...] = matrix
    shift, by_row, by_col = factorize(dot3(matrix, matrix, NT), t_ref)
    in_rank = rows.astype(F32) < points_ref[4:5, 0:1]
    value = jnp.where(in_rank, projected_rows(t_ref, by_row, by_col), 0.0)
    h_ref[...] = rows_gram(value) * shift


def basis_body(points_ref, t_ref, m_ref, b_ref):
    n = t_ref.shape[0]
    rows, cols = grids(n)
    held = t_ref[...]
    matrix = m_ref[...]
    shift = jnp.sum(jnp.sum(matrix * matrix, axis=0, keepdims=True), axis=1, keepdims=True) / n
    diagonal = jnp.where(rows == cols, held, 0.0)
    by_row = jnp.sum(diagonal, axis=1, keepdims=True)
    by_col = jnp.sum(diagonal, axis=0, keepdims=True)
    inverse = jnp.where(rows > cols, held / by_col, jnp.where(rows == cols, 1.0, 0.0))
    scale = jnp.where(rows.astype(F32) < points_ref[4:5, 0:1], lax.rsqrt(by_row * shift), 0.0)
    b_ref[...] = dot3(inverse * scale, matrix, NN)


def inverse(matrix):
    n = matrix.shape[0]
    rows, cols = grids(n)
    high, low = split_bf16(matrix)
    least, most = 1.0, 1.001 * (n + 1.0)
    scale = 2.0 / (least + most)
    guess = jnp.where(rows == cols, 2.0 * scale, 0.0) - scale * scale * matrix
    spread = (most - least) / (most + least)
    while spread > 1e-3:
        least = 1.0 - spread * spread
        scale = 2.0 / (1.0 + least)
        spread = (1.0 - least) / (1.0 + least)
        if spread > COARSE:
            rough = guess.astype(BF16)
            product = mxu(high, rough, NN).astype(BF16)
            change = mxu(rough, product, NN)
        else:
            gh, gl = split_bf16(guess)
            product = mxu(high, gh, NN) + (mxu(high, gl, NN) + mxu(low, gh, NN))
            ph, pl_ = split_bf16(product)
            change = mxu(gh, ph, NN) + (mxu(gh, pl_, NN) + mxu(gl, ph, NN))
        guess = (2.0 * scale) * guess - (scale * scale) * change
    return guess


def node_body(own_ref, other_ref, h_ref, packed_ref):
    gram = own_ref[...] + other_ref[...]
    n = gram.shape[0]
    rows, cols = grids(n)
    shift = trace(gram) / n
    scaled = gram / shift
    start = scaled + jnp.where(rows == cols, 1.0, 0.0)
    h_ref[...] = (scaled - jnp.where(rows == cols, 1.0, 0.0) + inverse(start)) * shift
    fold(h_ref, packed_ref)


def top_body(own_ref, other_ref, z_ref, t_ref):
    shift, by_row, by_col = factorize(unfold_add(other_ref, own_ref), t_ref)
    value = projected_rows(t_ref, by_row, by_col)
    z_ref[...] = (value * jnp.sqrt(shift)).T


def call(body, outs, operands, specs=None, scratch=(), flops=0):
    bytes_used = sum(x.size * x.dtype.itemsize for x in (*outs, *operands))
    return pl.pallas_call(
        body,
        out_shape=list(outs),
        in_specs=list(specs or [VMEM] * len(operands)),
        out_specs=[VMEM] * len(outs),
        scratch_shapes=list(scratch),
        cost_estimate=pl.CostEstimate(flops=flops, bytes_accessed=bytes_used, transcendentals=0),
        compiler_params=pltpu.CompilerParams(vmem_limit_bytes=2 * bytes_used + (6 << 20)),
    )(*operands)


def flip(value, rows_mask, probe_mask=0):
    probe_size = lax.axis_size("probe")
    if probe_mask == 0:
        pairs = [(i, i ^ rows_mask) for i in range(lax.axis_size("rows"))]
        return lax.ppermute(value, "rows", pairs)
    if rows_mask == 0:
        pairs = [(i, i ^ probe_mask) for i in range(probe_size)]
        return lax.ppermute(value, "probe", pairs)
    pairs = [
        (i * probe_size + j, (i ^ rows_mask) * probe_size + (j ^ probe_mask))
        for i in range(lax.axis_size("rows"))
        for j in range(probe_size)
    ]
    return lax.ppermute(value, ("rows", "probe"), pairs)


def per_device(targets, sources, probes, cluster_sizes, leaf_ranks):
    rows_size = lax.axis_size("rows")
    probe_size = lax.axis_size("probe")
    col_total = sources.shape[1] * rows_size
    high = probes.shape[0]
    n = high * probe_size
    leaf_rows = targets.shape[1] // probe_size
    place = lax.axis_index("probe")

    points = lax.dynamic_slice_in_dim(targets, place * leaf_rows, leaf_rows, 1)
    limits = [jnp.full((1, leaf_rows), x[0]).astype(F32) for x in (cluster_sizes, leaf_ranks)]
    points = jnp.concatenate([points, *limits, jnp.zeros((3, leaf_rows), F32)], axis=0)

    def evaluate(arrays):
        outs = [jax.ShapeDtypeStruct((x.shape[0], 2 * leaf_rows, x.shape[2]), BF16) for x in arrays]
        return call(
            lambda *refs: kernel_body(col_total, high, *refs), outs, [points, *arrays],
            flops=2000 * sum(x.size for x in outs),
        )

    pieces = jnp.concatenate([probes, jnp.pad(sources, ((0, 16 - sources.shape[0]), (0, 0)))], axis=0)[None]
    mask = rows_size // 2
    while mask > 2:
        low = mask // 2 if mask // 2 > 2 else 0
        received = []
        for m in [low, mask, mask + low] if low else [mask]:
            received.append(flip(pieces, m))
        pieces = jnp.concatenate([pieces, *received], axis=0)
        mask //= 4 if low else 2
    masks = [0, 2] if rows_size > 2 else [0]
    probes_only = pieces[:, :high]
    square = jax.ShapeDtypeStruct((n, n), F32)
    block = jax.ShapeDtypeStruct((high, n), F32)
    values = []
    samples = []
    for o in range(probe_size):
        held = []
        for m in masks:
            near = pieces if (m, o) == (0, 0) else flip(probes_only if o else pieces, m, o)
            far = flip(near, 1)
            held += [near, far]
            if o == 0:
                for x in (near, far):
                    values += evaluate([x])
        count = len(held) - (o == probe_size - 1)
        cuts = (0, 2, count) if o == 0 and count > 2 else (0, count)
        total = []
        for low, top in zip(cuts, cuts[1:]):
            total = call(
                lambda *refs, count=top - low: sample_body(count, *refs), [block],
                [*held[low:top], *values[low:top], *total], flops=200 * high * n * n,
            )
        samples += total
    scratch = [pltpu.VMEM((n, n), F32)]
    h, m, t = call(
        lambda *refs: leaf_body(probe_size, *refs), [square] * 3,
        [place[None], points, held[-1], values[-1], *samples],
        specs=[SMEM] + [VMEM] * (3 + len(samples)), flops=n**3,
    )
    other = flip(h, 1)
    basis = call(basis_body, [square], [points, t, m], flops=60 * n**3)[0]
    packed = jax.ShapeDtypeStruct((n + 8, n // 2), F32)
    h, sent = call(node_body, [square, packed], [h, other], flops=n**3)
    other = flip(sent, 2)
    top = call(top_body, [square], [h, other], scratch=scratch, flops=n**3)[0]
    return (basis.reshape(n, 2, leaf_rows), top[None])


def solution(mesh):
    return jax.shard_map(
        per_device,
        mesh=mesh,
        in_specs=(
            P(None, "rows"),
            P(None, "rows"),
            P("probe", "rows"),
            P(("rows", "probe")),
            P(("rows", "probe")),
        ),
        out_specs=(P(None, None, ("rows", "probe")), P(("rows", "probe"), None, None)),
        check_vma=False,
    )
```

```python
import math

import jax
import jax.numpy as jnp
from jax import lax
from jax.experimental import pallas as pl
from jax.experimental.pallas import tpu as pltpu
from jax.sharding import PartitionSpec as P


wavenumber = 30.0
softening = 0.02

F32 = jnp.float32
BF16 = jnp.bfloat16
VMEM = pl.BlockSpec(memory_space=pltpu.VMEM)
SMEM = pl.BlockSpec(memory_space=pltpu.SMEM)
NN = ((1,), (0,))
NT = ((1,), (1,))

SINE = (3.1415927410125732, -5.167710304260254, 2.550077438354492, -0.598291277885437, 0.07765766233205795)
COSINE = (0.9999999403953552, -4.934792995452881, 4.058411121368408, -1.331876516342163, 0.21968960762023926)

LANES = 128
PANEL = 64
CHUNK = 256
COARSE = 0.2


def split_bf16(value):
    high = value.astype(BF16)
    return high, (value - high.astype(F32)).astype(BF16)


def mxu(left, right, dims):
    return lax.dot_general(left, right, (dims, ((), ())), preferred_element_type=F32)


def dot3(left, right, dims):
    lh, ll = split_bf16(left)
    rh, rl = split_bf16(right)
    return mxu(lh, rh, dims) + (mxu(lh, rl, dims) + mxu(ll, rh, dims))


def pick_lane(tile, lane):
    where = jnp.full(tile.shape, lane, jnp.int32)
    return jnp.take_along_axis(tile, where, axis=1, mode="promise_in_bounds")


def pick_row(tile, row):
    return jnp.broadcast_to(tile[row : row + 1, :], tile.shape)


def sweep(t_ref, begin=0, stop=None):
    n = t_ref.shape[0]
    tiles = n // LANES
    steps = PANEL // 8
    lane = lax.broadcasted_iota(jnp.int32, (8, LANES), 1)
    row = lax.broadcasted_iota(jnp.int32, (8, LANES), 0)
    along_lanes = [jnp.zeros((8, LANES), F32) for _ in range(tiles)]
    along_rows = []
    for start in range(begin, stop or n, PANEL):
        at, low = divmod(start, LANES)
        block = [
            [t_ref[start + 8 * i : start + 8 * i + 8, LANES * t : LANES * (t + 1)] for t in range(tiles)]
            for i in range(steps)
        ]
        pivots = [jnp.zeros((8, LANES), F32) for _ in range(steps)]
        ahead = None
        for i0 in range(steps):
            first = low + 8 * i0

            def columns(i, base):
                return [pick_lane(block[i][at], base + a) for a in range(8)]

            cols = ahead or columns(i0, first)
            below = {i: columns(i, first) for i in range(i0 + 1, steps)}
            after = columns(i0 + 1, first + 8) if i0 + 1 < steps else None
            sums = [jnp.zeros((8, LANES), F32)] * 8
            for a in range(8):
                here = lane == first + a
                pivot = pick_row(cols[a], a)
                inverse = 1.0 / pivot
                pivots[i0] = jnp.where(row == a, pivot, pivots[i0])
                factor = jnp.where(row > a, cols[a] * inverse, 0.0)
                entries = {b: pick_row(cols[b], a) for b in range(a + 1, 8)}
                for b in entries:
                    cols[b] = cols[b] - factor * entries[b]
                swept = [pick_row(block[i0][t], a) for t in range(tiles)]
                swept[at] = jnp.where(here, 2.0 * swept[at], swept[at])
                for t in range(tiles):
                    block[i0][t] = block[i0][t] - factor * swept[t]
                for i, mine in below.items():
                    factor = mine[a] * inverse
                    for b in entries:
                        mine[b] = mine[b] - factor * entries[b]
                    for t in range(tiles):
                        block[i][t] = block[i][t] - factor * swept[t]
                    if after and i == i0 + 1:
                        sums = [x + factor * pick_row(mine[a], b) for b, x in enumerate(sums)]
            along_lanes[at] = along_lanes[at] + jnp.where(lane == first + row, block[i0][at], 0.0)
            ahead = after and [x - y for x, y in zip(after, sums)]
        for i in range(steps):
            for t in range(tiles):
                t_ref[start + 8 * i : start + 8 * i + 8, LANES * t : LANES * (t + 1)] = block[i][t]
        along_rows += pivots
        end = start + PANEL
        if end < n:
            rowi = lax.broadcasted_iota(jnp.int32, (PANEL, n), 0)
            coli = lax.broadcasted_iota(jnp.int32, (PANEL, n), 1)
            whole = jnp.concatenate([jnp.concatenate(x, axis=1) for x in block], axis=0)
            kept = jnp.where((coli < end) & (coli - start > rowi), 0.0, whole)
            scale = 1.0 / jnp.concatenate(pivots, axis=0)
            base = end // LANES * LANES
            factors = whole[:, base:] * jnp.concatenate([scale] * ((n - base) // LANES), axis=1)
            fh, fl = split_bf16(factors)
            kh, kl = split_bf16(kept)
            left = jnp.concatenate([fh, fh, fl], axis=0).T
            right = jnp.concatenate([kh, kl, kh], axis=0)
            for to in range(end, n, CHUNK):
                high = min(CHUNK, n - to)
                change = mxu(left[to - base : to - base + high, :], right, NN)
                colr = lax.broadcasted_iota(jnp.int32, (high, LANES), 1)
                for t in range(tiles):
                    at_t = slice(LANES * t, LANES * (t + 1))
                    rest = t_ref[to : to + high, at_t]
                    if t == at:
                        rest = jnp.where((colr >= low) & (colr < low + PANEL), 0.0, rest)
                    t_ref[to : to + high, at_t] = rest - change[:, at_t]
    return along_lanes, along_rows


def grids(n):
    rows = lax.broadcasted_iota(jnp.int32, (n, n), 0)
    cols = lax.broadcasted_iota(jnp.int32, (n, n), 1)
    return rows, cols


def trace(matrix):
    rows, cols = grids(matrix.shape[0])
    diagonal = jnp.where(rows == cols, matrix, 0.0)
    return jnp.sum(jnp.sum(diagonal, axis=0, keepdims=True), axis=1, keepdims=True)


def factorize(gram, t_ref):
    n = gram.shape[0]
    rows, cols = grids(n)
    shift = trace(gram) / n
    t_ref[...] = gram / shift + jnp.where(rows == cols, 1.0, 0.0)
    along_lanes, along_rows = sweep(t_ref)
    sums = [jnp.sum(x, axis=0, keepdims=True) for x in along_lanes]
    by_col = jnp.concatenate([jnp.broadcast_to(x, (n, LANES)) for x in sums], axis=1)
    by_row = jnp.concatenate([jnp.concatenate([x] * (n // LANES), axis=1) for x in along_rows], axis=0)
    return shift, by_row, by_col


def projected_rows(t_ref, by_row, by_col):
    rows, cols = grids(t_ref.shape[0])
    held = t_ref[...]
    return lax.rsqrt(by_row) * jnp.where(
        rows < cols, held, jnp.where(rows > cols, -held / by_col, by_row - 1.0)
    )


def fold(full_ref, packed_ref):
    n = full_ref.shape[0]
    half = n // 2
    rows, cols = grids(half)
    upper = full_ref[0:half, 0:half]
    lower = full_ref[half:n, half:n]
    packed_ref[0:half, :] = full_ref[0:half, half:n]
    packed_ref[half:n, :] = jnp.where(rows <= cols, upper, lower)
    packed_ref[n : n + 8, :] = jnp.broadcast_to(
        jnp.sum(jnp.where(rows == cols, lower, 0.0), axis=0, keepdims=True), (8, half)
    )


def unfold_add(packed_ref, full_ref):
    n = full_ref.shape[0]
    half = n // 2
    rows, cols = grids(half)
    corner = packed_ref[0:half, :]
    both = packed_ref[half:n, :]
    turned = both.T
    line = jnp.broadcast_to(packed_ref[n : n + 1, :], (half, half))
    upper = jnp.where(rows <= cols, both, turned)
    lower = jnp.where(rows == cols, line, jnp.where(rows > cols, both, turned))
    top = jnp.concatenate([upper, corner], axis=1)
    bottom = jnp.concatenate([corner.T, lower], axis=1)
    return full_ref[...] + jnp.concatenate([top, bottom], axis=0)


def kernel_body(col_total, high, targets_ref, *refs):
    m = targets_ref.shape[1]
    width = refs[0].shape[2]
    turned = jnp.concatenate([targets_ref[...], jnp.zeros((m - 8, m), F32)], axis=0).T
    points = [jnp.broadcast_to(turned[:, c : c + 1], (m, width)) for c in range(3)]
    count = len(refs) // 2
    for piece_ref, out_ref in zip(refs[:count], refs[count:]):
        for i in range(piece_ref.shape[0]):
            source = piece_ref[i, high : high + 3, :].astype(F32)
            first, second = kernel_values(source, points, col_total)
            out_ref[i, 0:m, :] = first
            out_ref[i, m : 2 * m, :] = second


def kernel_values(source, points, col_total):
    size = 1.0 / math.sqrt(col_total)
    square = softening * softening
    for c in range(3):
        diff = source[c : c + 1, :] - points[c]
        square = square + diff * diff
    near = lax.rsqrt(square)
    amplitude = near * size
    turns = (square * near) * (wavenumber / math.pi)
    whole = jnp.round(turns)
    rest = turns - whole
    r2 = rest * rest
    sine = rest * power_series(SINE, r2)
    cosine = power_series(COSINE, r2)
    odd = (whole.astype(jnp.int32) & 1) == 1
    amplitude = jnp.where(odd, -amplitude, amplitude)
    return (amplitude * cosine).astype(BF16), (amplitude * sine).astype(BF16)


def power_series(terms, x):
    value = terms[-1]
    for term in terms[-2::-1]:
        value = value * x + term
    return value


def accumulate(probe_ref, kernel_ref, high, total):
    pieces = probe_ref.shape[0]
    both = 2 if pieces % 2 == 0 else 1

    def one(i, total):
        left = jnp.concatenate([probe_ref[both * i + k, 0:high, :] for k in range(both)], axis=1)
        right = jnp.concatenate([kernel_ref[both * i + k] for k in range(both)], axis=1)
        return total + mxu(left, right, NT)

    count = pieces // both
    return lax.fori_loop(0, count, one, total, unroll=count <= 8)


def sample_body(groups, *refs):
    out_ref = refs[-1]
    high, n = out_ref.shape
    total = refs[2 * groups][...] if len(refs) == 2 * groups + 2 else jnp.zeros((high, n), F32)
    for g in range(groups):
        total = accumulate(refs[g], refs[groups + g], high, total)
    out_ref[...] = total


def leaf_body(blocks, place_ref, points_ref, probe_ref, kernel_ref, *refs):
    h_ref, m_ref, a_ref = refs[blocks:]
    n = h_ref.shape[0]
    rows, cols = grids(n)
    high = n // blocks
    for o in range(blocks):
        total = refs[o][...]
        if o == blocks - 1:
            total = accumulate(probe_ref, kernel_ref, high, total)
        at = pl.multiple_of((place_ref[0] ^ o) * high, high)
        m_ref[pl.ds(at, high), :] = total
    half = n // 2
    inside = (cols - jnp.where(cols >= half, half, 0)).astype(F32) < points_ref[3:4, 0:1]
    matrix = jnp.where(inside, m_ref[...], 0.0)
    m_ref[...] = matrix
    gram = dot3(matrix, matrix, NT)
    shift = trace(gram) / n
    scaled = gram / shift
    unit = jnp.where(rows == cols, 1.0, 0.0)
    a_ref[...] = scaled + unit
    rank = points_ref[4:5, 0:1]
    kept_row = rows.astype(F32) < rank
    kept_col = cols.astype(F32) < rank
    inner = jnp.where(kept_row & kept_col, scaled, 0.0)
    turned = inverse(inner + unit)
    outer = jnp.where(kept_row & (cols.astype(F32) >= rank), scaled, 0.0)
    solved = jnp.where(kept_row, jnp.where(kept_col, unit - turned, dot3(turned, outer, NN)), 0.0)
    h_ref[...] = dot3(jnp.where(kept_col, scaled, 0.0), solved, NN) * shift


def sweep_body(begin, stop, a_ref, t_ref):
    t_ref[...] = a_ref[...]
    sweep(t_ref, begin, stop)


def basis_body(points_ref, t_ref, m_ref, b_ref):
    n = t_ref.shape[0]
    rows, cols = grids(n)
    held = t_ref[...]
    matrix = m_ref[...]
    shift = jnp.sum(jnp.sum(matrix * matrix, axis=0, keepdims=True), axis=1, keepdims=True) / n
    diagonal = jnp.where(rows == cols, held, 0.0)
    by_row = jnp.sum(diagonal, axis=1, keepdims=True)
    by_col = jnp.sum(diagonal, axis=0, keepdims=True)
    inverse = jnp.where(rows > cols, held / by_col, jnp.where(rows == cols, 1.0, 0.0))
    scale = jnp.where(rows.astype(F32) < points_ref[4:5, 0:1], lax.rsqrt(by_row * shift), 0.0)
    b_ref[...] = dot3(inverse * scale, matrix, NN)


def inverse(matrix):
    n = matrix.shape[0]
    rows, cols = grids(n)
    high, low = split_bf16(matrix)
    least, most = 1.0, 1.001 * (n + 1.0)
    scale = 2.0 / (least + most)
    guess = jnp.where(rows == cols, 2.0 * scale, 0.0) - scale * scale * matrix
    spread = (most - least) / (most + least)
    while spread > 1e-3:
        least = 1.0 - spread * spread
        scale = 2.0 / (1.0 + least)
        spread = (1.0 - least) / (1.0 + least)
        if spread > COARSE:
            rough = guess.astype(BF16)
            product = mxu(high, rough, NN).astype(BF16)
            change = mxu(rough, product, NN)
        else:
            gh, gl = split_bf16(guess)
            product = mxu(high, gh, NN) + (mxu(high, gl, NN) + mxu(low, gh, NN))
            ph, pl_ = split_bf16(product)
            change = mxu(gh, ph, NN) + (mxu(gh, pl_, NN) + mxu(gl, ph, NN))
        guess = (2.0 * scale) * guess - (scale * scale) * change
    return guess


def node_body(own_ref, other_ref, h_ref, packed_ref):
    gram = own_ref[...] + other_ref[...]
    n = gram.shape[0]
    rows, cols = grids(n)
    shift = trace(gram) / n
    scaled = gram / shift
    start = scaled + jnp.where(rows == cols, 1.0, 0.0)
    h_ref[...] = (scaled - jnp.where(rows == cols, 1.0, 0.0) + inverse(start)) * shift
    fold(h_ref, packed_ref)


def top_body(own_ref, other_ref, z_ref, t_ref):
    shift, by_row, by_col = factorize(unfold_add(other_ref, own_ref), t_ref)
    value = projected_rows(t_ref, by_row, by_col)
    z_ref[...] = (value * jnp.sqrt(shift)).T


def call(body, outs, operands, specs=None, scratch=(), flops=0):
    bytes_used = sum(x.size * x.dtype.itemsize for x in (*outs, *operands))
    return pl.pallas_call(
        body,
        out_shape=list(outs),
        in_specs=list(specs or [VMEM] * len(operands)),
        out_specs=[VMEM] * len(outs),
        scratch_shapes=list(scratch),
        cost_estimate=pl.CostEstimate(flops=flops, bytes_accessed=bytes_used, transcendentals=0),
        compiler_params=pltpu.CompilerParams(vmem_limit_bytes=2 * bytes_used + (6 << 20)),
    )(*operands)


def flip(value, rows_mask, probe_mask=0):
    probe_size = lax.axis_size("probe")
    if probe_mask == 0:
        pairs = [(i, i ^ rows_mask) for i in range(lax.axis_size("rows"))]
        return lax.ppermute(value, "rows", pairs)
    if rows_mask == 0:
        pairs = [(i, i ^ probe_mask) for i in range(probe_size)]
        return lax.ppermute(value, "probe", pairs)
    pairs = [
        (i * probe_size + j, (i ^ rows_mask) * probe_size + (j ^ probe_mask))
        for i in range(lax.axis_size("rows"))
        for j in range(probe_size)
    ]
    return lax.ppermute(value, ("rows", "probe"), pairs)


def per_device(targets, sources, probes, cluster_sizes, leaf_ranks):
    rows_size = lax.axis_size("rows")
    probe_size = lax.axis_size("probe")
    col_total = sources.shape[1] * rows_size
    high = probes.shape[0]
    n = high * probe_size
    leaf_rows = targets.shape[1] // probe_size
    place = lax.axis_index("probe")

    points = lax.dynamic_slice_in_dim(targets, place * leaf_rows, leaf_rows, 1)
    limits = [jnp.full((1, leaf_rows), x[0]).astype(F32) for x in (cluster_sizes, leaf_ranks)]
    points = jnp.concatenate([points, *limits, jnp.zeros((3, leaf_rows), F32)], axis=0)

    def evaluate(arrays):
        outs = [jax.ShapeDtypeStruct((x.shape[0], 2 * leaf_rows, x.shape[2]), BF16) for x in arrays]
        return call(
            lambda *refs: kernel_body(col_total, high, *refs), outs, [points, *arrays],
            flops=2000 * sum(x.size for x in outs),
        )

    pieces = jnp.concatenate([probes, jnp.pad(sources, ((0, 16 - sources.shape[0]), (0, 0)))], axis=0)[None]
    mask = rows_size // 2
    while mask > 2:
        low = mask // 2 if mask // 2 > 2 else 0
        received = []
        for m in [low, mask, mask + low] if low else [mask]:
            received.append(flip(pieces, m))
        pieces = jnp.concatenate([pieces, *received], axis=0)
        mask //= 4 if low else 2
    masks = [0, 2] if rows_size > 2 else [0]
    probes_only = pieces[:, :high]
    square = jax.ShapeDtypeStruct((n, n), F32)
    block = jax.ShapeDtypeStruct((high, n), F32)
    values = []
    samples = []
    for o in range(probe_size):
        held = []
        for m in masks:
            near = pieces if (m, o) == (0, 0) else flip(probes_only if o else pieces, m, o)
            far = flip(near, 1)
            held += [near, far]
            if o == 0:
                for x in (near, far):
                    values += evaluate([x])
        count = len(held) - (o == probe_size - 1)
        cuts = (0, 2, count) if o == 0 and count > 2 else (0, count)
        total = []
        for low, top in zip(cuts, cuts[1:]):
            total = call(
                lambda *refs, count=top - low: sample_body(count, *refs), [block],
                [*held[low:top], *values[low:top], *total], flops=200 * high * n * n,
            )
        samples += total
    scratch = [pltpu.VMEM((n, n), F32)]
    h, m, t = call(
        lambda *refs: leaf_body(probe_size, *refs), [square] * 3,
        [place[None], points, held[-1], values[-1], *samples],
        specs=[SMEM] + [VMEM] * (3 + len(samples)), flops=n**3,
    )
    other = flip(h, 1)
    cuts = (0, PANEL, n)
    for begin, stop in zip(cuts, cuts[1:]):
        t = call(
            lambda *refs, begin=begin, stop=stop: sweep_body(begin, stop, *refs), [square], [t],
            flops=200 * n**3,
        )[0]
    basis = call(basis_body, [square], [points, t, m], flops=60 * n**3)[0]
    packed = jax.ShapeDtypeStruct((n + 8, n // 2), F32)
    h, sent = call(node_body, [square, packed], [h, other], flops=n**3)
    other = flip(sent, 2)
    top = call(top_body, [square], [h, other], scratch=scratch, flops=n**3)[0]
    return (basis.reshape(n, 2, leaf_rows), top[None])


def solution(mesh):
    return jax.shard_map(
        per_device,
        mesh=mesh,
        in_specs=(
            P(None, "rows"),
            P(None, "rows"),
            P("probe", "rows"),
            P(("rows", "probe")),
            P(("rows", "probe")),
        ),
        out_specs=(P(None, None, ("rows", "probe")), P(("rows", "probe"), None, None)),
        check_vma=False,
    )
```

```python
import math

import jax
import jax.numpy as jnp
from jax import lax
from jax.experimental import pallas as pl
from jax.experimental.pallas import tpu as pltpu
from jax.sharding import PartitionSpec as P


wavenumber = 30.0
softening = 0.02

F32 = jnp.float32
BF16 = jnp.bfloat16
VMEM = pl.BlockSpec(memory_space=pltpu.VMEM)
SMEM = pl.BlockSpec(memory_space=pltpu.SMEM)
NN = ((1,), (0,))
NT = ((1,), (1,))

SINE = (3.1415927410125732, -5.167710304260254, 2.550077438354492, -0.598291277885437, 0.07765766233205795)
COSINE = (0.9999999403953552, -4.934792995452881, 4.058411121368408, -1.331876516342163, 0.21968960762023926)

LANES = 128
PANEL = 64
CHUNK = 256
COARSE = 0.2


def split_bf16(value):
    high = value.astype(BF16)
    return high, (value - high.astype(F32)).astype(BF16)


def mxu(left, right, dims):
    return lax.dot_general(left, right, (dims, ((), ())), preferred_element_type=F32)


def dot3(left, right, dims):
    lh, ll = split_bf16(left)
    rh, rl = split_bf16(right)
    return mxu(lh, rh, dims) + (mxu(lh, rl, dims) + mxu(ll, rh, dims))


def pick_lane(tile, lane):
    where = jnp.full(tile.shape, lane, jnp.int32)
    return jnp.take_along_axis(tile, where, axis=1, mode="promise_in_bounds")


def pick_row(tile, row):
    return jnp.broadcast_to(tile[row : row + 1, :], tile.shape)


def sweep(t_ref, begin=0, stop=None):
    n = t_ref.shape[0]
    tiles = n // LANES
    steps = PANEL // 8
    lane = lax.broadcasted_iota(jnp.int32, (8, LANES), 1)
    row = lax.broadcasted_iota(jnp.int32, (8, LANES), 0)
    along_lanes = [jnp.zeros((8, LANES), F32) for _ in range(tiles)]
    along_rows = []
    for start in range(begin, stop or n, PANEL):
        at, low = divmod(start, LANES)
        block = [
            [t_ref[start + 8 * i : start + 8 * i + 8, LANES * t : LANES * (t + 1)] for t in range(tiles)]
            for i in range(steps)
        ]
        pivots = [jnp.zeros((8, LANES), F32) for _ in range(steps)]
        ahead = None
        for i0 in range(steps):
            first = low + 8 * i0

            def columns(i, base):
                return [pick_lane(block[i][at], base + a) for a in range(8)]

            cols = ahead or columns(i0, first)
            below = {i: columns(i, first) for i in range(i0 + 1, steps)}
            after = columns(i0 + 1, first + 8) if i0 + 1 < steps else None
            sums = [jnp.zeros((8, LANES), F32)] * 8
            for a in range(8):
                here = lane == first + a
                pivot = pick_row(cols[a], a)
                inverse = 1.0 / pivot
                pivots[i0] = jnp.where(row == a, pivot, pivots[i0])
                factor = jnp.where(row > a, cols[a] * inverse, 0.0)
                entries = {b: pick_row(cols[b], a) for b in range(a + 1, 8)}
                for b in entries:
                    cols[b] = cols[b] - factor * entries[b]
                swept = [pick_row(block[i0][t], a) for t in range(tiles)]
                swept[at] = jnp.where(here, 2.0 * swept[at], swept[at])
                for t in range(tiles):
                    block[i0][t] = block[i0][t] - factor * swept[t]
                for i, mine in below.items():
                    factor = mine[a] * inverse
                    for b in entries:
                        mine[b] = mine[b] - factor * entries[b]
                    for t in range(tiles):
                        block[i][t] = block[i][t] - factor * swept[t]
                    if after and i == i0 + 1:
                        sums = [x + factor * pick_row(mine[a], b) for b, x in enumerate(sums)]
            along_lanes[at] = along_lanes[at] + jnp.where(lane == first + row, block[i0][at], 0.0)
            ahead = after and [x - y for x, y in zip(after, sums)]
        for i in range(steps):
            for t in range(tiles):
                t_ref[start + 8 * i : start + 8 * i + 8, LANES * t : LANES * (t + 1)] = block[i][t]
        along_rows += pivots
        end = start + PANEL
        if end < n:
            rowi = lax.broadcasted_iota(jnp.int32, (PANEL, n), 0)
            coli = lax.broadcasted_iota(jnp.int32, (PANEL, n), 1)
            whole = jnp.concatenate([jnp.concatenate(x, axis=1) for x in block], axis=0)
            kept = jnp.where((coli < end) & (coli - start > rowi), 0.0, whole)
            scale = 1.0 / jnp.concatenate(pivots, axis=0)
            base = end // LANES * LANES
            factors = whole[:, base:] * jnp.concatenate([scale] * ((n - base) // LANES), axis=1)
            fh, fl = split_bf16(factors)
            kh, kl = split_bf16(kept)
            left = jnp.concatenate([fh, fh, fl], axis=0).T
            right = jnp.concatenate([kh, kl, kh], axis=0)
            for to in range(end, n, CHUNK):
                high = min(CHUNK, n - to)
                change = mxu(left[to - base : to - base + high, :], right, NN)
                colr = lax.broadcasted_iota(jnp.int32, (high, LANES), 1)
                for t in range(tiles):
                    at_t = slice(LANES * t, LANES * (t + 1))
                    rest = t_ref[to : to + high, at_t]
                    if t == at:
                        rest = jnp.where((colr >= low) & (colr < low + PANEL), 0.0, rest)
                    t_ref[to : to + high, at_t] = rest - change[:, at_t]
    return along_lanes, along_rows


def grids(n):
    rows = lax.broadcasted_iota(jnp.int32, (n, n), 0)
    cols = lax.broadcasted_iota(jnp.int32, (n, n), 1)
    return rows, cols


def trace(matrix):
    rows, cols = grids(matrix.shape[0])
    diagonal = jnp.where(rows == cols, matrix, 0.0)
    return jnp.sum(jnp.sum(diagonal, axis=0, keepdims=True), axis=1, keepdims=True)


def factorize(gram, t_ref):
    n = gram.shape[0]
    rows, cols = grids(n)
    shift = trace(gram) / n
    t_ref[...] = gram / shift + jnp.where(rows == cols, 1.0, 0.0)
    along_lanes, along_rows = sweep(t_ref)
    sums = [jnp.sum(x, axis=0, keepdims=True) for x in along_lanes]
    by_col = jnp.concatenate([jnp.broadcast_to(x, (n, LANES)) for x in sums], axis=1)
    by_row = jnp.concatenate([jnp.concatenate([x] * (n // LANES), axis=1) for x in along_rows], axis=0)
    return shift, by_row, by_col


def projected_rows(t_ref, by_row, by_col):
    rows, cols = grids(t_ref.shape[0])
    held = t_ref[...]
    return lax.rsqrt(by_row) * jnp.where(
        rows < cols, held, jnp.where(rows > cols, -held / by_col, by_row - 1.0)
    )


def fold(full_ref, packed_ref):
    n = full_ref.shape[0]
    half = n // 2
    rows, cols = grids(half)
    upper = full_ref[0:half, 0:half]
    lower = full_ref[half:n, half:n]
    packed_ref[0:half, :] = full_ref[0:half, half:n]
    packed_ref[half:n, :] = jnp.where(rows <= cols, upper, lower)
    packed_ref[n : n + 8, :] = jnp.broadcast_to(
        jnp.sum(jnp.where(rows == cols, lower, 0.0), axis=0, keepdims=True), (8, half)
    )


def unfold_add(packed_ref, full_ref):
    n = full_ref.shape[0]
    half = n // 2
    rows, cols = grids(half)
    corner = packed_ref[0:half, :]
    both = packed_ref[half:n, :]
    turned = both.T
    line = jnp.broadcast_to(packed_ref[n : n + 1, :], (half, half))
    upper = jnp.where(rows <= cols, both, turned)
    lower = jnp.where(rows == cols, line, jnp.where(rows > cols, both, turned))
    top = jnp.concatenate([upper, corner], axis=1)
    bottom = jnp.concatenate([corner.T, lower], axis=1)
    return full_ref[...] + jnp.concatenate([top, bottom], axis=0)


def kernel_body(col_total, high, targets_ref, *refs):
    m = targets_ref.shape[1]
    width = refs[0].shape[2]
    turned = jnp.concatenate([targets_ref[...], jnp.zeros((m - 8, m), F32)], axis=0).T
    points = [jnp.broadcast_to(turned[:, c : c + 1], (m, width)) for c in range(3)]
    count = len(refs) // 2
    for piece_ref, out_ref in zip(refs[:count], refs[count:]):
        for i in range(piece_ref.shape[0]):
            source = piece_ref[i, high : high + 3, :].astype(F32)
            first, second = kernel_values(source, points, col_total)
            out_ref[i, 0:m, :] = first
            out_ref[i, m : 2 * m, :] = second


def kernel_values(source, points, col_total):
    size = 1.0 / math.sqrt(col_total)
    square = softening * softening
    for c in range(3):
        diff = source[c : c + 1, :] - points[c]
        square = square + diff * diff
    near = lax.rsqrt(square)
    amplitude = near * size
    turns = (square * near) * (wavenumber / math.pi)
    whole = jnp.round(turns)
    rest = turns - whole
    r2 = rest * rest
    sine = rest * power_series(SINE, r2)
    cosine = power_series(COSINE, r2)
    odd = (whole.astype(jnp.int32) & 1) == 1
    amplitude = jnp.where(odd, -amplitude, amplitude)
    return (amplitude * cosine).astype(BF16), (amplitude * sine).astype(BF16)


def power_series(terms, x):
    value = terms[-1]
    for term in terms[-2::-1]:
        value = value * x + term
    return value


def accumulate(probe_ref, kernel_ref, high, total):
    pieces = probe_ref.shape[0]
    both = 2 if pieces % 2 == 0 else 1

    def one(i, total):
        left = jnp.concatenate([probe_ref[both * i + k, 0:high, :] for k in range(both)], axis=1)
        right = jnp.concatenate([kernel_ref[both * i + k] for k in range(both)], axis=1)
        return total + mxu(left, right, NT)

    count = pieces // both
    return lax.fori_loop(0, count, one, total, unroll=count <= 8)


def sample_body(groups, *refs):
    out_ref = refs[-1]
    high, n = out_ref.shape
    total = refs[2 * groups][...] if len(refs) == 2 * groups + 2 else jnp.zeros((high, n), F32)
    for g in range(groups):
        total = accumulate(refs[g], refs[groups + g], high, total)
    out_ref[...] = total


def leaf_body(blocks, place_ref, points_ref, probe_ref, kernel_ref, *refs):
    h_ref, m_ref, a_ref = refs[blocks:]
    n = h_ref.shape[0]
    rows, cols = grids(n)
    high = n // blocks
    for o in range(blocks):
        total = refs[o][...]
        if o == blocks - 1:
            total = accumulate(probe_ref, kernel_ref, high, total)
        at = pl.multiple_of((place_ref[0] ^ o) * high, high)
        m_ref[pl.ds(at, high), :] = total
    half = n // 2
    inside = (cols - jnp.where(cols >= half, half, 0)).astype(F32) < points_ref[3:4, 0:1]
    matrix = jnp.where(inside, m_ref[...], 0.0)
    m_ref[...] = matrix
    gram = dot3(matrix, matrix, NT)
    shift = trace(gram) / n
    scaled = gram / shift
    unit = jnp.where(rows == cols, 1.0, 0.0)
    a_ref[...] = scaled + unit
    rank = points_ref[4:5, 0:1]
    kept_row = rows.astype(F32) < rank
    kept_col = cols.astype(F32) < rank
    inner = jnp.where(kept_row & kept_col, scaled, 0.0)
    turned = inverse(inner + unit)
    outer = jnp.where(kept_row & (cols.astype(F32) >= rank), scaled, 0.0)
    solved = jnp.where(kept_row, jnp.where(kept_col, unit - turned, dot3(turned, outer, NN)), 0.0)
    h_ref[...] = dot3(jnp.where(kept_col, scaled, 0.0), solved, NN) * shift


def sweep_body(begin, stop, a_ref, t_ref):
    t_ref[...] = a_ref[...]
    sweep(t_ref, begin, stop)


def basis_body(points_ref, t_ref, m_ref, b_ref):
    n = t_ref.shape[0]
    rows, cols = grids(n)
    held = t_ref[...]
    matrix = m_ref[...]
    shift = jnp.sum(jnp.sum(matrix * matrix, axis=0, keepdims=True), axis=1, keepdims=True) / n
    diagonal = jnp.where(rows == cols, held, 0.0)
    by_row = jnp.sum(diagonal, axis=1, keepdims=True)
    by_col = jnp.sum(diagonal, axis=0, keepdims=True)
    inverse = jnp.where(rows > cols, held / by_col, jnp.where(rows == cols, 1.0, 0.0))
    scale = jnp.where(rows.astype(F32) < points_ref[4:5, 0:1], lax.rsqrt(by_row * shift), 0.0)
    basis = dot3(inverse * scale, matrix, NN)
    half = b_ref.shape[2]
    for c in range(2):
        b_ref[:, c, :] = basis[:, c * half : (c + 1) * half]


def inverse(matrix):
    n = matrix.shape[0]
    rows, cols = grids(n)
    high, low = split_bf16(matrix)
    least, most = 1.0, 1.001 * (n + 1.0)
    scale = 2.0 / (least + most)
    guess = jnp.where(rows == cols, 2.0 * scale, 0.0) - scale * scale * matrix
    spread = (most - least) / (most + least)
    while spread > 1e-3:
        least = 1.0 - spread * spread
        scale = 2.0 / (1.0 + least)
        spread = (1.0 - least) / (1.0 + least)
        if spread > COARSE:
            rough = guess.astype(BF16)
            product = mxu(high, rough, NN).astype(BF16)
            change = mxu(rough, product, NN)
        else:
            gh, gl = split_bf16(guess)
            product = mxu(high, gh, NN) + (mxu(high, gl, NN) + mxu(low, gh, NN))
            ph, pl_ = split_bf16(product)
            change = mxu(gh, ph, NN) + (mxu(gh, pl_, NN) + mxu(gl, ph, NN))
        guess = (2.0 * scale) * guess - (scale * scale) * change
    return guess


def node_body(own_ref, other_ref, h_ref, packed_ref):
    gram = own_ref[...] + other_ref[...]
    n = gram.shape[0]
    rows, cols = grids(n)
    shift = trace(gram) / n
    scaled = gram / shift
    start = scaled + jnp.where(rows == cols, 1.0, 0.0)
    h_ref[...] = (scaled - jnp.where(rows == cols, 1.0, 0.0) + inverse(start)) * shift
    fold(h_ref, packed_ref)


def top_body(own_ref, other_ref, basis_ref, z_ref, out_ref, t_ref, sem):
    copy = pltpu.make_async_copy(basis_ref, out_ref, sem)
    copy.start()
    shift, by_row, by_col = factorize(unfold_add(other_ref, own_ref), t_ref)
    value = projected_rows(t_ref, by_row, by_col)
    z_ref[...] = (value * jnp.sqrt(shift)).T
    copy.wait()


def call(body, outs, operands, specs=None, scratch=(), flops=0, out_specs=None):
    bytes_used = sum(x.size * x.dtype.itemsize for x in (*outs, *operands))
    return pl.pallas_call(
        body,
        out_shape=list(outs),
        in_specs=list(specs or [VMEM] * len(operands)),
        out_specs=list(out_specs or [VMEM] * len(outs)),
        scratch_shapes=list(scratch),
        cost_estimate=pl.CostEstimate(flops=flops, bytes_accessed=bytes_used, transcendentals=0),
        compiler_params=pltpu.CompilerParams(vmem_limit_bytes=2 * bytes_used + (6 << 20)),
    )(*operands)


def flip(value, rows_mask, probe_mask=0):
    probe_size = lax.axis_size("probe")
    if probe_mask == 0:
        pairs = [(i, i ^ rows_mask) for i in range(lax.axis_size("rows"))]
        return lax.ppermute(value, "rows", pairs)
    if rows_mask == 0:
        pairs = [(i, i ^ probe_mask) for i in range(probe_size)]
        return lax.ppermute(value, "probe", pairs)
    pairs = [
        (i * probe_size + j, (i ^ rows_mask) * probe_size + (j ^ probe_mask))
        for i in range(lax.axis_size("rows"))
        for j in range(probe_size)
    ]
    return lax.ppermute(value, ("rows", "probe"), pairs)


def per_device(targets, sources, probes, cluster_sizes, leaf_ranks):
    rows_size = lax.axis_size("rows")
    probe_size = lax.axis_size("probe")
    col_total = sources.shape[1] * rows_size
    high = probes.shape[0]
    n = high * probe_size
    leaf_rows = targets.shape[1] // probe_size
    place = lax.axis_index("probe")

    points = lax.dynamic_slice_in_dim(targets, place * leaf_rows, leaf_rows, 1)
    limits = [jnp.full((1, leaf_rows), x[0]).astype(F32) for x in (cluster_sizes, leaf_ranks)]
    points = jnp.concatenate([points, *limits, jnp.zeros((3, leaf_rows), F32)], axis=0)

    def evaluate(arrays):
        outs = [jax.ShapeDtypeStruct((x.shape[0], 2 * leaf_rows, x.shape[2]), BF16) for x in arrays]
        return call(
            lambda *refs: kernel_body(col_total, high, *refs), outs, [points, *arrays],
            flops=2000 * sum(x.size for x in outs),
        )

    pieces = jnp.concatenate([probes, jnp.pad(sources, ((0, 16 - sources.shape[0]), (0, 0)))], axis=0)[None]
    mask = rows_size // 2
    while mask > 2:
        low = mask // 2 if mask // 2 > 2 else 0
        received = []
        for m in [low, mask, mask + low] if low else [mask]:
            received.append(flip(pieces, m))
        pieces = jnp.concatenate([pieces, *received], axis=0)
        mask //= 4 if low else 2
    masks = [0, 2] if rows_size > 2 else [0]
    probes_only = pieces[:, :high]
    square = jax.ShapeDtypeStruct((n, n), F32)
    block = jax.ShapeDtypeStruct((high, n), F32)
    values = []
    samples = []
    for o in range(probe_size):
        held = []
        for m in masks:
            near = pieces if (m, o) == (0, 0) else flip(probes_only if o else pieces, m, o)
            far = flip(near, 1)
            held += [near, far]
            if o == 0:
                for x in (near, far):
                    values += evaluate([x])
        count = len(held) - (o == probe_size - 1)
        cuts = (0, 2, count) if o == 0 and count > 2 else (0, count)
        total = []
        for low, top in zip(cuts, cuts[1:]):
            total = call(
                lambda *refs, count=top - low: sample_body(count, *refs), [block],
                [*held[low:top], *values[low:top], *total], flops=200 * high * n * n,
            )
        samples += total
    scratch = [pltpu.VMEM((n, n), F32)]
    h, m, t = call(
        lambda *refs: leaf_body(probe_size, *refs), [square] * 3,
        [place[None], points, held[-1], values[-1], *samples],
        specs=[SMEM] + [VMEM] * (3 + len(samples)), flops=n**3,
    )
    other = flip(h, 1)
    cuts = (0, PANEL, n)
    for begin, stop in zip(cuts, cuts[1:]):
        t = call(
            lambda *refs, begin=begin, stop=stop: sweep_body(begin, stop, *refs), [square], [t],
            flops=200 * n**3,
        )[0]
    parts = jax.ShapeDtypeStruct((n, 2, leaf_rows), F32)
    basis = call(basis_body, [parts], [points, t, m], flops=60 * n**3)[0]
    packed = jax.ShapeDtypeStruct((n + 8, n // 2), F32)
    h, sent = call(node_body, [square, packed], [h, other], flops=n**3)
    other = flip(sent, 2)
    top, basis = call(
        top_body, [square, parts], [h, other, basis], scratch=[*scratch, pltpu.SemaphoreType.DMA],
        flops=n**3, out_specs=[VMEM, pl.BlockSpec(memory_space=pl.ANY)],
    )
    return (basis, top[None])


def solution(mesh):
    return jax.shard_map(
        per_device,
        mesh=mesh,
        in_specs=(
            P(None, "rows"),
            P(None, "rows"),
            P("probe", "rows"),
            P(("rows", "probe")),
            P(("rows", "probe")),
        ),
        out_specs=(P(None, None, ("rows", "probe")), P(("rows", "probe"), None, None)),
        check_vma=False,
    )
```

```python
import math

import jax
import jax.numpy as jnp
from jax import lax
from jax.experimental import pallas as pl
from jax.experimental.pallas import tpu as pltpu
from jax.sharding import PartitionSpec as P


wavenumber = 30.0
softening = 0.02

F32 = jnp.float32
BF16 = jnp.bfloat16
VMEM = pl.BlockSpec(memory_space=pltpu.VMEM)
SMEM = pl.BlockSpec(memory_space=pltpu.SMEM)
NN = ((1,), (0,))
NT = ((1,), (1,))

SINE = (3.1415927410125732, -5.167710304260254, 2.550077438354492, -0.598291277885437, 0.07765766233205795)
COSINE = (0.9999999403953552, -4.934792995452881, 4.058411121368408, -1.331876516342163, 0.21968960762023926)

LANES = 128
PANEL = 64
CHUNK = 256
COARSE = 0.15
NARROW = 40.0


def split_bf16(value):
    high = value.astype(BF16)
    return high, (value - high.astype(F32)).astype(BF16)


def mxu(left, right, dims):
    return lax.dot_general(left, right, (dims, ((), ())), preferred_element_type=F32)


def dot3(left, right, dims):
    lh, ll = split_bf16(left)
    rh, rl = split_bf16(right)
    return mxu(lh, rh, dims) + (mxu(lh, rl, dims) + mxu(ll, rh, dims))


def pick_lane(tile, lane):
    where = jnp.full(tile.shape, lane, jnp.int32)
    return jnp.take_along_axis(tile, where, axis=1, mode="promise_in_bounds")


def pick_row(tile, row):
    return jnp.broadcast_to(tile[row : row + 1, :], tile.shape)


def sweep(t_ref, begin=0, stop=None):
    n = t_ref.shape[0]
    tiles = n // LANES
    steps = PANEL // 8
    lane = lax.broadcasted_iota(jnp.int32, (8, LANES), 1)
    row = lax.broadcasted_iota(jnp.int32, (8, LANES), 0)
    along_lanes = [jnp.zeros((8, LANES), F32) for _ in range(tiles)]
    along_rows = []
    for start in range(begin, stop or n, PANEL):
        at, low = divmod(start, LANES)
        block = [
            [t_ref[start + 8 * i : start + 8 * i + 8, LANES * t : LANES * (t + 1)] for t in range(tiles)]
            for i in range(steps)
        ]
        pivots = [jnp.zeros((8, LANES), F32) for _ in range(steps)]
        ahead = None
        for i0 in range(steps):
            first = low + 8 * i0

            def columns(i, base):
                return [pick_lane(block[i][at], base + a) for a in range(8)]

            cols = ahead or columns(i0, first)
            below = {i: columns(i, first) for i in range(i0 + 1, steps)}
            after = columns(i0 + 1, first + 8) if i0 + 1 < steps else None
            sums = [jnp.zeros((8, LANES), F32)] * 8
            for a in range(8):
                here = lane == first + a
                pivot = pick_row(cols[a], a)
                inverse = 1.0 / pivot
                pivots[i0] = jnp.where(row == a, pivot, pivots[i0])
                factor = jnp.where(row > a, cols[a] * inverse, 0.0)
                entries = {b: pick_row(cols[b], a) for b in range(a + 1, 8)}
                for b in entries:
                    cols[b] = cols[b] - factor * entries[b]
                swept = [pick_row(block[i0][t], a) for t in range(tiles)]
                swept[at] = jnp.where(here, 2.0 * swept[at], swept[at])
                for t in range(tiles):
                    block[i0][t] = block[i0][t] - factor * swept[t]
                for i, mine in below.items():
                    factor = mine[a] * inverse
                    for b in entries:
                        mine[b] = mine[b] - factor * entries[b]
                    for t in range(tiles):
                        block[i][t] = block[i][t] - factor * swept[t]
                    if after and i == i0 + 1:
                        sums = [x + factor * pick_row(mine[a], b) for b, x in enumerate(sums)]
            along_lanes[at] = along_lanes[at] + jnp.where(lane == first + row, block[i0][at], 0.0)
            ahead = after and [x - y for x, y in zip(after, sums)]
        for i in range(steps):
            for t in range(tiles):
                t_ref[start + 8 * i : start + 8 * i + 8, LANES * t : LANES * (t + 1)] = block[i][t]
        along_rows += pivots
        end = start + PANEL
        if end < n:
            rowi = lax.broadcasted_iota(jnp.int32, (PANEL, n), 0)
            coli = lax.broadcasted_iota(jnp.int32, (PANEL, n), 1)
            whole = jnp.concatenate([jnp.concatenate(x, axis=1) for x in block], axis=0)
            kept = jnp.where((coli < end) & (coli - start > rowi), 0.0, whole)
            scale = 1.0 / jnp.concatenate(pivots, axis=0)
            base = end // LANES * LANES
            factors = whole[:, base:] * jnp.concatenate([scale] * ((n - base) // LANES), axis=1)
            fh, fl = split_bf16(factors)
            kh, kl = split_bf16(kept)
            left = jnp.concatenate([fh, fh, fl], axis=0).T
            right = jnp.concatenate([kh, kl, kh], axis=0)
            for to in range(end, n, CHUNK):
                high = min(CHUNK, n - to)
                change = mxu(left[to - base : to - base + high, :], right, NN)
                colr = lax.broadcasted_iota(jnp.int32, (high, LANES), 1)
                for t in range(tiles):
                    at_t = slice(LANES * t, LANES * (t + 1))
                    rest = t_ref[to : to + high, at_t]
                    if t == at:
                        rest = jnp.where((colr >= low) & (colr < low + PANEL), 0.0, rest)
                    t_ref[to : to + high, at_t] = rest - change[:, at_t]
    return along_lanes, along_rows


def grids(n):
    rows = lax.broadcasted_iota(jnp.int32, (n, n), 0)
    cols = lax.broadcasted_iota(jnp.int32, (n, n), 1)
    return rows, cols


def trace(matrix):
    rows, cols = grids(matrix.shape[0])
    diagonal = jnp.where(rows == cols, matrix, 0.0)
    return jnp.sum(jnp.sum(diagonal, axis=0, keepdims=True), axis=1, keepdims=True)


def factorize(gram, t_ref):
    n = gram.shape[0]
    rows, cols = grids(n)
    shift = trace(gram) / n
    t_ref[...] = gram / shift + jnp.where(rows == cols, 1.0, 0.0)
    along_lanes, along_rows = sweep(t_ref)
    sums = [jnp.sum(x, axis=0, keepdims=True) for x in along_lanes]
    by_col = jnp.concatenate([jnp.broadcast_to(x, (n, LANES)) for x in sums], axis=1)
    by_row = jnp.concatenate([jnp.concatenate([x] * (n // LANES), axis=1) for x in along_rows], axis=0)
    return shift, by_row, by_col


def projected_rows(t_ref, by_row, by_col):
    rows, cols = grids(t_ref.shape[0])
    held = t_ref[...]
    return lax.rsqrt(by_row) * jnp.where(
        rows < cols, held, jnp.where(rows > cols, -held / by_col, by_row - 1.0)
    )


def fold(full_ref, packed_ref):
    n = full_ref.shape[0]
    half = n // 2
    rows, cols = grids(half)
    upper = full_ref[0:half, 0:half]
    lower = full_ref[half:n, half:n]
    packed_ref[0:half, :] = full_ref[0:half, half:n]
    packed_ref[half:n, :] = jnp.where(rows <= cols, upper, lower)
    packed_ref[n : n + 8, :] = jnp.broadcast_to(
        jnp.sum(jnp.where(rows == cols, lower, 0.0), axis=0, keepdims=True), (8, half)
    )


def unfold_add(packed_ref, full_ref):
    n = full_ref.shape[0]
    half = n // 2
    rows, cols = grids(half)
    corner = packed_ref[0:half, :]
    both = packed_ref[half:n, :]
    turned = both.T
    line = jnp.broadcast_to(packed_ref[n : n + 1, :], (half, half))
    upper = jnp.where(rows <= cols, both, turned)
    lower = jnp.where(rows == cols, line, jnp.where(rows > cols, both, turned))
    top = jnp.concatenate([upper, corner], axis=1)
    bottom = jnp.concatenate([corner.T, lower], axis=1)
    return full_ref[...] + jnp.concatenate([top, bottom], axis=0)


def kernel_body(col_total, high, targets_ref, *refs):
    m = targets_ref.shape[1]
    width = refs[0].shape[2]
    turned = jnp.concatenate([targets_ref[...], jnp.zeros((m - 8, m), F32)], axis=0).T
    points = [jnp.broadcast_to(turned[:, c : c + 1], (m, width)) for c in range(3)]
    count = len(refs) // 2
    for piece_ref, out_ref in zip(refs[:count], refs[count:]):
        for i in range(piece_ref.shape[0]):
            source = piece_ref[i, high : high + 3, :].astype(F32)
            first, second = kernel_values(source, points, col_total)
            out_ref[i, 0:m, :] = first
            out_ref[i, m : 2 * m, :] = second


def kernel_values(source, points, col_total):
    size = 1.0 / math.sqrt(col_total)
    square = softening * softening
    for c in range(3):
        diff = source[c : c + 1, :] - points[c]
        square = square + diff * diff
    near = lax.rsqrt(square)
    amplitude = near * size
    turns = (square * near) * (wavenumber / math.pi)
    whole = jnp.round(turns)
    rest = turns - whole
    r2 = rest * rest
    sine = rest * power_series(SINE, r2)
    cosine = power_series(COSINE, r2)
    odd = (whole.astype(jnp.int32) & 1) == 1
    amplitude = jnp.where(odd, -amplitude, amplitude)
    return (amplitude * cosine).astype(BF16), (amplitude * sine).astype(BF16)


def power_series(terms, x):
    value = terms[-1]
    for term in terms[-2::-1]:
        value = value * x + term
    return value


def accumulate(probe_ref, kernel_ref, high, total):
    pieces = probe_ref.shape[0]
    both = 2 if pieces % 2 == 0 else 1

    def one(i, total):
        left = jnp.concatenate([probe_ref[both * i + k, 0:high, :] for k in range(both)], axis=1)
        right = jnp.concatenate([kernel_ref[both * i + k] for k in range(both)], axis=1)
        return total + mxu(left, right, NT)

    count = pieces // both
    return lax.fori_loop(0, count, one, total, unroll=count <= 8)


def sample_body(groups, *refs):
    out_ref = refs[-1]
    high, n = out_ref.shape
    total = refs[2 * groups][...] if len(refs) == 2 * groups + 2 else jnp.zeros((high, n), F32)
    for g in range(groups):
        total = accumulate(refs[g], refs[groups + g], high, total)
    out_ref[...] = total


def leaf_body(blocks, place_ref, points_ref, probe_ref, kernel_ref, *refs):
    h_ref, m_ref, a_ref = refs[blocks:]
    n = h_ref.shape[0]
    rows, cols = grids(n)
    high = n // blocks
    for o in range(blocks):
        total = refs[o][...]
        if o == blocks - 1:
            total = accumulate(probe_ref, kernel_ref, high, total)
        at = pl.multiple_of((place_ref[0] ^ o) * high, high)
        m_ref[pl.ds(at, high), :] = total
    half = n // 2
    inside = (cols - jnp.where(cols >= half, half, 0)).astype(F32) < points_ref[3:4, 0:1]
    matrix = jnp.where(inside, m_ref[...], 0.0)
    m_ref[...] = matrix
    gram = dot3(matrix, matrix, NT)
    shift = trace(gram) / n
    scaled = gram / shift
    unit = jnp.where(rows == cols, 1.0, 0.0)
    a_ref[...] = scaled + unit
    rank = points_ref[4:5, 0:1]
    kept_row = rows.astype(F32) < rank
    kept_col = cols.astype(F32) < rank
    inner = jnp.where(kept_row & kept_col, scaled, 0.0)
    turned = inverse(inner + unit, h_ref)
    outer = jnp.where(kept_row & (cols.astype(F32) >= rank), scaled, 0.0)
    solved = jnp.where(kept_row, jnp.where(kept_col, unit - turned, dot3(turned, outer, NN)), 0.0)
    h_ref[...] = dot3(jnp.where(kept_col, scaled, 0.0), solved, NN) * shift


def sweep_body(begin, stop, a_ref, t_ref):
    t_ref[...] = a_ref[...]
    sweep(t_ref, begin, stop)


def basis_body(points_ref, t_ref, m_ref, b_ref):
    n = t_ref.shape[0]
    rows, cols = grids(n)
    held = t_ref[...]
    matrix = m_ref[...]
    shift = jnp.sum(jnp.sum(matrix * matrix, axis=0, keepdims=True), axis=1, keepdims=True) / n
    diagonal = jnp.where(rows == cols, held, 0.0)
    by_row = jnp.sum(diagonal, axis=1, keepdims=True)
    by_col = jnp.sum(diagonal, axis=0, keepdims=True)
    inverse = jnp.where(rows > cols, held / by_col, jnp.where(rows == cols, 1.0, 0.0))
    scale = jnp.where(rows.astype(F32) < points_ref[4:5, 0:1], lax.rsqrt(by_row * shift), 0.0)
    basis = dot3(inverse * scale, matrix, NN)
    half = b_ref.shape[2]
    for c in range(2):
        b_ref[:, c, :] = basis[:, c * half : (c + 1) * half]


def inverse(matrix, x_ref):
    n = matrix.shape[0]
    bound = jnp.max(jnp.sum(jnp.abs(matrix), axis=0, keepdims=True))

    @pl.when(bound <= NARROW)
    def _():
        x_ref[...] = iterate(matrix, NARROW)

    @pl.when(jnp.logical_not(bound <= NARROW))
    def _():
        x_ref[...] = iterate(matrix, 1.001 * (n + 1.0))

    return x_ref[...]


def iterate(matrix, most):
    n = matrix.shape[0]
    rows, cols = grids(n)
    high, low = split_bf16(matrix)
    least = 1.0
    scale = 2.0 / (least + most)
    guess = jnp.where(rows == cols, 2.0 * scale, 0.0) - scale * scale * matrix
    spread = (most - least) / (most + least)
    while spread > 0.013:
        least = 1.0 - spread * spread
        scale = 2.0 / (1.0 + least)
        spread = (1.0 - least) / (1.0 + least)
        if spread > COARSE:
            rough = guess.astype(BF16)
            product = mxu(high, rough, NN).astype(BF16)
            change = mxu(rough, product, NN)
        else:
            gh, gl = split_bf16(guess)
            product = mxu(high, gh, NN) + (mxu(high, gl, NN) + mxu(low, gh, NN))
            ph, pl_ = split_bf16(product)
            change = mxu(gh, ph, NN) + (mxu(gh, pl_, NN) + mxu(gl, ph, NN))
        guess = (2.0 * scale) * guess - (scale * scale) * change
    return guess


def node_body(own_ref, other_ref, h_ref, packed_ref):
    gram = own_ref[...] + other_ref[...]
    n = gram.shape[0]
    rows, cols = grids(n)
    shift = trace(gram) / n
    scaled = gram / shift
    start = scaled + jnp.where(rows == cols, 1.0, 0.0)
    h_ref[...] = (scaled - jnp.where(rows == cols, 1.0, 0.0) + inverse(start, h_ref)) * shift
    fold(h_ref, packed_ref)


def top_body(own_ref, other_ref, basis_ref, z_ref, out_ref, t_ref, sem):
    copy = pltpu.make_async_copy(basis_ref, out_ref, sem)
    copy.start()
    shift, by_row, by_col = factorize(unfold_add(other_ref, own_ref), t_ref)
    value = projected_rows(t_ref, by_row, by_col)
    z_ref[...] = (value * jnp.sqrt(shift)).T
    copy.wait()


def call(body, outs, operands, specs=None, scratch=(), flops=0, out_specs=None):
    bytes_used = sum(x.size * x.dtype.itemsize for x in (*outs, *operands))
    return pl.pallas_call(
        body,
        out_shape=list(outs),
        in_specs=list(specs or [VMEM] * len(operands)),
        out_specs=list(out_specs or [VMEM] * len(outs)),
        scratch_shapes=list(scratch),
        cost_estimate=pl.CostEstimate(flops=flops, bytes_accessed=bytes_used, transcendentals=0),
        compiler_params=pltpu.CompilerParams(vmem_limit_bytes=2 * bytes_used + (6 << 20)),
    )(*operands)


def flip(value, rows_mask, probe_mask=0):
    probe_size = lax.axis_size("probe")
    if probe_mask == 0:
        pairs = [(i, i ^ rows_mask) for i in range(lax.axis_size("rows"))]
        return lax.ppermute(value, "rows", pairs)
    if rows_mask == 0:
        pairs = [(i, i ^ probe_mask) for i in range(probe_size)]
        return lax.ppermute(value, "probe", pairs)
    pairs = [
        (i * probe_size + j, (i ^ rows_mask) * probe_size + (j ^ probe_mask))
        for i in range(lax.axis_size("rows"))
        for j in range(probe_size)
    ]
    return lax.ppermute(value, ("rows", "probe"), pairs)


def per_device(targets, sources, probes, cluster_sizes, leaf_ranks):
    rows_size = lax.axis_size("rows")
    probe_size = lax.axis_size("probe")
    col_total = sources.shape[1] * rows_size
    high = probes.shape[0]
    n = high * probe_size
    leaf_rows = targets.shape[1] // probe_size
    place = lax.axis_index("probe")

    points = lax.dynamic_slice_in_dim(targets, place * leaf_rows, leaf_rows, 1)
    limits = [jnp.full((1, leaf_rows), x[0]).astype(F32) for x in (cluster_sizes, leaf_ranks)]
    points = jnp.concatenate([points, *limits, jnp.zeros((3, leaf_rows), F32)], axis=0)

    def evaluate(arrays):
        outs = [jax.ShapeDtypeStruct((x.shape[0], 2 * leaf_rows, x.shape[2]), BF16) for x in arrays]
        return call(
            lambda *refs: kernel_body(col_total, high, *refs), outs, [points, *arrays],
            flops=2000 * sum(x.size for x in outs),
        )

    pieces = jnp.concatenate([probes, jnp.pad(sources, ((0, 16 - sources.shape[0]), (0, 0)))], axis=0)[None]
    mask = rows_size // 2
    while mask > 2:
        low = mask // 2 if mask // 2 > 2 else 0
        received = []
        for m in [low, mask, mask + low] if low else [mask]:
            received.append(flip(pieces, m))
        pieces = jnp.concatenate([pieces, *received], axis=0)
        mask //= 4 if low else 2
    masks = [0, 2] if rows_size > 2 else [0]
    probes_only = pieces[:, :high]
    square = jax.ShapeDtypeStruct((n, n), F32)
    block = jax.ShapeDtypeStruct((high, n), F32)
    values = []
    samples = []
    for o in range(probe_size):
        held = []
        for m in masks:
            near = pieces if (m, o) == (0, 0) else flip(probes_only if o else pieces, m, o)
            far = flip(near, 1)
            held += [near, far]
            if o == 0:
                for x in (near, far):
                    values += evaluate([x])
        count = len(held) - (o == probe_size - 1)
        cuts = (0, 2, count) if o == 0 and count > 2 else (0, count)
        total = []
        for low, top in zip(cuts, cuts[1:]):
            total = call(
                lambda *refs, count=top - low: sample_body(count, *refs), [block],
                [*held[low:top], *values[low:top], *total], flops=200 * high * n * n,
            )
        samples += total
    scratch = [pltpu.VMEM((n, n), F32)]
    h, m, t = call(
        lambda *refs: leaf_body(probe_size, *refs), [square] * 3,
        [place[None], points, held[-1], values[-1], *samples],
        specs=[SMEM] + [VMEM] * (3 + len(samples)), flops=n**3,
    )
    other = flip(h, 1)
    cuts = (0, PANEL, n)
    for begin, stop in zip(cuts, cuts[1:]):
        t = call(
            lambda *refs, begin=begin, stop=stop: sweep_body(begin, stop, *refs), [square], [t],
            flops=200 * n**3,
        )[0]
    parts = jax.ShapeDtypeStruct((n, 2, leaf_rows), F32)
    basis = call(basis_body, [parts], [points, t, m], flops=60 * n**3)[0]
    packed = jax.ShapeDtypeStruct((n + 8, n // 2), F32)
    h, sent = call(node_body, [square, packed], [h, other], flops=n**3)
    other = flip(sent, 2)
    top, basis = call(
        top_body, [square, parts], [h, other, basis], scratch=[*scratch, pltpu.SemaphoreType.DMA],
        flops=n**3, out_specs=[VMEM, pl.BlockSpec(memory_space=pl.ANY)],
    )
    return (basis, top[None])


def solution(mesh):
    return jax.shard_map(
        per_device,
        mesh=mesh,
        in_specs=(
            P(None, "rows"),
            P(None, "rows"),
            P("probe", "rows"),
            P(("rows", "probe")),
            P(("rows", "probe")),
        ),
        out_specs=(P(None, None, ("rows", "probe")), P(("rows", "probe"), None, None)),
        check_vma=False,
    )
```
